256 devices in a mesh: clip: 8 (over x_hi, y), feat: 32 (over z, x_lo, core).
Axes of the slice: x: 4 (x_hi: 2, x_lo: 2; x = x_hi * 2 + x_lo), y: 4, z: 8, core: 2. Of those that a mesh axis runs over, the one named last changes fastest.
Arguments:
- embeds: float32 [8192, 1152], P('clip', 'feat'), may hold values from -6 to 6
- frequencies: float32 [1152, 20480], P('clip', 'feat'), may hold values from -0.5 to 0.5
- phases: float32 [20480], P('feat'), may hold values from -3.140625 to 3.140625
- weights: float32 [20480, 128], P('feat', 'clip'), may hold values from -6 to 6
- labels: int32 [8192, 128], P('clip'), may hold values 0 or 1
Outputs:
- trained: float32 [20480, 128], P('feat', 'clip')
- scores: float32 [8192, 128], P('clip', 'feat')
The draws below stay inside these ranges and needn't reach their ends.
All inputs are finite; a program needn't handle non-finite values. No bound on the sum of `labels` on one device may be relied on, other than what follows from the above.
Results may differ from the reference program's by a relative error of at most 0.0055.
Values may be sent and summed in bfloat16 or wider, within the bound.
A program may use at most 64 MiB of HBM per device.

```python
import math
import jax
import jax.numpy as jnp
from jax import lax

E = 1152
K = 128
FD = 640
STEPS = 2
NCLIPS = 8192
FEATURES = 20480
N_FEAT = 32


def with_ends(entries, rng, smallest, largest):
    extent = entries.shape
    index_at = [jax.random.randint(jax.random.fold_in(rng, axis), (), 0, extent[axis]) for axis in range(len(extent))]
    entries = entries.at[tuple(index_at)].set(smallest)
    longest = extent.index(max(extent))
    index_at[longest] = (index_at[longest] + 1) % extent[longest]
    return entries.at[tuple(index_at)].set(largest)


def steps_of(rng, shape, split, smallest, largest):
    factor_of = 1.0
    for axis_at, blocks in split:
        draws = jax.random.uniform(jax.random.fold_in(jax.random.fold_in(rng, 6), axis_at), (blocks,), jnp.float32, smallest / len(split), largest / len(split))
        factor_of = factor_of * jnp.repeat(jnp.exp(draws), shape[axis_at] // blocks).reshape((-1,) + (1,) * (len(shape) - 1 - axis_at))
    return factor_of


def bell_draw(rng, dims, deviation, bound, pieces=(), kind=jnp.bfloat16):
    loudness = steps_of(rng, dims, pieces, -0.22, 0.18) if pieces else 1.0
    array = jax.random.normal(rng, dims, jnp.float32) * deviation * loudness
    return jnp.minimum(jnp.maximum(array, -bound), bound).astype(kind)


def setup_inputs(seed: int = 0) -> dict:
    arg_keys = jax.random.split(jax.random.key(seed), 6)
    return {
        "embeds": bell_draw(arg_keys[0], (NCLIPS, E), 1.0, 6.0, ((0, 8), (1, 32)), jnp.float32),
        "frequencies": bell_draw(arg_keys[1], (E, FEATURES), (E // 9) ** -0.5, 0.5, ((0, 8), (1, 32)), jnp.float32),
        "phases": jnp.clip(jax.random.uniform(arg_keys[2], (FEATURES,), jnp.float32, -3.140625, 3.140625), -3.140625, 3.140625),
        "weights": bell_draw(arg_keys[3], (FEATURES, K), 1.0, 6.0, ((0, 32), (1, 8)), jnp.float32),
        "labels": with_ends((jax.random.randint(arg_keys[4], (NCLIPS, K), 0, 2) < 1).astype(jnp.int32), jax.random.fold_in(arg_keys[4], 1), 0, 1),
    }


def features(embeds, frequencies, phases, start):
    columns = lax.dynamic_slice_in_dim(frequencies, start, FD, 1)
    offset = lax.dynamic_slice_in_dim(phases, start, FD, 0)
    angles = jnp.dot(embeds, columns, precision=lax.Precision.HIGHEST, preferred_element_type=jnp.float32)
    feature_scale = math.sqrt(2.0 / FEATURES)
    return (feature_scale * jnp.cos(angles + offset[None, :])).astype(jnp.bfloat16)

def reference(embeds, frequencies, phases, weights, labels):
    starts = jnp.arange(N_FEAT, dtype=jnp.int32) * FD
    targets = labels.astype(jnp.float32)

    def logits_of(beta):
        beta_half = beta.astype(jnp.bfloat16)

        def accumulate(carry, start):
            phi = features(embeds, frequencies, phases, start)
            block = lax.dynamic_slice_in_dim(beta_half, start, FD, 0)
            return (carry + jnp.dot(phi, block, preferred_element_type=jnp.float32), None)
        total, unused = lax.scan(accumulate, jnp.zeros((NCLIPS, K), jnp.float32), starts)
        return total
    beta = weights
    for step in range(STEPS):
        logits = logits_of(beta)
        residual = (jax.nn.sigmoid(logits) - targets).astype(jnp.bfloat16)

        def gradient_block(start):
            phi = features(embeds, frequencies, phases, start)
            return lax.dot_general(phi, residual, (((0,), (0,)), ((), ())), preferred_element_type=jnp.float32)
        gradient = lax.map(gradient_block, starts).reshape(FEATURES, K)
        beta = beta - 0.25 * gradient
    return (beta, logits_of(beta))
```

```python
import functools
import math

import jax
import jax.numpy as jnp
from jax import lax
from jax.experimental import pallas as pl
from jax.experimental.pallas import tpu as pltpu
from jax.sharding import PartitionSpec as P

STEPS = 2
MESH = pl.DeviceIdType.MESH

NY = 4
NZ = 8

PI_A = 3.1416015625
PI_B = -8.909031748771667e-06
PI_C = 1.2154188766544394e-10
SIN = (9.99999976e-01, -1.66666473e-01, 8.33289467e-03, -1.98005800e-04, 2.58984559e-06)


def scaled_cos(x, scale):
    q = jnp.round(x * (0.5 / math.pi))
    w = ((0.5 * x - q * PI_A) - q * PI_B) - q * PI_C
    w2 = w * w
    p = SIN[4]
    for c in SIN[3::-1]:
        p = p * w2 + c
    s = w * p
    return scale - (2.0 * scale) * (s * s)


def bytes_of(ref, sem):
    pltpu.make_async_copy(ref, ref, sem).wait()


def kernel(
    scale,
    e_ref, f_ref, ph_ref, w_ref, lab_ref,
    tr_ref, sc_ref,
    e_all, f_all, e_oth, e_two, f_rel,
    e_hi, e_lo, ft_hi, ft_lo, ph_t, ang, phi, lab_t,
    w_own, w_send, w_t,
    part, c_send, c_recv, l_send, l_recv, r_t,
    grad, g_send, g_recv, fin,
    e0_s, e0_r, ex_s, ex_r, er_s, er_r, ep_s, ep_r,
    fx_s, fx_r, fy_s, fy_r,
    w_s, w_r, c_s, c_r, l_s, l_r, r_s, r_r, rc_s, rc_r, g_s, g_r, q_s, q_r,
):
    clip = lax.axis_index("clip")
    feat = lax.axis_index("feat")
    c = lax.rem(feat, 2)
    xl = lax.rem(feat // 2, 2)
    z = feat // 4
    y = lax.rem(clip, NY)
    xh = clip // NY

    ke = e_ref.shape[0]
    kc = 4 * ke
    nf = f_ref.shape[1]
    nn = e_ref.shape[1]
    half = nn // 2
    quarter = nn // 4
    kk = w_ref.shape[0] * 8

    def feat_of(z_, xl_, c_):
        return (z_ * 2 + xl_) * 2 + c_

    def dev(clip_, feat_):
        return (clip_, feat_)

    partner = dev(clip, feat_of(z, xl, 1 - c))
    x_near = dev(clip, feat_of(z, 1 - xl, c))
    x_cross = dev((1 - xh) * NY + y, feat_of(z, 1 - xl, c))
    diag = dev(clip, feat_of(z, 1 - xl, 1 - c))

    def feat_peer(dz, dx):
        return lax.rem(z + dz, NZ), (1 - xl if dx else xl)

    feat_offsets = [(dz, dx) for dz in (4, 3, 5, 2, 6, 1, 7, 0) for dx in (1, 0) if (dz, dx) != (0, 0)]

    def clip_peer(d):
        return lax.rem(clip + d, 8)

    clip_offsets = [6, 2, 5, 7, 3, 1, 4]

    barrier = pltpu.get_barrier_semaphore()
    peers = [partner, x_cross, diag]
    for dz, dx in feat_offsets:
        pz, px = feat_peer(dz, dx)
        peers.append(dev(clip, feat_of(pz, px, c)))
    for d in clip_offsets:
        peers.append(dev(clip_peer(d), feat))
    for peer in peers:
        pl.semaphore_signal(barrier, inc=1, device_id=peer, device_id_type=MESH)

    w_own[...] = w_ref[...]
    w_send[0] = w_ref[...].astype(jnp.bfloat16)
    kw = w_ref.shape[0]
    my_rows = pl.ds(pl.multiple_of(clip * kw, kw), kw)
    w_t[0, my_rows, :] = w_ref[...].astype(jnp.bfloat16)

    pl.semaphore_wait(barrier, len(peers))

    sends = []

    def put(src, dst, s_sem, r_sem, to, own_sem=True):
        copy = pltpu.make_async_remote_copy(
            src_ref=src, dst_ref=dst, send_sem=s_sem, recv_sem=r_sem, device_id=to, device_id_type=MESH)
        copy.start()
        if own_sem:
            sends.append(copy)

    lanes_c = pl.ds(pl.multiple_of(c * half, half), half)
    lanes_o = pl.ds(pl.multiple_of((1 - c) * half, half), half)

    def e_rows(z_, xl_):
        return pl.ds(pl.multiple_of(z_ * kc + xl_ * (2 * ke), 8), 2 * ke)

    def e_piece(z_, xl_):
        return e_all.at[e_rows(z_, xl_), lanes_c]

    def f_rows(clip_, part_):
        if part_ is None:
            return f_all.at[pl.ds(pl.multiple_of(clip_ * kc, 8), kc), :]
        return f_all.at[pl.ds(pl.multiple_of(clip_ * kc + part_ * (kc // 2), 8), kc // 2), :]

    put(e_ref.at[:, lanes_o], e_oth, e0_s, e0_r, partner)

    hk = kc // 2
    put(f_ref.at[0:hk, :], f_rel.at[0], fx_s.at[0], fx_r.at[0], x_near)
    put(f_ref.at[hk:kc, :], f_rel.at[1], fx_s.at[1], fx_r.at[1], x_cross)
    y_right = dev(xh * NY + lax.rem(y + 1, NY), feat)
    y_left = dev(xh * NY + lax.rem(y + NY - 1, NY), feat)
    put(f_ref, f_rows(clip, None), fy_s.at[0, 0, 0], fy_r.at[0, 0, 0], y_right)
    put(f_ref, f_rows(clip, None), fy_s.at[1, 0, 0], fy_r.at[1, 0, 0], y_left)
    f_all[pl.ds(pl.multiple_of(clip * kc, 8), kc), :] = f_ref[...]

    for d in clip_offsets:
        put(w_send.at[0], w_t.at[0, my_rows, :], w_s.at[0], w_r.at[0], dev(clip_peer(d), feat), False)

    z_up = dev(clip, feat_of(lax.rem(z + 1, NZ), xl, c))
    z_down = dev(clip, feat_of(lax.rem(z + NZ - 1, NZ), xl, c))

    bytes_of(e_oth, e0_r)
    mine = e_ref[:, lanes_c]
    other = e_oth[...]
    first = c == 0
    e_two[0:ke, :] = jnp.where(first, mine, other)
    e_two[ke:2 * ke, :] = jnp.where(first, other, mine)
    e_all[e_rows(z, xl), lanes_c] = e_two[...]

    own_piece = e_piece(z, xl)
    put(own_piece, own_piece, ex_s, ex_r, x_near)
    put(own_piece, own_piece, er_s.at[0, 0, 0], er_r.at[0, 0, 0], z_up)
    put(own_piece, own_piece, er_s.at[1, 0, 0], er_r.at[1, 0, 0], z_down)

    def to_partner(z_, xl_, dz, o):
        put(e_piece(z_, xl_), e_piece(z_, xl_), ep_s.at[o, dz], ep_r.at[o, dz], partner)

    def split_e(z_, lanes):
        rows = pl.ds(pl.multiple_of(z_ * kc, 16), kc)
        x = e_all[rows, lanes]
        hi = x.astype(jnp.bfloat16)
        e_hi[rows, lanes] = hi
        e_lo[rows, lanes] = (x - hi.astype(jnp.float32)).astype(jnp.bfloat16)

    to_partner(z, xl, 0, 0)

    qn = pl.multiple_of((2 * c + xl) * quarter, quarter)
    lab_t[...] = lab_ref[pl.ds(qn, quarter), :].astype(jnp.float32).T
    ph_t[...] = jnp.broadcast_to(ph_ref[...], (128, nf)).T

    near_piece = e_piece(z, 1 - xl)
    bytes_of(near_piece, ex_r)
    put(near_piece, near_piece, er_s.at[0, 1, 0], er_r.at[0, 1, 0], z_up)
    put(near_piece, near_piece, er_s.at[1, 1, 0], er_r.at[1, 1, 0], z_down)
    to_partner(z, 1 - xl, 0, 1)
    split_e(z, lanes_c)

    def e_step(direction, o, s):
        dz = (NZ - s) if direction == 0 else s
        z_ = lax.rem(z + dz, NZ)
        xl_ = (1 - xl) if o else xl
        piece = e_piece(z_, xl_)
        bytes_of(piece, er_r.at[direction, o, s - 1])
        if s < 3 or (s == 3 and o == direction):
            put(piece, piece, er_s.at[direction, o, s], er_r.at[direction, o, s], z_up if direction == 0 else z_down)
        to_partner(z_, xl_, dz, o)

    xh_clip = (1 - xh) * NY + y

    def f_relay():
        bytes_of(f_rel.at[0], fx_r.at[0])
        put(f_rel.at[0], f_rows(xh_near_clip, 0), fx_s.at[2], fx_r.at[2], x_cross)
        bytes_of(f_rel.at[1], fx_r.at[1])
        put(f_rel.at[1], f_rows(xh_cross_clip, 1), fx_s.at[3], fx_r.at[3], x_near)

    xh_near_clip = clip
    xh_cross_clip = xh_clip

    def f_across():
        bytes_of(f_rows(xh_clip, 0), fx_r.at[2])
        bytes_of(f_rows(xh_clip, 1), fx_r.at[3])
        whole = f_rows(xh_clip, None)
        put(whole, whole, fy_s.at[0, 1, 0], fy_r.at[0, 1, 0], y_right)
        put(whole, whole, fy_s.at[1, 1, 0], fy_r.at[1, 1, 0], y_left)

    def f_turn(u):
        xh_ = (1 - xh) if u else xh
        from_left = xh_ * NY + lax.rem(y + NY - 1, NY)
        from_right = xh_ * NY + lax.rem(y + 1, NY)
        bytes_of(f_rows(from_left, None), fy_r.at[0, u, 0])
        put(f_rows(from_left, 0), f_rows(from_left, 0), fy_s.at[0, u, 1], fy_r.at[0, u, 1], y_right)
        bytes_of(f_rows(from_right, None), fy_r.at[1, u, 0])
        put(f_rows(from_right, 1), f_rows(from_right, 1), fy_s.at[1, u, 1], fy_r.at[1, u, 1], y_left)

    def f_last(u):
        xh_ = (1 - xh) if u else xh
        far = xh_ * NY + lax.rem(y + 2, NY)
        bytes_of(f_rows(far, 0), fy_r.at[0, u, 1])
        bytes_of(f_rows(far, 1), fy_r.at[1, u, 1])

    e_step(0, 0, 1)
    e_step(1, 0, 1)
    f_relay()
    e_step(0, 1, 1)
    e_step(1, 1, 1)
    split_e(lax.rem(z + NZ - 1, NZ), lanes_c)
    split_e(lax.rem(z + 1, NZ), lanes_c)
    f_turn(0)
    e_step(0, 0, 2)
    e_step(1, 0, 2)
    f_across()
    e_step(0, 1, 2)
    e_step(1, 1, 2)
    split_e(lax.rem(z + NZ - 2, NZ), lanes_c)
    split_e(lax.rem(z + 2, NZ), lanes_c)
    e_step(0, 0, 3)
    e_step(1, 0, 3)
    f_last(0)
    e_step(0, 1, 3)
    e_step(1, 1, 3)
    split_e(lax.rem(z + NZ - 3, NZ), lanes_c)
    split_e(lax.rem(z + 3, NZ), lanes_c)
    f_turn(1)
    e_step(0, 0, 4)
    e_step(1, 1, 4)
    split_e(lax.rem(z + 4, NZ), lanes_c)
    for dz in (0, 7, 1, 6, 2, 5, 3, 4):
        z_ = lax.rem(z + dz, NZ)
        for o in (0, 1):
            xl_ = (1 - xl) if o else xl
            bytes_of(e_all.at[e_rows(z_, xl_), lanes_o], ep_r.at[o, dz])
        split_e(z_, lanes_o)
    f_last(1)

    kt = e_all.shape[0]
    for b in range(kt // 128):
        x = f_all[128 * b:128 * b + 128, :].T
        hi = x.astype(jnp.bfloat16)
        ft_hi[:, 128 * b:128 * b + 128] = hi
        ft_lo[:, 128 * b:128 * b + 128] = (x - hi.astype(jnp.float32)).astype(jnp.bfloat16)

    dot = functools.partial(jnp.dot, preferred_element_type=jnp.float32)

    @pl.loop(0, nn // 256)
    def _(n):
        cols = pl.ds(pl.multiple_of(n * 256, 256), 256)
        ang[...] = dot(ft_hi[...], e_lo[:, cols]) + dot(ft_lo[...], e_hi[:, cols]) + dot(ft_hi[...], e_hi[:, cols])

        @pl.loop(0, nf // 32)
        def _(m):
            rows = pl.ds(pl.multiple_of(m * 32, 32), 32)
            p = ph_t[rows, :]
            x = ang[rows, :] + jnp.concatenate([p, p], axis=1)
            phi[rows, cols] = scaled_cos(x, scale).astype(jnp.bfloat16)

    my_block = pl.ds(pl.multiple_of(z * 16, 16), 16)
    my_lanes = pl.ds(pl.multiple_of(xl * quarter, quarter), quarter)

    def summed_logits(t):
        w = w_t[t]
        c_send[t] = dot(w, phi[:, lanes_o]).astype(jnp.bfloat16)
        put(c_send.at[t], c_recv.at[t], c_s.at[t], c_r.at[t], partner)
        part[...] = dot(w, phi[:, lanes_c])
        bytes_of(c_recv.at[t], c_r.at[t])
        total = part[...] + c_recv[t].astype(jnp.float32)
        part[...] = total
        l_send[t] = total.astype(jnp.bfloat16)
        for dz, dx in feat_offsets:
            pz, px = feat_peer(dz, dx)
            src = l_send.at[t, pl.ds(pl.multiple_of(pz * 16, 16), 16), pl.ds(pl.multiple_of(px * quarter, quarter), quarter)]
            put(src, l_recv.at[t, dx * NZ + dz - 1], l_s.at[t], l_r.at[t], dev(clip, feat_of(pz, px, c)), False)
        acc = part[my_block, my_lanes]
        bytes_of(l_recv.at[t], l_r.at[t])
        for i in range(2 * NZ - 1):
            acc = acc + l_recv[t, i].astype(jnp.float32)
        return acc

    nt = (((1,), (1,)), ((), ()))
    full_lanes = pl.ds(pl.multiple_of(c * half + xl * quarter, quarter), quarter)

    for t in range(STEPS):
        bytes_of(g_recv.at[0], w_r.at[t])
        acc = summed_logits(t)
        residual = (jax.nn.sigmoid(acc) - lab_t[my_block, :]).astype(jnp.bfloat16)
        r_t[t, my_block, full_lanes] = residual
        mine_r = r_t.at[t, my_block, full_lanes]
        for dz, dx in feat_offsets:
            pz, px = feat_peer(dz, dx)
            put(mine_r, mine_r, r_s.at[t], r_r.at[t], dev(clip, feat_of(pz, px, c)), False)
        bytes_of(l_recv.at[t], r_r.at[t])
        half_r = r_t.at[t, :, lanes_c]
        put(half_r, half_r, rc_s.at[t], rc_r.at[t], partner)
        grad[...] = lax.dot_general(r_t[t, :, lanes_c], phi[:, lanes_c], nt, preferred_element_type=jnp.float32)
        bytes_of(r_t.at[t, :, lanes_o], rc_r.at[t])
        total = grad[...] + lax.dot_general(r_t[t, :, lanes_o], phi[:, lanes_o], nt, preferred_element_type=jnp.float32)
        grad[...] = total
        g_send[t] = total.astype(jnp.bfloat16)
        for d in clip_offsets:
            j = clip_peer(d)
            put(g_send.at[t, pl.ds(pl.multiple_of(j * kw, kw), kw), :], g_recv.at[t, d - 1], g_s.at[t], g_r.at[t], dev(j, feat), False)
        g = grad[my_rows, :]
        bytes_of(g_recv.at[t], g_r.at[t])
        for i in range(7):
            g = g + g_recv[t, i].astype(jnp.float32)
        w_new = w_own[...] - 0.25 * g
        w_own[...] = w_new
        w_half = w_new.astype(jnp.bfloat16)
        w_send[t + 1] = w_half
        w_t[t + 1, my_rows, :] = w_half
        for d in clip_offsets:
            put(w_send.at[t + 1], w_t.at[t + 1, my_rows, :], w_s.at[t + 1], w_r.at[t + 1], dev(clip_peer(d), feat), False)
    tr_ref[...] = w_own[...]

    bytes_of(g_recv.at[0], w_r.at[STEPS])
    acc = summed_logits(STEPS)
    fin[:, full_lanes] = acc
    mine_f = fin.at[:, full_lanes]
    for to in (diag, x_near, partner):
        put(mine_f, mine_f, q_s, q_r, to, False)
    bytes_of(fin.at[:, 0:3 * quarter], q_r)
    which = 2 * xl + c
    out = fin[0:4, :]
    for i in range(1, 4):
        out = jnp.where(which == i, fin[4 * i:4 * i + 4, :], out)
    sc_ref[...] = out

    for copy in sends:
        copy.wait_send()
    for t in range(STEPS + 1):
        bytes_of(g_recv.at[0], w_s.at[t])
        bytes_of(l_recv.at[0], l_s.at[t])
    for t in range(STEPS):
        bytes_of(l_recv.at[0], r_s.at[t])
        bytes_of(g_recv.at[0], g_s.at[t])
    bytes_of(fin.at[:, 0:3 * quarter], q_s)


def per_device(embeds, frequencies, phases, weights, labels):
    nn, ke = embeds.shape
    kc, nf = frequencies.shape
    kw = weights.shape[1]
    kk = labels.shape[1]
    kt = kc * lax.axis_size("clip")
    total_features = nf * lax.axis_size("feat")
    scale = math.sqrt(2.0 / total_features)
    f32, b16 = jnp.float32, jnp.bfloat16
    dma = pltpu.SemaphoreType.DMA
    vm = pl.BlockSpec(memory_space=pltpu.VMEM)
    half, quarter = nn // 2, nn // 4
    steps = STEPS + 1
    scratch = [
        pltpu.VMEM((kt, nn), f32),
        pltpu.VMEM((kt, nf), f32),
        pltpu.VMEM((ke, half), f32),
        pltpu.VMEM((2 * ke, half), f32),
        pltpu.VMEM((2, kc // 2, nf), f32),
        pltpu.VMEM((kt, nn), b16),
        pltpu.VMEM((kt, nn), b16),
        pltpu.VMEM((nf, kt), b16),
        pltpu.VMEM((nf, kt), b16),
        pltpu.VMEM((nf, 128), f32),
        pltpu.VMEM((nf, 256), f32),
        pltpu.VMEM((nf, nn), b16),
        pltpu.VMEM((kk, quarter), f32),
        pltpu.VMEM((kw, nf), f32),
        pltpu.VMEM((steps, kw, nf), b16),
        pltpu.VMEM((steps, kk, nf), b16),
        pltpu.VMEM((kk, half), f32),
        pltpu.VMEM((steps, kk, half), b16),
        pltpu.VMEM((steps, kk, half), b16),
        pltpu.VMEM((steps, kk, half), b16),
        pltpu.VMEM((steps, 2 * NZ - 1, 16, quarter), b16),
        pltpu.VMEM((STEPS, kk, nn), b16),
        pltpu.VMEM((kk, nf), f32),
        pltpu.VMEM((STEPS, kk, nf), b16),
        pltpu.VMEM((STEPS, 7, kw, nf), b16),
        pltpu.VMEM((16, nn), f32),
        dma, dma, dma, dma, dma((2, 2, 4)), dma((2, 2, 4)), dma((2, NZ)), dma((2, NZ)),
        dma((4,)), dma((4,)), dma((2, 2, 2)), dma((2, 2, 2)),
        dma((steps,)), dma((steps,)), dma((steps,)), dma((steps,)), dma((steps,)), dma((steps,)),
        dma((STEPS,)), dma((STEPS,)), dma((STEPS,)), dma((STEPS,)), dma((STEPS,)), dma((STEPS,)), dma, dma,
    ]
    trained_t, scores_t = pl.pallas_call(
        functools.partial(kernel, scale),
        out_shape=(jax.ShapeDtypeStruct((kw, nf), f32), jax.ShapeDtypeStruct((4, nn), f32)),
        in_specs=[vm] * 5,
        out_specs=(vm, vm),
        scratch_shapes=scratch,
        compiler_params=pltpu.CompilerParams(
            collective_id=0, has_side_effects=True, vmem_limit_bytes=60 * 1024 * 1024),
    )(embeds.T, frequencies, phases[None, :], weights.T, labels)
    return trained_t.T, scores_t.T


def solution(mesh):
    placed = (P("clip", "feat"), P("clip", "feat"), P("feat"), P("feat", "clip"), P("clip", None))
    return jax.shard_map(
        per_device,
        mesh=mesh,
        in_specs=placed,
        out_specs=(P("feat", "clip"), P("clip", "feat")),
        check_vma=False,
    )
```

```python
import functools
import math

import jax
import jax.numpy as jnp
from jax import lax
from jax.experimental import pallas as pl
from jax.experimental.pallas import tpu as pltpu
from jax.sharding import PartitionSpec as P

STEPS = 2
MESH = pl.DeviceIdType.MESH

NY = 4
NZ = 8

PI_A = 3.1416015625
PI_B = -8.909031748771667e-06
PI_C = 1.2154188766544394e-10
SIN = (9.99999976e-01, -1.66666473e-01, 8.33289467e-03, -1.98005800e-04, 2.58984559e-06)


def scaled_cos(x, scale):
    q = jnp.round(x * (0.5 / math.pi))
    w = ((0.5 * x - q * PI_A) - q * PI_B) - q * PI_C
    w2 = w * w
    p = SIN[4]
    for c in SIN[3::-1]:
        p = p * w2 + c
    s = w * p
    return scale - (2.0 * scale) * (s * s)


def bytes_of(ref, sem):
    pltpu.make_async_copy(ref, ref, sem).wait()


def kernel(
    scale,
    e_ref, f_ref, ph_ref, w_ref, lab_ref,
    tr_ref, sc_ref,
    e_all, f_all, e_raw, e_two, f_rel,
    e3, f3, ang, phi, lab_t,
    w_own, w_send, w_t,
    part, c_send, c_recv, l_send, l_recv, r_t,
    grad, g_send, g_recv,
    eq_s, eq_r, er_s, er_r, ep_s, ep_r,
    fx_s, fx_r, fy_s, fy_r,
    w_s, w_r, c_s, c_r, l_s, l_r, r_s, r_r, rc_s, rc_r, g_s, g_r,
):
    clip = lax.axis_index("clip")
    feat = lax.axis_index("feat")
    c = lax.rem(feat, 2)
    xl = lax.rem(feat // 2, 2)
    z = feat // 4
    y = lax.rem(clip, NY)
    xh = clip // NY

    ke = e_ref.shape[0]
    kc = 4 * ke
    nf = f_ref.shape[1]
    nn = e_ref.shape[1]
    half = nn // 2
    quarter = nn // 4
    kw = w_ref.shape[0]

    def feat_of(z_, xl_, c_):
        return (z_ * 2 + xl_) * 2 + c_

    def clip_of(u, dy):
        return ((1 - xh) if u else xh) * NY + lax.rem(y + dy, NY)

    partner = (clip, feat_of(z, xl, 1 - c))
    x_near = (clip, feat_of(z, 1 - xl, c))
    diag = (clip, feat_of(z, 1 - xl, 1 - c))
    x_cross = (clip_of(1, 0), feat_of(z, 1 - xl, c))
    y_right = (clip_of(0, 1), feat)
    y_left = (clip_of(0, NY - 1), feat)
    z_up = (clip, feat_of(lax.rem(z + 1, NZ), xl, c))
    z_down = (clip, feat_of(lax.rem(z + NZ - 1, NZ), xl, c))

    def feat_peer(dz, dx):
        return lax.rem(z + dz, NZ), (1 - xl if dx else xl)

    feat_offsets = [(dz, dx) for dz in (4, 3, 5, 2, 6, 1, 7, 0) for dx in (1, 0) if (dz, dx) != (0, 0)]
    clip_offsets = [(u, dy) for dy in (2, 1, 3, 0) for u in (1, 0) if (u, dy) != (0, 0)]

    def slot_of(u, dy):
        return u * NY + dy - 1

    barrier = pltpu.get_barrier_semaphore()
    neighbours = [partner, x_near, x_cross, diag, z_up, z_down, y_right, y_left]
    for peer in neighbours:
        pl.semaphore_signal(barrier, inc=1, device_id=peer, device_id_type=MESH)

    my_rows = pl.ds(pl.multiple_of(clip * kw, kw), kw)
    w_own[...] = w_ref[...]
    w_send[0] = w_ref[...].astype(jnp.bfloat16)
    w_t[0, my_rows, :] = w_ref[...].astype(jnp.bfloat16)

    pl.semaphore_wait(barrier, len(neighbours))

    sends = []

    def put(src, dst, s_sem, r_sem, to, own_sem=True):
        copy = pltpu.make_async_remote_copy(
            src_ref=src, dst_ref=dst, send_sem=s_sem, recv_sem=r_sem, device_id=to, device_id_type=MESH)
        copy.start()
        if own_sem:
            sends.append(copy)

    lanes_c = pl.ds(pl.multiple_of(c * half, half), half)
    lanes_o = pl.ds(pl.multiple_of((1 - c) * half, half), half)

    def e_rows(z_, xl_):
        return pl.ds(pl.multiple_of(z_ * kc + xl_ * (2 * ke), 8), 2 * ke)

    def e_piece(z_, xl_):
        return e_all.at[e_rows(z_, xl_), lanes_c]

    def f_block(clip_, lo, hi):
        return f_all.at[pl.ds(pl.multiple_of(clip_ * kc + lo, 8), hi - lo), :]

    def send_w(u, dy):
        put(w_send.at[0], w_t.at[0, my_rows, :], w_s.at[0], w_r.at[0], (clip_of(u, dy), feat), False)

    put(e_ref.at[:, lanes_o], e_raw.at[0], eq_s.at[0], eq_r.at[0], partner)
    put(e_ref.at[:, lanes_c], e_raw.at[1], eq_s.at[1], eq_r.at[1], x_near)
    put(e_ref.at[:, lanes_o], e_raw.at[2], eq_s.at[2], eq_r.at[2], diag)

    cut = kc // 3
    mid = kc // 2
    put(f_ref.at[cut:kc, :], f_rel.at[cut:kc, :], fx_s.at[1], fx_r.at[1], x_cross)
    put(f_ref.at[0:cut, :], f_rel.at[0:cut, :], fx_s.at[0], fx_r.at[0], x_near)
    lows = (0, mid)

    def f_send(direction, u, k, clip_, lo, hi, src=None):
        dst = f_block(clip_, lo, hi)
        put(dst if src is None else src, dst, fy_s.at[direction, u, k], fy_r.at[direction, u, k],
            y_right if direction == 0 else y_left)

    for k in (0, 1):
        for direction in (0, 1):
            lo = lows[k ^ direction]
            f_send(direction, 0, k, clip, lo, lo + mid, f_ref.at[lo:lo + mid, :])
    for dy in (1, 3):
        send_w(0, dy)

    def join(own, oth):
        first = c == 0
        e_two[0:ke, :] = jnp.where(first, own, oth)
        e_two[ke:2 * ke, :] = jnp.where(first, oth, own)
        return e_two[...]

    def e_start(o, xl_):
        piece = e_piece(z, xl_)
        put(piece, piece, er_s.at[0, o, 0], er_r.at[0, o, 0], z_up)
        put(piece, piece, er_s.at[1, o, 0], er_r.at[1, o, 0], z_down)
        put(piece, piece, ep_s.at[o, 0], ep_r.at[0], partner)

    bytes_of(e_raw.at[0], eq_r.at[0])
    e_all[e_rows(z, xl), lanes_c] = join(e_ref[:, lanes_c], e_raw[0])
    e_start(0, xl)

    f_all[pl.ds(pl.multiple_of(clip * kc, 8), kc), :] = f_ref[...]
    qn = pl.multiple_of((2 * c + xl) * quarter, quarter)
    lab_t[...] = lab_ref[pl.ds(qn, quarter), :].astype(jnp.float32).T
    for b in range(nf // 128):
        column = jnp.broadcast_to(ph_ref[b:b + 1, :], (128, 128)).T
        for n in range(nn // 128):
            ang[128 * b:128 * b + 128, 128 * n:128 * n + 128] = column

    bytes_of(e_raw.at[1], eq_r.at[1])
    bytes_of(e_raw.at[2], eq_r.at[2])
    e_all[e_rows(z, 1 - xl), lanes_c] = join(e_raw[1], e_raw[2])
    e_start(1, 1 - xl)

    def e_step(direction, o, s):
        dz = (NZ - s) if direction == 0 else s
        z_ = lax.rem(z + dz, NZ)
        xl_ = (1 - xl) if o else xl
        piece = e_piece(z_, xl_)
        bytes_of(piece, er_r.at[direction, o, s - 1])
        if s < 3 or (s == 3 and o == direction):
            put(piece, piece, er_s.at[direction, o, s], er_r.at[direction, o, s], z_up if direction == 0 else z_down)
        put(piece, piece, ep_s.at[o, dz], ep_r.at[dz], partner)

    def e_prep(dz, lanes):
        z_ = lax.rem(z + dz, NZ)
        x = e_all[pl.ds(pl.multiple_of(z_ * kc, 16), kc), lanes]
        hi = x.astype(jnp.bfloat16)
        e3[z_, 0:kc, lanes] = hi
        e3[z_, kc:2 * kc, lanes] = (x - hi.astype(jnp.float32)).astype(jnp.bfloat16)
        e3[z_, 2 * kc:3 * kc, lanes] = hi

    def e_other(dz):
        z_ = lax.rem(z + dz, NZ)
        bytes_of(e_all.at[pl.ds(pl.multiple_of(z_ * kc, 16), kc), lanes_o], ep_r.at[dz])
        e_prep(dz, lanes_o)

    def f_prep(u, dy):
        j = clip_of(u, dy)
        x = f_all[pl.ds(pl.multiple_of(j * kc, 16), kc), :]
        hi = x.astype(jnp.bfloat16)
        lo = (x - hi.astype(jnp.float32)).astype(jnp.bfloat16)
        f3[j] = jnp.concatenate([hi, hi, lo], axis=0).T

    def f_wait(direction, u, k, clip_, lo, hi):
        bytes_of(f_block(clip_, lo, hi), fy_r.at[direction, u, k])

    dot = functools.partial(jnp.dot, preferred_element_type=jnp.float32)

    def stage_of(j):
        up = lax.rem(j - z + NZ, NZ)
        e_turn = jnp.minimum(up, NZ - up)
        right = lax.rem(lax.rem(j, NY) - y + NY, NY)
        away = jnp.minimum(right, NY - right)
        f_turn = jnp.where(j // NY == xh, away, 2 + away + away // 2)
        return jnp.maximum(e_turn, f_turn)

    def products(stage, first, last):
        @pl.loop(first, last)
        def _(j):
            @pl.when(stage_of(j) == stage)
            def _():
                @pl.loop(0, nn // 256)
                def _(n):
                    cols = pl.ds(pl.multiple_of(n * 256, 256), 256)
                    ang[:, cols] = ang[:, cols] + dot(f3[j], e3[j, :, cols])

    e_step(0, 0, 1)
    e_step(1, 0, 1)
    f_wait(0, 0, 0, clip_of(0, 3), 0, mid)
    f_send(0, 0, 2, clip_of(0, 3), 0, mid)
    f_wait(1, 0, 0, clip_of(0, 1), mid, kc)
    f_send(1, 0, 2, clip_of(0, 1), mid, kc)
    bytes_of(f_rel.at[cut:kc, :], fx_r.at[1])
    put(f_rel.at[cut:kc, :], f_block(clip_of(1, 0), cut, kc), fx_s.at[3], fx_r.at[3], x_near)
    bytes_of(f_rel.at[0:cut, :], fx_r.at[0])
    put(f_rel.at[0:cut, :], f_block(clip, 0, cut), fx_s.at[2], fx_r.at[2], x_cross)
    e_prep(0, lanes_c)
    f_prep(0, 0)
    e_other(0)
    products(0, 0, 8)
    e_step(0, 1, 1)
    e_step(1, 1, 1)
    e_prep(1, lanes_c)
    e_prep(7, lanes_c)
    e_step(0, 0, 2)
    e_step(1, 0, 2)
    f_wait(0, 0, 1, clip_of(0, 3), mid, kc)
    f_wait(1, 0, 1, clip_of(0, 1), 0, mid)
    over = clip_of(1, 0)
    bytes_of(f_block(over, 0, cut), fx_r.at[2])
    f_send(0, 1, 0, over, 0, cut)
    f_send(1, 1, 0, over, 0, cut)
    bytes_of(f_block(over, cut, kc), fx_r.at[3])
    f_send(0, 1, 1, over, cut, mid)
    f_send(1, 1, 1, over, mid, kc)
    f_send(0, 1, 2, over, mid, kc)
    f_send(1, 1, 2, over, cut, mid)
    send_w(1, 0)
    f_prep(0, 1)
    f_prep(0, 3)
    e_step(0, 1, 2)
    e_step(1, 1, 2)
    e_other(1)
    e_other(7)
    products(1, 0, 8)
    e_prep(2, lanes_c)
    e_prep(6, lanes_c)
    f_wait(0, 0, 2, clip_of(0, 2), 0, mid)
    f_wait(1, 0, 2, clip_of(0, 2), mid, kc)
    send_w(0, 2)
    f_prep(0, 2)
    f_prep(1, 0)
    e_step(0, 0, 3)
    e_step(1, 0, 3)
    e_other(2)
    e_other(6)
    f_wait(0, 1, 0, clip_of(1, 3), 0, cut)
    f_wait(0, 1, 1, clip_of(1, 3), cut, mid)
    f_send(0, 1, 3, clip_of(1, 3), 0, mid)
    f_wait(1, 1, 0, clip_of(1, 1), 0, cut)
    f_wait(1, 1, 1, clip_of(1, 1), mid, kc)
    f_send(1, 1, 3, clip_of(1, 1), mid, kc)
    products(2, 0, 4)
    e_step(0, 1, 3)
    e_step(1, 1, 3)
    products(2, 4, 8)
    e_prep(3, lanes_c)
    e_prep(5, lanes_c)
    f_wait(0, 1, 2, clip_of(1, 3), mid, kc)
    f_wait(1, 1, 2, clip_of(1, 1), cut, mid)
    send_w(1, 1)
    send_w(1, 3)
    f_prep(1, 1)
    f_prep(1, 3)
    e_step(0, 0, 4)
    e_step(1, 1, 4)
    e_prep(4, lanes_c)
    e_other(3)
    e_other(5)
    products(3, 0, 8)
    e_other(4)
    products(4, 0, 8)
    last_block = clip_of(1, 2)
    f_wait(0, 1, 3, last_block, 0, mid)
    f_wait(1, 1, 3, last_block, mid, kc)
    send_w(1, 2)
    f_prep(1, 2)

    @pl.loop(0, nn // 256)
    def _(n):
        cols = pl.ds(pl.multiple_of(n * 256, 256), 256)
        for m in range(nf // 128):
            rows = slice(128 * m, 128 * m + 128)
            x = ang[rows, cols] + dot(f3[last_block, rows, :], e3[last_block, :, cols])
            phi[rows, cols] = scaled_cos(x, scale).astype(jnp.bfloat16)

    my_block = pl.ds(pl.multiple_of(z * 16, 16), 16)
    my_lanes = pl.ds(pl.multiple_of(xl * quarter, quarter), quarter)

    def exchange(t, source, own):
        for dz, dx in feat_offsets:
            pz, px = feat_peer(dz, dx)
            put(source(pz, px), l_recv.at[t, dx * NZ + dz - 1], l_s.at[t], l_r.at[t], (clip, feat_of(pz, px, c)), False)
        acc = own()
        bytes_of(l_recv.at[t], l_r.at[t])
        for i in range(2 * NZ - 1):
            acc = acc + l_recv[t, i].astype(jnp.float32)
        return acc

    def summed_logits(t):
        w = w_t[t]
        c_send[t] = dot(w, phi[:, lanes_o]).astype(jnp.bfloat16)
        put(c_send.at[t], c_recv.at[t], c_s.at[t], c_r.at[t], partner)
        part[...] = dot(w, phi[:, lanes_c])
        bytes_of(c_recv.at[t], c_r.at[t])
        total = part[...] + c_recv[t].astype(jnp.float32)
        part[...] = total
        l_send[t] = total.astype(jnp.bfloat16)

        def source(pz, px):
            return l_send.at[t, pl.ds(pl.multiple_of(pz * 16, 16), 16), pl.ds(pl.multiple_of(px * quarter, quarter), quarter)]

        return exchange(t, source, lambda: part[my_block, my_lanes])

    nt = (((1,), (1,)), ((), ()))
    full_lanes = pl.ds(pl.multiple_of(c * half + xl * quarter, quarter), quarter)

    for t in range(STEPS):
        bytes_of(g_recv.at[0], w_r.at[t])
        acc = summed_logits(t)
        residual = (jax.nn.sigmoid(acc) - lab_t[my_block, :]).astype(jnp.bfloat16)
        r_t[t, my_block, full_lanes] = residual
        mine_r = r_t.at[t, my_block, full_lanes]
        for dz, dx in feat_offsets:
            pz, px = feat_peer(dz, dx)
            put(mine_r, mine_r, r_s.at[t], r_r.at[t], (clip, feat_of(pz, px, c)), False)
        bytes_of(l_recv.at[t], r_r.at[t])
        half_r = r_t.at[t, :, lanes_c]
        put(half_r, half_r, rc_s.at[t], rc_r.at[t], partner)
        grad[...] = lax.dot_general(r_t[t, :, lanes_c], phi[:, lanes_c], nt, preferred_element_type=jnp.float32)
        bytes_of(r_t.at[t, :, lanes_o], rc_r.at[t])
        total = grad[...] + lax.dot_general(r_t[t, :, lanes_o], phi[:, lanes_o], nt, preferred_element_type=jnp.float32)
        grad[...] = total
        g_send[t] = total.astype(jnp.bfloat16)
        for u, dy in clip_offsets:
            j = clip_of(u, dy)
            put(g_send.at[t, pl.ds(pl.multiple_of(j * kw, kw), kw), :], g_recv.at[t, slot_of(u, dy)], g_s.at[t], g_r.at[t], (j, feat), False)
        g = grad[my_rows, :]
        bytes_of(g_recv.at[t], g_r.at[t])
        for i in range(7):
            g = g + g_recv[t, i].astype(jnp.float32)
        w_new = w_own[...] - 0.25 * g
        w_own[...] = w_new
        w_half = w_new.astype(jnp.bfloat16)
        w_send[t + 1] = w_half
        w_t[t + 1, my_rows, :] = w_half
        for u, dy in clip_offsets:
            put(w_send.at[t + 1], w_t.at[t + 1, my_rows, :], w_s.at[t + 1], w_r.at[t + 1], (clip_of(u, dy), feat), False)
    tr_ref[...] = w_own[...]

    t = STEPS
    bytes_of(g_recv.at[0], w_r.at[t])
    row = lax.broadcasted_iota(jnp.int32, (2 * 128, 128), 0)
    col = lax.broadcasted_iota(jnp.int32, (2 * 128, 128), 1)
    row_q = lax.broadcasted_iota(jnp.int32, (2 * 128, 1), 0) // 4 % 4

    def chip_blocks(core):
        pick = col == 8 * (row // 16) + 4 * core + row % 4
        w = dot(pick.astype(jnp.float32).astype(jnp.bfloat16), w_t[t])
        out = jnp.zeros((2 * 128, quarter), jnp.float32)
        for q in range(4):
            w_q = jnp.where(row_q == q, w, 0.0).astype(jnp.bfloat16)
            out = out + dot(w_q, phi[:, q * quarter:(q + 1) * quarter])
        return out

    out = chip_blocks(1 - c).astype(jnp.bfloat16)
    l_send[t, :, 0:quarter] = out[0:128, :]
    l_send[t, :, quarter:half] = out[128:256, :]
    put(l_send.at[t], c_recv.at[t], c_s.at[t], c_r.at[t], partner)
    out = chip_blocks(c)
    bytes_of(c_recv.at[t], c_r.at[t])
    for h in range(2):
        lanes = slice(h * quarter, (h + 1) * quarter)
        total = out[128 * h:128 * h + 128, :] + c_recv[t, :, lanes].astype(jnp.float32)
        part[:, lanes] = total
        c_send[t, :, lanes] = total.astype(jnp.bfloat16)

    def block_of(z_, xl_):
        i = 2 * z_ + xl_
        return pl.ds(pl.multiple_of(lax.rem(i, 8) * 16, 16), 16), pl.ds(pl.multiple_of(i // 8 * quarter, quarter), quarter)

    acc = exchange(t, lambda pz, px: c_send.at[(t, *block_of(pz, px))], lambda: part[block_of(z, xl)])
    for q in range(4):
        sc_ref[:, q * quarter:(q + 1) * quarter] = acc[4 * q:4 * q + 4, :]

    for copy in sends:
        copy.wait_send()
    for t in range(STEPS + 1):
        bytes_of(g_recv.at[0], w_s.at[t])
        bytes_of(l_recv.at[0], l_s.at[t])
    for t in range(STEPS):
        bytes_of(l_recv.at[0], r_s.at[t])
        bytes_of(g_recv.at[0], g_s.at[t])


def per_device(embeds, frequencies, phases, weights, labels):
    nn, ke = embeds.shape
    kc, nf = frequencies.shape
    kw = weights.shape[1]
    kk = labels.shape[1]
    kt = kc * lax.axis_size("clip")
    total_features = nf * lax.axis_size("feat")
    scale = math.sqrt(2.0 / total_features)
    f32, b16 = jnp.float32, jnp.bfloat16
    dma = pltpu.SemaphoreType.DMA
    vm = pl.BlockSpec(memory_space=pltpu.VMEM)
    half, quarter = nn // 2, nn // 4
    steps = STEPS + 1
    scratch = [
        pltpu.VMEM((kt, nn), f32),
        pltpu.VMEM((kt, nf), f32),
        pltpu.VMEM((3, ke, half), f32),
        pltpu.VMEM((2 * ke, half), f32),
        pltpu.VMEM((kc, nf), f32),
        pltpu.VMEM((8, 3 * kc, nn), b16),
        pltpu.VMEM((8, nf, 3 * kc), b16),
        pltpu.VMEM((nf, nn), f32),
        pltpu.VMEM((nf, nn), b16),
        pltpu.VMEM((kk, quarter), f32),
        pltpu.VMEM((kw, nf), f32),
        pltpu.VMEM((steps, kw, nf), b16),
        pltpu.VMEM((steps, kk, nf), b16),
        pltpu.VMEM((kk, half), f32),
        pltpu.VMEM((steps, kk, half), b16),
        pltpu.VMEM((steps, kk, half), b16),
        pltpu.VMEM((steps, kk, half), b16),
        pltpu.VMEM((steps, 2 * NZ - 1, 16, quarter), b16),
        pltpu.VMEM((STEPS, kk, nn), b16),
        pltpu.VMEM((kk, nf), f32),
        pltpu.VMEM((STEPS, kk, nf), b16),
        pltpu.VMEM((STEPS, 7, kw, nf), b16),
        dma((3,)), dma((3,)), dma((2, 2, 4)), dma((2, 2, 4)), dma((2, NZ)), dma((NZ,)),
        dma((4,)), dma((4,)), dma((2, 2, 4)), dma((2, 2, 4)),
        dma((steps,)), dma((steps,)), dma((steps,)), dma((steps,)), dma((steps,)), dma((steps,)),
        dma((STEPS,)), dma((STEPS,)), dma((STEPS,)), dma((STEPS,)), dma((STEPS,)), dma((STEPS,)),
    ]
    trained_t, scores_t = pl.pallas_call(
        functools.partial(kernel, scale),
        out_shape=(jax.ShapeDtypeStruct((kw, nf), f32), jax.ShapeDtypeStruct((4, nn), f32)),
        in_specs=[vm] * 5,
        out_specs=(vm, vm),
        scratch_shapes=scratch,
        compiler_params=pltpu.CompilerParams(
            collective_id=0, has_side_effects=True, vmem_limit_bytes=60 * 1024 * 1024),
    )(embeds.T, frequencies, phases.reshape(nf // 128, 128), weights.T, labels)
    return trained_t.T, scores_t.T


def solution(mesh):
    placed = (P("clip", "feat"), P("clip", "feat"), P("feat"), P("feat", "clip"), P("clip", None))
    return jax.shard_map(
        per_device,
        mesh=mesh,
        in_specs=placed,
        out_specs=(P("feat", "clip"), P("clip", "feat")),
        check_vma=False,
    )
```

```python
import functools
import math

import jax
import jax.numpy as jnp
from jax import lax
from jax.experimental import pallas as pl
from jax.experimental.pallas import tpu as pltpu
from jax.sharding import PartitionSpec as P

STEPS = 2
MESH = pl.DeviceIdType.MESH

NY = 4
NZ = 8

PI_A = 3.1416015625
PI_B = -8.909031748771667e-06
PI_C = 1.2154188766544394e-10
SIN = (9.99999976e-01, -1.66666473e-01, 8.33289467e-03, -1.98005800e-04, 2.58984559e-06)


def scaled_cos(x, scale):
    q = jnp.round(x * (0.5 / math.pi))
    w = ((0.5 * x - q * PI_A) - q * PI_B) - q * PI_C
    w2 = w * w
    p = SIN[4]
    for c in SIN[3::-1]:
        p = p * w2 + c
    s = w * p
    return scale - (2.0 * scale) * (s * s)


def bytes_of(ref, sem):
    pltpu.make_async_copy(ref, ref, sem).wait()


def kernel(
    scale,
    e_hbm, f_hbm, ph_hbm, w_hbm, lab_hbm,
    tr_hbm, sc_hbm,
    e_ref, f_ref, ph_ref, w_ref, lab_ref, sc_ref, picks,
    e_all, f_all, e_raw, e_two, f_rel,
    e3, f3, ang, phi, lab_t,
    w_own, w_send, w_t,
    part, c_send, c_recv, l_send, l_recv, r_t,
    grad, g_send, g_recv, logits,
    eq_s, eq_r, er_s, er_r, ep_s, ep_r,
    fx_s, fx_r, fy_s, fy_r,
    w_s, w_r, c_s, c_r, l_s, l_r, r_s, r_r, rc_s, rc_r, g_s, g_r,
    in_s, out_s, hello,
):
    loads = [
        pltpu.make_async_copy(src, dst, in_s.at[i])
        for i, (src, dst) in enumerate(
            ((e_hbm, e_ref), (f_hbm, f_ref), (w_hbm, w_ref), (ph_hbm, ph_ref), (lab_hbm, lab_ref)))
    ]
    for load in loads:
        load.start()

    clip = lax.axis_index("clip")
    feat = lax.axis_index("feat")
    c = lax.rem(feat, 2)
    xl = lax.rem(feat // 2, 2)
    z = feat // 4
    y = lax.rem(clip, NY)
    xh = clip // NY

    ke = e_ref.shape[0]
    kc = 4 * ke
    nf = f_ref.shape[1]
    nn = e_ref.shape[1]
    half = nn // 2
    quarter = nn // 4
    kw = w_ref.shape[0]

    def feat_of(z_, xl_, c_):
        return (z_ * 2 + xl_) * 2 + c_

    def clip_of(u, dy):
        return ((1 - xh) if u else xh) * NY + lax.rem(y + dy, NY)

    partner = (clip, feat_of(z, xl, 1 - c))
    x_near = (clip, feat_of(z, 1 - xl, c))
    diag = (clip, feat_of(z, 1 - xl, 1 - c))
    x_cross = (clip_of(1, 0), feat_of(z, 1 - xl, c))
    y_right = (clip_of(0, 1), feat)
    y_left = (clip_of(0, NY - 1), feat)
    z_up = (clip, feat_of(lax.rem(z + 1, NZ), xl, c))
    z_down = (clip, feat_of(lax.rem(z + NZ - 1, NZ), xl, c))

    def feat_peer(dz, dx):
        return lax.rem(z + dz, NZ), (1 - xl if dx else xl)

    feat_offsets = [(dz, dx) for dz in (4, 3, 5, 2, 6, 1, 7, 0) for dx in (1, 0) if (dz, dx) != (0, 0)]
    clip_offsets = [(u, dy) for dy in (2, 1, 3, 0) for u in (1, 0) if (u, dy) != (0, 0)]

    def slot_of(u, dy):
        return u * NY + dy - 1

    barrier = pltpu.get_barrier_semaphore()
    neighbours = [partner, x_near, x_cross, diag, z_up, z_down, y_right, y_left]
    for peer in neighbours:
        pl.semaphore_signal(barrier, inc=1, device_id=peer, device_id_type=MESH)

    my_rows = pl.ds(pl.multiple_of(clip * kw, kw), kw)
    for load in loads[0:3]:
        load.wait()
    w_own[...] = w_ref[...]
    w_send[0] = w_ref[...].astype(jnp.bfloat16)
    w_t[0, my_rows, :] = w_ref[...].astype(jnp.bfloat16)

    pl.semaphore_wait(barrier, len(neighbours))

    def greet(n):
        for peer in (x_near, x_cross, y_right, y_left):
            pl.semaphore_signal(hello.at[n], inc=1, device_id=peer, device_id_type=MESH)

    def greeted(n):
        pl.semaphore_wait(hello.at[n], 4)

    greet(0)
    sends = []

    def put(src, dst, s_sem, r_sem, to, own_sem=True):
        copy = pltpu.make_async_remote_copy(
            src_ref=src, dst_ref=dst, send_sem=s_sem, recv_sem=r_sem, device_id=to, device_id_type=MESH)
        copy.start()
        if own_sem:
            sends.append(copy)

    lanes_c = pl.ds(pl.multiple_of(c * half, half), half)
    lanes_o = pl.ds(pl.multiple_of((1 - c) * half, half), half)

    def e_rows(z_, xl_):
        return pl.ds(pl.multiple_of(z_ * kc + xl_ * (2 * ke), 8), 2 * ke)

    def e_piece(z_, xl_):
        return e_all.at[e_rows(z_, xl_), lanes_c]

    def f_block(clip_, lo, hi):
        return f_all.at[pl.ds(pl.multiple_of(clip_ * kc + lo, 8), hi - lo), :]

    def send_w(u, dy):
        put(w_send.at[0], w_t.at[0, my_rows, :], w_s.at[0], w_r.at[0], (clip_of(u, dy), feat), False)

    put(e_ref.at[:, lanes_o], e_raw.at[0], eq_s.at[0], eq_r.at[0], partner)
    put(e_ref.at[:, lanes_c], e_raw.at[1], eq_s.at[1], eq_r.at[1], x_near)
    put(e_ref.at[:, lanes_o], e_raw.at[2], eq_s.at[2], eq_r.at[2], diag)

    cut = kc // 3
    mid = kc // 2
    put(f_ref.at[cut:kc, :], f_rel.at[cut:kc, :], fx_s.at[1], fx_r.at[1], x_cross)
    put(f_ref.at[0:cut, :], f_rel.at[0:cut, :], fx_s.at[0], fx_r.at[0], x_near)
    lows = (0, mid)

    def f_send(direction, u, k, clip_, lo, hi, src=None):
        dst = f_block(clip_, lo, hi)
        put(dst if src is None else src, dst, fy_s.at[direction, u, k], fy_r.at[direction, u, k],
            y_right if direction == 0 else y_left)

    for k in (0, 1):
        for direction in (0, 1):
            lo = lows[k ^ direction]
            f_send(direction, 0, k, clip, lo, lo + mid, f_ref.at[lo:lo + mid, :])
    greeted(0)
    greet(1)

    def join(own, oth):
        first = c == 0
        e_two[0:ke, :] = jnp.where(first, own, oth)
        e_two[ke:2 * ke, :] = jnp.where(first, oth, own)
        return e_two[...]

    def e_start(o, xl_):
        piece = e_piece(z, xl_)
        put(piece, piece, er_s.at[0, o, 0], er_r.at[0, o, 0], z_up)
        put(piece, piece, er_s.at[1, o, 0], er_r.at[1, o, 0], z_down)
        put(piece, piece, ep_s.at[o, 0], ep_r.at[0], partner)

    bytes_of(e_raw.at[0], eq_r.at[0])
    e_all[e_rows(z, xl), lanes_c] = join(e_ref[:, lanes_c], e_raw[0])
    e_start(0, xl)

    greeted(1)
    greet(2)
    for load in loads[3:]:
        load.wait()
    f_all[pl.ds(pl.multiple_of(clip * kc, 8), kc), :] = f_ref[...]
    row = lax.broadcasted_iota(jnp.int32, (2 * 128, 128), 0)
    col = lax.broadcasted_iota(jnp.int32, (2 * 128, 128), 1)
    for core in range(2):
        there = col == 8 * (row // 16) + 4 * core + row % 4
        for q in range(4):
            pick = there & (row // 4 % 4 == q)
            picks[core, q] = jnp.where(pick, 1.0, 0.0).astype(jnp.bfloat16)
    qn = pl.multiple_of((2 * c + xl) * quarter, quarter)
    lab_t[...] = lab_ref[pl.ds(qn, quarter), :].astype(jnp.float32).T
    for b in range(nf // 128):
        column = jnp.broadcast_to(ph_ref[b:b + 1, :], (128, 128)).T
        for n in range(nn // 128):
            ang[128 * b:128 * b + 128, 128 * n:128 * n + 128] = column
    greeted(2)
    for u, dy in clip_offsets:
        send_w(u, dy)

    bytes_of(e_raw.at[1], eq_r.at[1])
    bytes_of(e_raw.at[2], eq_r.at[2])
    e_all[e_rows(z, 1 - xl), lanes_c] = join(e_raw[1], e_raw[2])
    e_start(1, 1 - xl)

    def e_step(direction, o, s):
        dz = (NZ - s) if direction == 0 else s
        z_ = lax.rem(z + dz, NZ)
        xl_ = (1 - xl) if o else xl
        piece = e_piece(z_, xl_)
        bytes_of(piece, er_r.at[direction, o, s - 1])
        if s < 3 or (s == 3 and o == direction):
            put(piece, piece, er_s.at[direction, o, s], er_r.at[direction, o, s], z_up if direction == 0 else z_down)
        put(piece, piece, ep_s.at[o, dz], ep_r.at[dz], partner)

    def e_prep(dz, lanes):
        z_ = lax.rem(z + dz, NZ)
        x = e_all[pl.ds(pl.multiple_of(z_ * kc, 16), kc), lanes]
        hi = x.astype(jnp.bfloat16)
        e3[z_, 0:kc, lanes] = hi
        e3[z_, kc:2 * kc, lanes] = (x - hi.astype(jnp.float32)).astype(jnp.bfloat16)
        e3[z_, 2 * kc:3 * kc, lanes] = hi

    def e_other(dz):
        z_ = lax.rem(z + dz, NZ)
        bytes_of(e_all.at[pl.ds(pl.multiple_of(z_ * kc, 16), kc), lanes_o], ep_r.at[dz])
        e_prep(dz, lanes_o)

    def f_prep(u, dy):
        j = clip_of(u, dy)
        x = f_all[pl.ds(pl.multiple_of(j * kc, 16), kc), :]
        hi = x.astype(jnp.bfloat16)
        lo = (x - hi.astype(jnp.float32)).astype(jnp.bfloat16)
        f3[j] = jnp.concatenate([hi, hi, lo], axis=0).T

    def f_wait(direction, u, k, clip_, lo, hi):
        bytes_of(f_block(clip_, lo, hi), fy_r.at[direction, u, k])

    dot = functools.partial(jnp.dot, preferred_element_type=jnp.float32)

    def stage_of(j):
        up = lax.rem(j - z + NZ, NZ)
        e_turn = jnp.minimum(up, NZ - up)
        right = lax.rem(lax.rem(j, NY) - y + NY, NY)
        away = jnp.minimum(right, NY - right)
        f_turn = jnp.where(j // NY == xh, away, 2 + away + away // 2)
        return jnp.maximum(e_turn, f_turn)

    def products(stage, first, count):
        @pl.loop(0, count)
        def _(i):
            j = lax.rem(xh * NY + first + i, 2 * NY)

            @pl.when(stage_of(j) == stage)
            def _():
                ang[...] = ang[...] + dot(f3[j], e3[j])

    e_step(0, 0, 1)
    e_step(1, 0, 1)
    f_wait(0, 0, 0, clip_of(0, 3), 0, mid)
    f_send(0, 0, 2, clip_of(0, 3), 0, mid)
    f_wait(1, 0, 0, clip_of(0, 1), mid, kc)
    f_send(1, 0, 2, clip_of(0, 1), mid, kc)
    bytes_of(f_rel.at[cut:kc, :], fx_r.at[1])
    put(f_rel.at[cut:kc, :], f_block(clip_of(1, 0), cut, kc), fx_s.at[3], fx_r.at[3], x_near)
    bytes_of(f_rel.at[0:cut, :], fx_r.at[0])
    put(f_rel.at[0:cut, :], f_block(clip, 0, cut), fx_s.at[2], fx_r.at[2], x_cross)
    e_prep(0, lanes_c)
    f_prep(0, 0)
    e_other(0)
    products(0, 0, 8)
    e_step(0, 1, 1)
    e_step(1, 1, 1)
    e_prep(1, lanes_c)
    e_prep(7, lanes_c)
    f_wait(0, 0, 1, clip_of(0, 3), mid, kc)
    f_wait(1, 0, 1, clip_of(0, 1), 0, mid)
    f_prep(0, 1)
    f_prep(0, 3)
    over = clip_of(1, 0)
    bytes_of(f_block(over, 0, cut), fx_r.at[2])
    f_send(0, 1, 0, over, 0, cut)
    f_send(1, 1, 0, over, 0, cut)
    e_step(0, 0, 2)
    e_step(1, 0, 2)
    e_other(1)
    e_other(7)
    bytes_of(f_block(over, cut, kc), fx_r.at[3])
    f_send(0, 1, 1, over, cut, mid)
    f_send(1, 1, 1, over, mid, kc)
    f_send(0, 1, 2, over, mid, kc)
    f_send(1, 1, 2, over, cut, mid)
    products(1, 0, 4)
    e_step(0, 1, 2)
    e_step(1, 1, 2)
    products(1, 4, 4)
    e_prep(2, lanes_c)
    e_prep(6, lanes_c)
    f_wait(0, 0, 2, clip_of(0, 2), 0, mid)
    f_wait(1, 0, 2, clip_of(0, 2), mid, kc)
    f_prep(0, 2)
    f_prep(1, 0)
    e_other(2)
    e_other(6)
    e_step(0, 0, 3)
    e_step(1, 0, 3)
    products(2, 0, 2)
    f_wait(0, 1, 0, clip_of(1, 3), 0, cut)
    f_wait(0, 1, 1, clip_of(1, 3), cut, mid)
    f_send(0, 1, 3, clip_of(1, 3), 0, mid)
    f_wait(1, 1, 0, clip_of(1, 1), 0, cut)
    f_wait(1, 1, 1, clip_of(1, 1), mid, kc)
    f_send(1, 1, 3, clip_of(1, 1), mid, kc)
    products(2, 2, 2)
    e_step(0, 1, 3)
    e_step(1, 1, 3)
    products(2, 4, 4)
    e_prep(3, lanes_c)
    e_prep(5, lanes_c)
    f_wait(0, 1, 2, clip_of(1, 3), mid, kc)
    f_wait(1, 1, 2, clip_of(1, 1), cut, mid)
    f_prep(1, 1)
    f_prep(1, 3)
    e_step(0, 0, 4)
    e_other(3)
    e_other(5)
    products(3, 0, 4)
    e_step(1, 1, 4)
    e_prep(4, lanes_c)
    products(3, 4, 4)
    e_other(4)
    products(4, 0, 8)
    last_block = clip_of(1, 2)
    f_wait(0, 1, 3, last_block, 0, mid)
    f_wait(1, 1, 3, last_block, mid, kc)
    f_prep(1, 2)

    @pl.loop(0, nn // 256)
    def _(n):
        cols = pl.ds(pl.multiple_of(n * 256, 256), 256)
        for m in range(nf // 128):
            rows = slice(128 * m, 128 * m + 128)
            x = ang[rows, cols] + dot(f3[last_block, rows, :], e3[last_block, :, cols])
            phi[rows, cols] = scaled_cos(x, scale).astype(jnp.bfloat16)

    my_block = pl.ds(pl.multiple_of(z * 16, 16), 16)
    my_lanes = pl.ds(pl.multiple_of(xl * quarter, quarter), quarter)

    def exchange(t, source, own):
        for dz, dx in feat_offsets:
            pz, px = feat_peer(dz, dx)
            put(source(pz, px), l_recv.at[t, dx * NZ + dz - 1], l_s.at[t], l_r.at[t], (clip, feat_of(pz, px, c)), False)
        acc = own()
        bytes_of(l_recv.at[t], l_r.at[t])
        for i in range(2 * NZ - 1):
            acc = acc + l_recv[t, i].astype(jnp.float32)
        return acc

    def summed_logits(t):
        w = w_t[t]
        c_send[t] = dot(w, phi[:, lanes_o]).astype(jnp.bfloat16)
        put(c_send.at[t], c_recv.at[t], c_s.at[t], c_r.at[t], partner)
        part[...] = dot(w, phi[:, lanes_c])
        bytes_of(c_recv.at[t], c_r.at[t])
        total = part[...] + c_recv[t].astype(jnp.float32)
        part[...] = total
        l_send[t] = total.astype(jnp.bfloat16)

        def source(pz, px):
            return l_send.at[t, pl.ds(pl.multiple_of(pz * 16, 16), 16), pl.ds(pl.multiple_of(px * quarter, quarter), quarter)]

        return exchange(t, source, lambda: part[my_block, my_lanes])

    nt = (((1,), (1,)), ((), ()))
    full_lanes = pl.ds(pl.multiple_of(c * half + xl * quarter, quarter), quarter)

    for t in range(STEPS):
        bytes_of(g_recv.at[0], w_r.at[t])
        acc = summed_logits(t)
        residual = (jax.nn.sigmoid(acc) - lab_t[my_block, :]).astype(jnp.bfloat16)
        r_t[t, my_block, full_lanes] = residual
        mine_r = r_t.at[t, my_block, full_lanes]
        for dz, dx in feat_offsets:
            pz, px = feat_peer(dz, dx)
            put(mine_r, mine_r, r_s.at[t], r_r.at[t], (clip, feat_of(pz, px, c)), False)
        bytes_of(l_recv.at[t], r_r.at[t])
        half_r = r_t.at[t, :, lanes_c]
        put(half_r, half_r, rc_s.at[t], rc_r.at[t], partner)
        grad[...] = lax.dot_general(r_t[t, :, lanes_c], phi[:, lanes_c], nt, preferred_element_type=jnp.float32)
        bytes_of(r_t.at[t, :, lanes_o], rc_r.at[t])
        total = grad[...] + lax.dot_general(r_t[t, :, lanes_o], phi[:, lanes_o], nt, preferred_element_type=jnp.float32)
        grad[...] = total
        g_send[t] = total.astype(jnp.bfloat16)
        for u, dy in clip_offsets:
            j = clip_of(u, dy)
            put(g_send.at[t, pl.ds(pl.multiple_of(j * kw, kw), kw), :], g_recv.at[t, slot_of(u, dy)], g_s.at[t], g_r.at[t], (j, feat), False)
        g = grad[my_rows, :]
        bytes_of(g_recv.at[t], g_r.at[t])
        for i in range(7):
            g = g + g_recv[t, i].astype(jnp.float32)
        w_new = w_own[...] - 0.25 * g
        w_own[...] = w_new
        w_half = w_new.astype(jnp.bfloat16)
        w_send[t + 1] = w_half
        w_t[t + 1, my_rows, :] = w_half
        for u, dy in clip_offsets:
            put(w_send.at[t + 1], w_t.at[t + 1, my_rows, :], w_s.at[t + 1], w_r.at[t + 1], (clip_of(u, dy), feat), False)
    store_trained = pltpu.make_async_copy(w_own, tr_hbm, out_s.at[0])
    store_trained.start()

    t = STEPS
    bytes_of(g_recv.at[0], w_r.at[t])
    logits[...] = dot(w_t[t], phi[...]).astype(jnp.bfloat16)

    def chip_blocks(core):
        out = dot(picks[core, 0], logits[:, 0:quarter])
        for q in range(1, 4):
            out = out + dot(picks[core, q], logits[:, q * quarter:(q + 1) * quarter])
        return out

    out = chip_blocks(1 - c).astype(jnp.bfloat16)
    l_send[t, :, 0:quarter] = out[0:128, :]
    l_send[t, :, quarter:half] = out[128:256, :]
    put(l_send.at[t], c_recv.at[t], c_s.at[t], c_r.at[t], partner)
    out = chip_blocks(c)
    bytes_of(c_recv.at[t], c_r.at[t])
    for h in range(2):
        lanes = slice(h * quarter, (h + 1) * quarter)
        total = out[128 * h:128 * h + 128, :] + c_recv[t, :, lanes].astype(jnp.float32)
        part[:, lanes] = total
        c_send[t, :, lanes] = total.astype(jnp.bfloat16)

    def block_of(z_, xl_):
        i = 2 * z_ + xl_
        return pl.ds(pl.multiple_of(lax.rem(i, 8) * 16, 16), 16), pl.ds(pl.multiple_of(i // 8 * quarter, quarter), quarter)

    acc = exchange(t, lambda pz, px: c_send.at[(t, *block_of(pz, px))], lambda: part[block_of(z, xl)])
    for q in range(4):
        sc_ref[:, q * quarter:(q + 1) * quarter] = acc[4 * q:4 * q + 4, :]
    store_scores = pltpu.make_async_copy(sc_ref, sc_hbm, out_s.at[1])
    store_scores.start()
    store_trained.wait()
    store_scores.wait()

    for copy in sends:
        copy.wait_send()
    for t in range(STEPS + 1):
        bytes_of(g_recv.at[0], w_s.at[t])
        bytes_of(l_recv.at[0], l_s.at[t])
    for t in range(STEPS):
        bytes_of(l_recv.at[0], r_s.at[t])
        bytes_of(g_recv.at[0], g_s.at[t])


def per_device(embeds, frequencies, phases, weights, labels):
    nn, ke = embeds.shape
    kc, nf = frequencies.shape
    kw = weights.shape[1]
    kk = labels.shape[1]
    kt = kc * lax.axis_size("clip")
    total_features = nf * lax.axis_size("feat")
    scale = math.sqrt(2.0 / total_features)
    f32, b16 = jnp.float32, jnp.bfloat16
    dma = pltpu.SemaphoreType.DMA
    hbm = pl.BlockSpec(memory_space=pl.ANY)
    half, quarter = nn // 2, nn // 4
    steps = STEPS + 1
    scratch = [
        pltpu.VMEM((ke, nn), f32),
        pltpu.VMEM((kc, nf), f32),
        pltpu.VMEM((nf // 128, 128), f32),
        pltpu.VMEM((kw, nf), f32),
        pltpu.VMEM((nn, kk), jnp.int32),
        pltpu.VMEM((4, nn), f32),
        pltpu.VMEM((2, 4, 256, 128), b16),
        pltpu.VMEM((kt, nn), f32),
        pltpu.VMEM((kt, nf), f32),
        pltpu.VMEM((3, ke, half), f32),
        pltpu.VMEM((2 * ke, half), f32),
        pltpu.VMEM((kc, nf), f32),
        pltpu.VMEM((8, 3 * kc, nn), b16),
        pltpu.VMEM((8, nf, 3 * kc), b16),
        pltpu.VMEM((nf, nn), f32),
        pltpu.VMEM((nf, nn), b16),
        pltpu.VMEM((kk, quarter), f32),
        pltpu.VMEM((kw, nf), f32),
        pltpu.VMEM((steps, kw, nf), b16),
        pltpu.VMEM((steps, kk, nf), b16),
        pltpu.VMEM((kk, half), f32),
        pltpu.VMEM((steps, kk, half), b16),
        pltpu.VMEM((steps, kk, half), b16),
        pltpu.VMEM((steps, kk, half), b16),
        pltpu.VMEM((steps, 2 * NZ - 1, 16, quarter), b16),
        pltpu.VMEM((STEPS, kk, nn), b16),
        pltpu.VMEM((kk, nf), f32),
        pltpu.VMEM((STEPS, kk, nf), b16),
        pltpu.VMEM((STEPS, 7, kw, nf), b16),
        pltpu.VMEM((kk, nn), b16),
        dma((3,)), dma((3,)), dma((2, 2, 4)), dma((2, 2, 4)), dma((2, NZ)), dma((NZ,)),
        dma((4,)), dma((4,)), dma((2, 2, 4)), dma((2, 2, 4)),
        dma((steps,)), dma((steps,)), dma((steps,)), dma((steps,)), dma((steps,)), dma((steps,)),
        dma((STEPS,)), dma((STEPS,)), dma((STEPS,)), dma((STEPS,)), dma((STEPS,)), dma((STEPS,)),
        dma((5,)), dma((2,)), pltpu.SemaphoreType.REGULAR((3,)),
    ]
    trained_t, scores_t = pl.pallas_call(
        functools.partial(kernel, scale),
        out_shape=(jax.ShapeDtypeStruct((kw, nf), f32), jax.ShapeDtypeStruct((4, nn), f32)),
        in_specs=[hbm] * 5,
        out_specs=(hbm, hbm),
        scratch_shapes=scratch,
        compiler_params=pltpu.CompilerParams(
            collective_id=0, has_side_effects=True, vmem_limit_bytes=60 * 1024 * 1024),
    )(embeds.T, frequencies, phases.reshape(nf // 128, 128), weights.T, labels)
    return trained_t.T, scores_t.T


def solution(mesh):
    placed = (P("clip", "feat"), P("clip", "feat"), P("feat"), P("feat", "clip"), P("clip", None))
    return jax.shard_map(
        per_device,
        mesh=mesh,
        in_specs=placed,
        out_specs=(P("feat", "clip"), P("clip", "feat")),
        check_vma=False,
    )
```

```python
import functools
import math

import jax
import jax.numpy as jnp
from jax import lax
from jax.experimental import pallas as pl
from jax.experimental.pallas import tpu as pltpu
from jax.sharding import PartitionSpec as P

STEPS = 2
MESH = pl.DeviceIdType.MESH

NY = 4
NZ = 8

PI_A = 3.1416015625
PI_B = -8.90890987648163e-06
SIN = (9.99999976e-01, -1.66666473e-01, 8.33289467e-03, -1.98005800e-04, 2.58984559e-06)


def scaled_cos_of_twice(h, scale):
    q = jnp.round(h * (1.0 / math.pi))
    w = (h - q * PI_A) - q * PI_B
    w2 = w * w
    root = math.sqrt(2.0 * scale)
    p = root * SIN[4]
    for c in SIN[3::-1]:
        p = p * w2 + root * c
    s = w * p
    return scale - s * s


def bytes_of(ref, sem):
    pltpu.make_async_copy(ref, ref, sem).wait()


def kernel(
    scale,
    e_hbm, f_hbm, ph_hbm, w_hbm, lab_hbm,
    tr_ref, sc_ref,
    e_ref, f_ref, ph_ref, w_ref, lab_ref, picks,
    e_all, f_all, e_raw, e_two, f_rel,
    e3, f3, ang, phi, lab_t,
    w_own, w_send, w_t,
    part, c_send, c_recv, l_send, l_recv, r_t,
    grad, g_send, g_recv, logits,
    eq_s, eq_r, er_s, er_r, ep_s, ep_r,
    fx_s, fx_r, fy_s, fy_r,
    w_s, w_r, c_s, c_r, l_s, l_r, r_s, r_r, rc_s, rc_r, g_s, g_r,
    in_s, hello,
):
    loads = [
        pltpu.make_async_copy(src, dst, in_s.at[i])
        for i, (src, dst) in enumerate(
            ((e_hbm, e_ref), (f_hbm, f_ref), (w_hbm, w_ref), (ph_hbm, ph_ref), (lab_hbm, lab_ref)))
    ]
    for load in loads:
        load.start()

    clip = lax.axis_index("clip")
    feat = lax.axis_index("feat")
    c = lax.rem(feat, 2)
    xl = lax.rem(feat // 2, 2)
    z = feat // 4
    y = lax.rem(clip, NY)
    xh = clip // NY

    ke = e_ref.shape[0]
    kc = 4 * ke
    nf = f_ref.shape[1]
    nn = e_ref.shape[1]
    half = nn // 2
    quarter = nn // 4
    kw = w_ref.shape[0]

    def feat_of(z_, xl_, c_):
        return (z_ * 2 + xl_) * 2 + c_

    def clip_of(u, dy):
        return ((1 - xh) if u else xh) * NY + lax.rem(y + dy, NY)

    partner = (clip, feat_of(z, xl, 1 - c))
    x_near = (clip, feat_of(z, 1 - xl, c))
    diag = (clip, feat_of(z, 1 - xl, 1 - c))
    x_cross = (clip_of(1, 0), feat_of(z, 1 - xl, c))
    y_right = (clip_of(0, 1), feat)
    y_left = (clip_of(0, NY - 1), feat)
    z_up = (clip, feat_of(lax.rem(z + 1, NZ), xl, c))
    z_down = (clip, feat_of(lax.rem(z + NZ - 1, NZ), xl, c))

    def feat_peer(dz, dx):
        return lax.rem(z + dz, NZ), (1 - xl if dx else xl)

    feat_offsets = [(dz, dx) for dz in (4, 3, 5, 2, 6, 1, 7, 0) for dx in (1, 0) if (dz, dx) != (0, 0)]
    clip_offsets = [(u, dy) for dy in (2, 1, 3, 0) for u in (1, 0) if (u, dy) != (0, 0)]

    def slot_of(u, dy):
        return u * NY + dy - 1

    barrier = pltpu.get_barrier_semaphore()
    neighbours = [partner, x_near, x_cross, diag, z_up, z_down, y_right, y_left]
    for peer in neighbours:
        pl.semaphore_signal(barrier, inc=1, device_id=peer, device_id_type=MESH)

    my_rows = pl.ds(pl.multiple_of(clip * kw, kw), kw)
    for load in loads[0:3]:
        load.wait()
    w_own[...] = w_ref[...]
    w_send[0] = w_ref[...].astype(jnp.bfloat16)
    w_t[0, my_rows, :] = w_ref[...].astype(jnp.bfloat16)

    pl.semaphore_wait(barrier, len(neighbours))

    def greet(n):
        for peer in (x_near, x_cross, y_right, y_left):
            pl.semaphore_signal(hello.at[n], inc=1, device_id=peer, device_id_type=MESH)

    def greeted(n):
        pl.semaphore_wait(hello.at[n], 4)

    greet(0)
    sends = []

    def put(src, dst, s_sem, r_sem, to, own_sem=True):
        copy = pltpu.make_async_remote_copy(
            src_ref=src, dst_ref=dst, send_sem=s_sem, recv_sem=r_sem, device_id=to, device_id_type=MESH)
        copy.start()
        if own_sem:
            sends.append(copy)

    lanes_c = pl.ds(pl.multiple_of(c * half, half), half)
    lanes_o = pl.ds(pl.multiple_of((1 - c) * half, half), half)

    def e_rows(z_, xl_):
        return pl.ds(pl.multiple_of(z_ * kc + xl_ * (2 * ke), 8), 2 * ke)

    def e_piece(z_, xl_):
        return e_all.at[e_rows(z_, xl_), lanes_c]

    def f_block(clip_, lo, hi):
        return f_all.at[pl.ds(pl.multiple_of(clip_ * kc + lo, 8), hi - lo), :]

    def send_w(u, dy):
        put(w_send.at[0], w_t.at[0, my_rows, :], w_s.at[0], w_r.at[0], (clip_of(u, dy), feat), False)

    put(e_ref.at[:, lanes_o], e_raw.at[0], eq_s.at[0], eq_r.at[0], partner)
    put(e_ref.at[:, lanes_c], e_raw.at[1], eq_s.at[1], eq_r.at[1], x_near)
    put(e_ref.at[:, lanes_o], e_raw.at[2], eq_s.at[2], eq_r.at[2], diag)

    cut = kc // 3
    mid = kc // 2
    put(f_ref.at[cut:kc, :], f_rel.at[cut:kc, :], fx_s.at[1], fx_r.at[1], x_cross)
    put(f_ref.at[0:cut, :], f_rel.at[0:cut, :], fx_s.at[0], fx_r.at[0], x_near)
    lows = (0, mid)

    def f_send(direction, u, k, clip_, lo, hi, src=None):
        dst = f_block(clip_, lo, hi)
        put(dst if src is None else src, dst, fy_s.at[direction, u, k], fy_r.at[direction, u, k],
            y_right if direction == 0 else y_left)

    for k in (0, 1):
        for direction in (0, 1):
            lo = lows[k ^ direction]
            f_send(direction, 0, k, clip, lo, lo + mid, f_ref.at[lo:lo + mid, :])
    def join(own, oth):
        first = c == 0
        e_two[0:ke, :] = jnp.where(first, own, oth)
        e_two[ke:2 * ke, :] = jnp.where(first, oth, own)
        return e_two[...]

    def e_start(o, xl_):
        piece = e_piece(z, xl_)
        put(piece, piece, er_s.at[0, o, 0], er_r.at[0, o, 0], z_up)
        put(piece, piece, er_s.at[1, o, 0], er_r.at[1, o, 0], z_down)
        put(piece, piece, ep_s.at[o, 0], ep_r.at[0], partner)

    bytes_of(e_raw.at[0], eq_r.at[0])
    e_all[e_rows(z, xl), lanes_c] = join(e_ref[:, lanes_c], e_raw[0])
    e_start(0, xl)

    greeted(0)
    greet(1)
    for load in loads[3:]:
        load.wait()
    f_all[pl.ds(pl.multiple_of(clip * kc, 8), kc), :] = f_ref[...]
    row = lax.broadcasted_iota(jnp.int32, (2 * 128, 128), 0)
    col = lax.broadcasted_iota(jnp.int32, (2 * 128, 128), 1)
    for core in range(2):
        there = col == 8 * (row // 16) + 4 * core + row % 4
        for q in range(4):
            pick = there & (row // 4 % 4 == q)
            picks[core, q] = jnp.where(pick, 1.0, 0.0).astype(jnp.bfloat16)
    qn = pl.multiple_of((2 * c + xl) * quarter, quarter)
    lab_t[...] = lab_ref[pl.ds(qn, quarter), :].astype(jnp.float32).T
    for b in range(nf // 128):
        column = jnp.broadcast_to(0.5 * ph_ref[b:b + 1, :], (128, 128)).T
        for n in range(nn // 128):
            ang[128 * b:128 * b + 128, 128 * n:128 * n + 128] = column

    bytes_of(e_raw.at[1], eq_r.at[1])
    bytes_of(e_raw.at[2], eq_r.at[2])
    e_all[e_rows(z, 1 - xl), lanes_c] = join(e_raw[1], e_raw[2])
    e_start(1, 1 - xl)

    def e_step(direction, o, s):
        dz = (NZ - s) if direction == 0 else s
        z_ = lax.rem(z + dz, NZ)
        xl_ = (1 - xl) if o else xl
        piece = e_piece(z_, xl_)
        bytes_of(piece, er_r.at[direction, o, s - 1])
        if s < 3 or (s == 3 and o == direction):
            put(piece, piece, er_s.at[direction, o, s], er_r.at[direction, o, s], z_up if direction == 0 else z_down)
        put(piece, piece, ep_s.at[o, dz], ep_r.at[dz], partner)

    def e_prep(dz, lanes):
        z_ = lax.rem(z + dz, NZ)
        x = 0.5 * e_all[pl.ds(pl.multiple_of(z_ * kc, 16), kc), lanes]
        hi = x.astype(jnp.bfloat16)
        e3[z_, 0:kc, lanes] = hi
        e3[z_, kc:2 * kc, lanes] = (x - hi.astype(jnp.float32)).astype(jnp.bfloat16)
        e3[z_, 2 * kc:3 * kc, lanes] = hi

    def e_other(dz):
        z_ = lax.rem(z + dz, NZ)
        bytes_of(e_all.at[pl.ds(pl.multiple_of(z_ * kc, 16), kc), lanes_o], ep_r.at[dz])
        e_prep(dz, lanes_o)

    def f_prep(u, dy):
        j = clip_of(u, dy)
        x = f_all[pl.ds(pl.multiple_of(j * kc, 16), kc), :]
        hi = x.astype(jnp.bfloat16)
        lo = (x - hi.astype(jnp.float32)).astype(jnp.bfloat16)
        f3[j] = jnp.concatenate([hi, hi, lo], axis=0).T

    def f_wait(direction, u, k, clip_, lo, hi):
        bytes_of(f_block(clip_, lo, hi), fy_r.at[direction, u, k])

    dot = functools.partial(jnp.dot, preferred_element_type=jnp.float32)

    def stage_of(j):
        up = lax.rem(j - z + NZ, NZ)
        e_turn = jnp.minimum(up, NZ - up)
        e_turn = e_turn + e_turn // 4
        right = lax.rem(lax.rem(j, NY) - y + NY, NY)
        away = jnp.minimum(right, NY - right)
        f_turn = jnp.where(j // NY == xh, away, 2 + away)
        return jnp.maximum(e_turn, f_turn)

    def products(stage, first, count):
        @pl.loop(0, count)
        def _(i):
            j = lax.rem(xh * NY + first + i, 2 * NY)

            @pl.when(stage_of(j) == stage)
            def _():
                ang[...] = ang[...] + dot(f3[j], e3[j])

    e_step(0, 0, 1)
    e_step(1, 0, 1)
    greeted(1)
    greet(2)
    f_wait(0, 0, 0, clip_of(0, 3), 0, mid)
    f_send(0, 0, 2, clip_of(0, 3), 0, mid)
    f_wait(1, 0, 0, clip_of(0, 1), mid, kc)
    f_send(1, 0, 2, clip_of(0, 1), mid, kc)
    bytes_of(f_rel.at[cut:kc, :], fx_r.at[1])
    put(f_rel.at[cut:kc, :], f_block(clip_of(1, 0), cut, kc), fx_s.at[3], fx_r.at[3], x_near)
    bytes_of(f_rel.at[0:cut, :], fx_r.at[0])
    put(f_rel.at[0:cut, :], f_block(clip, 0, cut), fx_s.at[2], fx_r.at[2], x_cross)
    greeted(2)
    for u, dy in clip_offsets:
        send_w(u, dy)
    e_prep(0, lanes_c)
    f_prep(0, 0)
    e_other(0)
    products(0, 0, 8)
    e_step(0, 1, 1)
    e_step(1, 1, 1)
    e_prep(1, lanes_c)
    e_prep(7, lanes_c)
    f_wait(0, 0, 1, clip_of(0, 3), mid, kc)
    f_wait(1, 0, 1, clip_of(0, 1), 0, mid)
    f_prep(0, 1)
    f_prep(0, 3)
    over = clip_of(1, 0)
    bytes_of(f_block(over, 0, cut), fx_r.at[2])
    f_send(0, 1, 0, over, 0, cut)
    f_send(1, 1, 0, over, 0, cut)
    e_step(0, 0, 2)
    e_step(1, 0, 2)
    e_other(1)
    e_other(7)
    bytes_of(f_block(over, cut, kc), fx_r.at[3])
    f_send(0, 1, 1, over, cut, mid)
    f_send(1, 1, 1, over, mid, kc)
    f_send(0, 1, 2, over, mid, kc)
    f_send(1, 1, 2, over, cut, mid)
    products(1, 0, 4)
    e_step(0, 1, 2)
    e_step(1, 1, 2)
    products(1, 4, 4)
    e_prep(2, lanes_c)
    e_prep(6, lanes_c)
    f_wait(0, 0, 2, clip_of(0, 2), 0, mid)
    f_wait(1, 0, 2, clip_of(0, 2), mid, kc)
    f_prep(0, 2)
    f_prep(1, 0)
    e_other(2)
    e_other(6)
    e_step(0, 0, 3)
    e_step(1, 0, 3)
    products(2, 0, 2)
    f_wait(0, 1, 0, clip_of(1, 3), 0, cut)
    f_wait(0, 1, 1, clip_of(1, 3), cut, mid)
    f_send(0, 1, 3, clip_of(1, 3), 0, mid)
    f_wait(1, 1, 0, clip_of(1, 1), 0, cut)
    f_wait(1, 1, 1, clip_of(1, 1), mid, kc)
    f_send(1, 1, 3, clip_of(1, 1), mid, kc)
    products(2, 2, 2)
    e_step(0, 1, 3)
    e_step(1, 1, 3)
    products(2, 4, 4)
    e_prep(3, lanes_c)
    e_prep(5, lanes_c)
    f_wait(0, 1, 2, clip_of(1, 3), mid, kc)
    f_wait(1, 1, 2, clip_of(1, 1), cut, mid)
    f_prep(1, 1)
    f_prep(1, 3)
    e_step(0, 0, 4)
    e_other(3)
    e_other(5)
    products(3, 0, 4)
    products(3, 4, 4)
    e_step(1, 1, 4)
    e_prep(4, lanes_c)
    last_f = clip_of(1, 2)
    last = lax.rem(z + 4, NZ)
    f_wait(0, 1, 3, last_f, 0, mid)
    f_wait(1, 1, 3, last_f, mid, kc)
    f_prep(1, 2)

    @pl.when(last_f != last)
    def _():
        ang[...] = ang[...] + dot(f3[last_f], e3[last_f])

    e_other(4)

    for n in range(nn // 256):
        cols = slice(256 * n, 256 * n + 256)
        x = ang[:, cols] + dot(f3[last], e3[last, :, cols])
        phi[:, cols] = scaled_cos_of_twice(x, scale).astype(jnp.bfloat16)

    my_block = pl.ds(pl.multiple_of(z * 16, 16), 16)
    my_lanes = pl.ds(pl.multiple_of(xl * quarter, quarter), quarter)

    def exchange(t, source, own):
        for dz, dx in feat_offsets:
            pz, px = feat_peer(dz, dx)
            put(source(pz, px), l_recv.at[t, dx * NZ + dz - 1], l_s.at[t], l_r.at[t], (clip, feat_of(pz, px, c)), False)
        acc = own()
        bytes_of(l_recv.at[t], l_r.at[t])
        for i in range(2 * NZ - 1):
            acc = acc + l_recv[t, i].astype(jnp.float32)
        return acc

    def summed_logits(t):
        w = w_t[t]
        c_send[t] = dot(w, phi[:, lanes_o]).astype(jnp.bfloat16)
        put(c_send.at[t], c_recv.at[t], c_s.at[t], c_r.at[t], partner)
        part[...] = dot(w, phi[:, lanes_c])
        bytes_of(c_recv.at[t], c_r.at[t])
        total = part[...] + c_recv[t].astype(jnp.float32)
        part[...] = total
        l_send[t] = total.astype(jnp.bfloat16)

        def source(pz, px):
            return l_send.at[t, pl.ds(pl.multiple_of(pz * 16, 16), 16), pl.ds(pl.multiple_of(px * quarter, quarter), quarter)]

        return exchange(t, source, lambda: part[my_block, my_lanes])

    nt = (((1,), (1,)), ((), ()))
    full_lanes = pl.ds(pl.multiple_of(c * half + xl * quarter, quarter), quarter)

    for t in range(STEPS):
        bytes_of(g_recv.at[0], w_r.at[t])
        acc = summed_logits(t)
        residual = (jax.nn.sigmoid(acc) - lab_t[my_block, :]).astype(jnp.bfloat16)
        r_t[t, my_block, full_lanes] = residual
        mine_r = r_t.at[t, my_block, full_lanes]
        for dz, dx in feat_offsets:
            pz, px = feat_peer(dz, dx)
            put(mine_r, mine_r, r_s.at[t], r_r.at[t], (clip, feat_of(pz, px, c)), False)
        bytes_of(l_recv.at[t], r_r.at[t])
        half_r = r_t.at[t, :, lanes_c]
        put(half_r, half_r, rc_s.at[t], rc_r.at[t], partner)
        grad[...] = lax.dot_general(r_t[t, :, lanes_c], phi[:, lanes_c], nt, preferred_element_type=jnp.float32)
        bytes_of(r_t.at[t, :, lanes_o], rc_r.at[t])
        total = grad[...] + lax.dot_general(r_t[t, :, lanes_o], phi[:, lanes_o], nt, preferred_element_type=jnp.float32)
        grad[...] = total
        g_send[t] = total.astype(jnp.bfloat16)
        for u, dy in clip_offsets:
            j = clip_of(u, dy)
            put(g_send.at[t, pl.ds(pl.multiple_of(j * kw, kw), kw), :], g_recv.at[t, slot_of(u, dy)], g_s.at[t], g_r.at[t], (j, feat), False)
        g = grad[my_rows, :]
        bytes_of(g_recv.at[t], g_r.at[t])
        for i in range(7):
            g = g + g_recv[t, i].astype(jnp.float32)
        w_new = w_own[...] - 0.25 * g
        w_own[...] = w_new
        w_half = w_new.astype(jnp.bfloat16)
        w_send[t + 1] = w_half
        w_t[t + 1, my_rows, :] = w_half
        for u, dy in clip_offsets:
            put(w_send.at[t + 1], w_t.at[t + 1, my_rows, :], w_s.at[t + 1], w_r.at[t + 1], (clip_of(u, dy), feat), False)
    tr_ref[...] = w_own[...]

    t = STEPS
    bytes_of(g_recv.at[0], w_r.at[t])
    logits[...] = dot(w_t[t], phi[...]).astype(jnp.bfloat16)

    def chip_blocks(core):
        out = dot(picks[core, 0], logits[:, 0:quarter])
        for q in range(1, 4):
            out = out + dot(picks[core, q], logits[:, q * quarter:(q + 1) * quarter])
        return out

    out = chip_blocks(1 - c).astype(jnp.bfloat16)
    l_send[t, :, 0:quarter] = out[0:128, :]
    l_send[t, :, quarter:half] = out[128:256, :]
    put(l_send.at[t], c_recv.at[t], c_s.at[t], c_r.at[t], partner)
    out = chip_blocks(c)
    bytes_of(c_recv.at[t], c_r.at[t])
    for h in range(2):
        lanes = slice(h * quarter, (h + 1) * quarter)
        total = out[128 * h:128 * h + 128, :] + c_recv[t, :, lanes].astype(jnp.float32)
        part[:, lanes] = total
        c_send[t, :, lanes] = total.astype(jnp.bfloat16)

    def block_of(z_, xl_):
        i = 2 * z_ + xl_
        return pl.ds(pl.multiple_of(lax.rem(i, 8) * 16, 16), 16), pl.ds(pl.multiple_of(i // 8 * quarter, quarter), quarter)

    acc = exchange(t, lambda pz, px: c_send.at[(t, *block_of(pz, px))], lambda: part[block_of(z, xl)])
    for q in range(4):
        sc_ref[:, q * quarter:(q + 1) * quarter] = acc[4 * q:4 * q + 4, :]

    for copy in sends:
        copy.wait_send()
    for t in range(STEPS + 1):
        bytes_of(g_recv.at[0], w_s.at[t])
        bytes_of(l_recv.at[0], l_s.at[t])
    for t in range(STEPS):
        bytes_of(l_recv.at[0], r_s.at[t])
        bytes_of(g_recv.at[0], g_s.at[t])


def per_device(embeds, frequencies, phases, weights, labels):
    nn, ke = embeds.shape
    kc, nf = frequencies.shape
    kw = weights.shape[1]
    kk = labels.shape[1]
    kt = kc * lax.axis_size("clip")
    total_features = nf * lax.axis_size("feat")
    scale = math.sqrt(2.0 / total_features)
    f32, b16 = jnp.float32, jnp.bfloat16
    dma = pltpu.SemaphoreType.DMA
    hbm = pl.BlockSpec(memory_space=pl.ANY)
    vmem = pl.BlockSpec(memory_space=pltpu.VMEM)
    half, quarter = nn // 2, nn // 4
    steps = STEPS + 1
    scratch = [
        pltpu.VMEM((ke, nn), f32),
        pltpu.VMEM((kc, nf), f32),
        pltpu.VMEM((nf // 128, 128), f32),
        pltpu.VMEM((kw, nf), f32),
        pltpu.VMEM((nn, kk), jnp.int32),
        pltpu.VMEM((2, 4, 256, 128), b16),
        pltpu.VMEM((kt, nn), f32),
        pltpu.VMEM((kt, nf), f32),
        pltpu.VMEM((3, ke, half), f32),
        pltpu.VMEM((2 * ke, half), f32),
        pltpu.VMEM((kc, nf), f32),
        pltpu.VMEM((8, 3 * kc, nn), b16),
        pltpu.VMEM((8, nf, 3 * kc), b16),
        pltpu.VMEM((nf, nn), f32),
        pltpu.VMEM((nf, nn), b16),
        pltpu.VMEM((kk, quarter), f32),
        pltpu.VMEM((kw, nf), f32),
        pltpu.VMEM((steps, kw, nf), b16),
        pltpu.VMEM((steps, kk, nf), b16),
        pltpu.VMEM((kk, half), f32),
        pltpu.VMEM((steps, kk, half), b16),
        pltpu.VMEM((steps, kk, half), b16),
        pltpu.VMEM((steps, kk, half), b16),
        pltpu.VMEM((steps, 2 * NZ - 1, 16, quarter), b16),
        pltpu.VMEM((STEPS, kk, nn), b16),
        pltpu.VMEM((kk, nf), f32),
        pltpu.VMEM((STEPS, kk, nf), b16),
        pltpu.VMEM((STEPS, 7, kw, nf), b16),
        pltpu.VMEM((kk, nn), b16),
        dma((3,)), dma((3,)), dma((2, 2, 4)), dma((2, 2, 4)), dma((2, NZ)), dma((NZ,)),
        dma((4,)), dma((4,)), dma((2, 2, 4)), dma((2, 2, 4)),
        dma((steps,)), dma((steps,)), dma((steps,)), dma((steps,)), dma((steps,)), dma((steps,)),
        dma((STEPS,)), dma((STEPS,)), dma((STEPS,)), dma((STEPS,)), dma((STEPS,)), dma((STEPS,)),
        dma((5,)), pltpu.SemaphoreType.REGULAR((3,)),
    ]
    trained_t, scores_t = pl.pallas_call(
        functools.partial(kernel, scale),
        out_shape=(pltpu.VMEM((kw, nf), f32), pltpu.VMEM((4, nn), f32)),
        in_specs=[hbm] * 5,
        out_specs=(vmem, vmem),
        scratch_shapes=scratch,
        compiler_params=pltpu.CompilerParams(
            collective_id=0, has_side_effects=True, vmem_limit_bytes=60 * 1024 * 1024),
    )(embeds.T, frequencies, phases.reshape(nf // 128, 128), weights.T, labels)
    return trained_t.T, scores_t.T


def solution(mesh):
    placed = (P("clip", "feat"), P("clip", "feat"), P("feat"), P("feat", "clip"), P("clip", None))
    return jax.shard_map(
        per_device,
        mesh=mesh,
        in_specs=placed,
        out_specs=(P("feat", "clip"), P("clip", "feat")),
        check_vma=False,
    )
```

```python
import functools
import math

import jax
import jax.numpy as jnp
from jax import lax
from jax.experimental import pallas as pl
from jax.experimental.pallas import tpu as pltpu
from jax.sharding import PartitionSpec as P

STEPS = 2
MESH = pl.DeviceIdType.MESH

NY = 4
NZ = 8

PI_A = 3.1416015625
PI_B = -8.90890987648163e-06
SIN = (9.99999976e-01, -1.66666473e-01, 8.33289467e-03, -1.98005800e-04, 2.58984559e-06)


def scaled_cos_of_twice(h, scale):
    q = jnp.round(h * (1.0 / math.pi))
    w = (h - q * PI_A) - q * PI_B
    w2 = w * w
    root = math.sqrt(2.0 * scale)
    p = root * SIN[4]
    for c in SIN[3::-1]:
        p = p * w2 + root * c
    s = w * p
    return scale - s * s


def bytes_of(ref, sem):
    pltpu.make_async_copy(ref, ref, sem).wait()


def kernel(
    scale,
    e_hbm, f_hbm, ph_hbm, w_hbm, lab_hbm,
    tr_ref, sc_ref,
    e_ref, f_ref, ph_ref, w_ref, lab_ref, picks,
    e_all, f_all, e_raw, e_two, f_rel,
    e3, f3, ang, phi, lab_t,
    w_own, w_send, w_t,
    part, c_send, c_recv, l_send, l_recv, r_t,
    grad, g_send, g_recv, logits, s_out, s_in, s_own, s_sum, s_recv,
    eq_s, eq_r, er_s, er_r, ep_s, ep_r,
    fx_s, fx_r, fy_s, fy_r,
    w_s, w_r, c_s, c_r, l_s, l_r, r_s, r_r, rc_s, rc_r, g_s, g_r,
    in_s, hello,
):
    loads = [
        pltpu.make_async_copy(src, dst, in_s.at[i])
        for i, (src, dst) in enumerate(
            ((e_hbm, e_ref), (f_hbm, f_ref), (w_hbm, w_ref), (ph_hbm, ph_ref), (lab_hbm, lab_ref)))
    ]
    for load in loads:
        load.start()

    clip = lax.axis_index("clip")
    feat = lax.axis_index("feat")
    c = lax.rem(feat, 2)
    xl = lax.rem(feat // 2, 2)
    z = feat // 4
    y = lax.rem(clip, NY)
    xh = clip // NY

    ke = e_ref.shape[0]
    kc = 4 * ke
    nf = f_ref.shape[1]
    nn = e_ref.shape[1]
    half = nn // 2
    quarter = nn // 4
    kw = w_ref.shape[0]

    def feat_of(z_, xl_, c_):
        return (z_ * 2 + xl_) * 2 + c_

    def clip_of(u, dy):
        return ((1 - xh) if u else xh) * NY + lax.rem(y + dy, NY)

    partner = (clip, feat_of(z, xl, 1 - c))
    x_near = (clip, feat_of(z, 1 - xl, c))
    diag = (clip, feat_of(z, 1 - xl, 1 - c))
    x_cross = (clip_of(1, 0), feat_of(z, 1 - xl, c))
    y_right = (clip_of(0, 1), feat)
    y_left = (clip_of(0, NY - 1), feat)
    z_up = (clip, feat_of(lax.rem(z + 1, NZ), xl, c))
    z_down = (clip, feat_of(lax.rem(z + NZ - 1, NZ), xl, c))

    def feat_peer(dz, dx):
        return lax.rem(z + dz, NZ), (1 - xl if dx else xl)

    feat_offsets = [(dz, dx) for dz in (4, 3, 5, 2, 6, 1, 7, 0) for dx in (1, 0) if (dz, dx) != (0, 0)]
    clip_offsets = [(u, dy) for dy in (2, 1, 3, 0) for u in (1, 0) if (u, dy) != (0, 0)]

    barrier = pltpu.get_barrier_semaphore()
    neighbours = [partner, x_near, x_cross, diag, z_up, z_down, y_right, y_left]
    for peer in neighbours:
        pl.semaphore_signal(barrier, inc=1, device_id=peer, device_id_type=MESH)

    my_rows = pl.ds(pl.multiple_of(clip * kw, kw), kw)
    for load in loads[0:3]:
        load.wait()
    w_own[...] = w_ref[...]
    w_send[0] = w_ref[...].astype(jnp.bfloat16)
    w_t[0, my_rows, :] = w_ref[...].astype(jnp.bfloat16)

    pl.semaphore_wait(barrier, len(neighbours))

    def greet(n):
        for peer in (x_near, x_cross, y_right, y_left):
            pl.semaphore_signal(hello.at[n], inc=1, device_id=peer, device_id_type=MESH)

    def greeted(n):
        pl.semaphore_wait(hello.at[n], 4)

    greet(0)
    sends = []

    def put(src, dst, s_sem, r_sem, to, own_sem=True):
        copy = pltpu.make_async_remote_copy(
            src_ref=src, dst_ref=dst, send_sem=s_sem, recv_sem=r_sem, device_id=to, device_id_type=MESH)
        copy.start()
        if own_sem:
            sends.append(copy)

    lanes_c = pl.ds(pl.multiple_of(c * half, half), half)
    lanes_o = pl.ds(pl.multiple_of((1 - c) * half, half), half)

    def e_rows(z_, xl_):
        return pl.ds(pl.multiple_of(z_ * kc + xl_ * (2 * ke), 8), 2 * ke)

    def e_piece(z_, xl_):
        return e_all.at[e_rows(z_, xl_), lanes_c]

    def f_block(clip_, lo, hi):
        return f_all.at[pl.ds(pl.multiple_of(clip_ * kc + lo, 8), hi - lo), :]

    def send_w(u, dy):
        put(w_send.at[0], w_t.at[0, my_rows, :], w_s.at[0], w_r.at[0, 0], (clip_of(u, dy), feat), False)

    put(e_ref.at[:, lanes_o], e_raw.at[0], eq_s.at[0], eq_r.at[0], partner)
    put(e_ref.at[:, lanes_c], e_raw.at[1], eq_s.at[1], eq_r.at[1], x_near)
    put(e_ref.at[:, lanes_o], e_raw.at[2], eq_s.at[2], eq_r.at[2], diag)

    cut = kc // 3
    mid = kc // 2
    put(f_ref.at[cut:kc, :], f_rel.at[cut:kc, :], fx_s.at[1], fx_r.at[1], x_cross)
    put(f_ref.at[0:cut, :], f_rel.at[0:cut, :], fx_s.at[0], fx_r.at[0], x_near)
    lows = (0, mid)

    def f_send(direction, u, k, clip_, lo, hi, src=None):
        dst = f_block(clip_, lo, hi)
        put(dst if src is None else src, dst, fy_s.at[direction, u, k], fy_r.at[direction, u, k],
            y_right if direction == 0 else y_left)

    for k in (0, 1):
        for direction in (0, 1):
            lo = lows[k ^ direction]
            f_send(direction, 0, k, clip, lo, lo + mid, f_ref.at[lo:lo + mid, :])
    def join(own, oth):
        first = c == 0
        e_two[0:ke, :] = jnp.where(first, own, oth)
        e_two[ke:2 * ke, :] = jnp.where(first, oth, own)
        return e_two[...]

    def e_start(o, xl_):
        piece = e_piece(z, xl_)
        put(piece, piece, er_s.at[0, o, 0], er_r.at[0, o, 0], z_up)
        put(piece, piece, er_s.at[1, o, 0], er_r.at[1, o, 0], z_down)
        put(piece, piece, ep_s.at[o, 0], ep_r.at[0], partner)

    bytes_of(e_raw.at[0], eq_r.at[0])
    e_all[e_rows(z, xl), lanes_c] = join(e_ref[:, lanes_c], e_raw[0])
    e_start(0, xl)

    greeted(0)
    greet(1)
    for load in loads[3:]:
        load.wait()
    f_all[pl.ds(pl.multiple_of(clip * kc, 8), kc), :] = f_ref[...]
    row = lax.broadcasted_iota(jnp.int32, (128, 64), 0)
    col = lax.broadcasted_iota(jnp.int32, (128, 64), 1)
    for core in range(2):
        there = col == 8 * (row // 16) + 4 * core + row % 4
        for q in range(4):
            pick = there & (row // 4 % 4 == q)
            picks[core, q] = jnp.where(pick, 1.0, 0.0).astype(jnp.bfloat16)
    first = pl.multiple_of(c * half + (xl * 2 + z // 4) * (nn // 8), nn // 8)
    lab = lab_ref[pl.ds(first, nn // 8), :].astype(jnp.float32).T
    lab_t[0] = lab[0:4 * kw, :]
    lab_t[1] = lab[4 * kw:8 * kw, :]
    for b in range(nf // 128):
        column = jnp.broadcast_to(0.5 * ph_ref[b:b + 1, :], (128, 128)).T
        for n in range(nn // 128):
            ang[128 * b:128 * b + 128, 128 * n:128 * n + 128] = column

    bytes_of(e_raw.at[1], eq_r.at[1])
    bytes_of(e_raw.at[2], eq_r.at[2])
    e_all[e_rows(z, 1 - xl), lanes_c] = join(e_raw[1], e_raw[2])
    e_start(1, 1 - xl)

    def e_step(direction, o, s):
        dz = (NZ - s) if direction == 0 else s
        z_ = lax.rem(z + dz, NZ)
        xl_ = (1 - xl) if o else xl
        piece = e_piece(z_, xl_)
        bytes_of(piece, er_r.at[direction, o, s - 1])
        if s < 3 or (s == 3 and o == direction):
            put(piece, piece, er_s.at[direction, o, s], er_r.at[direction, o, s], z_up if direction == 0 else z_down)
        put(piece, piece, ep_s.at[o, dz], ep_r.at[dz], partner)

    def e_prep(dz, lanes):
        z_ = lax.rem(z + dz, NZ)
        x = 0.5 * e_all[pl.ds(pl.multiple_of(z_ * kc, 16), kc), lanes]
        hi = x.astype(jnp.bfloat16)
        e3[z_, 0:kc, lanes] = hi
        e3[z_, kc:2 * kc, lanes] = (x - hi.astype(jnp.float32)).astype(jnp.bfloat16)
        e3[z_, 2 * kc:3 * kc, lanes] = hi

    def e_other(dz):
        z_ = lax.rem(z + dz, NZ)
        bytes_of(e_all.at[pl.ds(pl.multiple_of(z_ * kc, 16), kc), lanes_o], ep_r.at[dz])
        e_prep(dz, lanes_o)

    def f_prep(u, dy):
        j = clip_of(u, dy)
        x = f_all[pl.ds(pl.multiple_of(j * kc, 16), kc), :]
        hi = x.astype(jnp.bfloat16)
        lo = (x - hi.astype(jnp.float32)).astype(jnp.bfloat16)
        f3[j] = jnp.concatenate([hi, hi, lo], axis=0).T

    def f_wait(direction, u, k, clip_, lo, hi):
        bytes_of(f_block(clip_, lo, hi), fy_r.at[direction, u, k])

    dot = functools.partial(jnp.dot, preferred_element_type=jnp.float32)

    def stage_of(j):
        up = lax.rem(j - z + NZ, NZ)
        e_turn = jnp.minimum(up, NZ - up)
        e_turn = e_turn + e_turn // 4
        right = lax.rem(lax.rem(j, NY) - y + NY, NY)
        away = jnp.minimum(right, NY - right)
        f_turn = jnp.where(j // NY == xh, away, 2 + away)
        return jnp.maximum(e_turn, f_turn)

    def products(stage, first, count):
        @pl.loop(0, count)
        def _(i):
            j = lax.rem(xh * NY + first + i, 2 * NY)

            @pl.when(stage_of(j) == stage)
            def _():
                ang[...] = ang[...] + dot(f3[j], e3[j])

    e_step(0, 0, 1)
    e_step(1, 0, 1)
    greeted(1)
    greet(2)
    f_wait(0, 0, 0, clip_of(0, 3), 0, mid)
    f_send(0, 0, 2, clip_of(0, 3), 0, mid)
    f_wait(1, 0, 0, clip_of(0, 1), mid, kc)
    f_send(1, 0, 2, clip_of(0, 1), mid, kc)
    bytes_of(f_rel.at[cut:kc, :], fx_r.at[1])
    put(f_rel.at[cut:kc, :], f_block(clip_of(1, 0), cut, kc), fx_s.at[3], fx_r.at[3], x_near)
    bytes_of(f_rel.at[0:cut, :], fx_r.at[0])
    put(f_rel.at[0:cut, :], f_block(clip, 0, cut), fx_s.at[2], fx_r.at[2], x_cross)
    greeted(2)
    for u, dy in clip_offsets:
        send_w(u, dy)
    e_prep(0, lanes_c)
    f_prep(0, 0)
    e_other(0)
    products(0, 0, 8)
    e_step(0, 1, 1)
    e_step(1, 1, 1)
    e_prep(1, lanes_c)
    e_prep(7, lanes_c)
    f_wait(0, 0, 1, clip_of(0, 3), mid, kc)
    f_wait(1, 0, 1, clip_of(0, 1), 0, mid)
    f_prep(0, 1)
    f_prep(0, 3)
    over = clip_of(1, 0)
    bytes_of(f_block(over, 0, cut), fx_r.at[2])
    f_send(0, 1, 0, over, 0, cut)
    f_send(1, 1, 0, over, 0, cut)
    e_step(0, 0, 2)
    e_step(1, 0, 2)
    e_other(1)
    e_other(7)
    bytes_of(f_block(over, cut, kc), fx_r.at[3])
    f_send(0, 1, 1, over, cut, mid)
    f_send(1, 1, 1, over, mid, kc)
    f_send(0, 1, 2, over, mid, kc)
    f_send(1, 1, 2, over, cut, mid)
    products(1, 0, 4)
    e_step(0, 1, 2)
    e_step(1, 1, 2)
    products(1, 4, 4)
    e_prep(2, lanes_c)
    e_prep(6, lanes_c)
    f_wait(0, 0, 2, clip_of(0, 2), 0, mid)
    f_wait(1, 0, 2, clip_of(0, 2), mid, kc)
    f_prep(0, 2)
    f_prep(1, 0)
    e_other(2)
    e_other(6)
    e_step(0, 0, 3)
    e_step(1, 0, 3)
    products(2, 0, 2)
    f_wait(0, 1, 0, clip_of(1, 3), 0, cut)
    f_wait(0, 1, 1, clip_of(1, 3), cut, mid)
    f_send(0, 1, 3, clip_of(1, 3), 0, mid)
    f_wait(1, 1, 0, clip_of(1, 1), 0, cut)
    f_wait(1, 1, 1, clip_of(1, 1), mid, kc)
    f_send(1, 1, 3, clip_of(1, 1), mid, kc)
    products(2, 2, 2)
    e_step(0, 1, 3)
    e_step(1, 1, 3)
    products(2, 4, 4)
    e_prep(3, lanes_c)
    e_prep(5, lanes_c)
    f_wait(0, 1, 2, clip_of(1, 3), mid, kc)
    f_wait(1, 1, 2, clip_of(1, 1), cut, mid)
    f_prep(1, 1)
    f_prep(1, 3)
    e_step(0, 0, 4)
    e_other(3)
    e_other(5)
    products(3, 0, 4)
    products(3, 4, 4)
    e_step(1, 1, 4)
    e_prep(4, lanes_c)
    last_f = clip_of(1, 2)
    last = lax.rem(z + 4, NZ)
    f_wait(0, 1, 3, last_f, 0, mid)
    f_wait(1, 1, 3, last_f, mid, kc)
    f_prep(1, 2)

    @pl.when(last_f != last)
    def _():
        ang[...] = ang[...] + dot(f3[last_f], e3[last_f])

    e_other(4)

    for n in range(nn // 256):
        cols = slice(256 * n, 256 * n + 256)
        x = ang[:, cols] + dot(f3[last], e3[last, :, cols])
        phi[:, cols] = scaled_cos_of_twice(x, scale).astype(jnp.bfloat16)

    hk = w_t.shape[1] // 2
    block = nn // 8
    chains = range(2)

    def chain_rows(h):
        return slice(h * hk, (h + 1) * hk)

    def block_rows(z_):
        return pl.ds(pl.multiple_of(lax.rem(z_, 4) * 16, 16), 16)

    def block_lanes(z_, xl_, core=None):
        lane = (xl_ * 2 + z_ // 4) * block
        if core is not None:
            lane = lane + core * half
        return pl.ds(pl.multiple_of(lane, block), block)

    nt = functools.partial(
        lax.dot_general, dimension_numbers=(((1,), (1,)), ((), ())), preferred_element_type=jnp.float32)

    def wait_w(t, h):
        for own, count in ((True, 3), (False, 4)):
            @pl.when((xh == h) == own)
            def _():
                bytes_of(g_recv.at[0, 0:count], w_r.at[t, h])

    def start_logits(t, h):
        w = w_t[t, chain_rows(h), :]
        c_send[t, h] = dot(w, phi[:, lanes_o]).astype(jnp.bfloat16)
        put(c_send.at[t, h], c_recv.at[t, h], c_s.at[t, h], c_r.at[t, h], partner)
        part[h] = dot(w, phi[:, lanes_c])

    def share_logits(t, h):
        bytes_of(c_recv.at[t, h], c_r.at[t, h])
        total = part[h] + c_recv[t, h].astype(jnp.float32)
        part[h] = total
        l_send[t, h] = total.astype(jnp.bfloat16)
        for dz, dx in feat_offsets:
            pz, px = feat_peer(dz, dx)
            put(l_send.at[t, h, block_rows(pz), block_lanes(pz, px)], l_recv.at[t, h, dx * NZ + dz - 1],
                l_s.at[t, h], l_r.at[t, h], (clip, feat_of(pz, px, c)), False)

    bytes_of(g_recv.at[0], w_r.at[0, 0])
    for h in chains:
        start_logits(0, h)
    for t in range(STEPS):
        for h in chains:
            if t > 0:
                wait_w(t, h)
                start_logits(t, h)
            share_logits(t, h)
        for h in chains:
            acc = part[h, block_rows(z), block_lanes(z, xl)]
            bytes_of(l_recv.at[t, h], l_r.at[t, h])
            for i in range(2 * NZ - 1):
                acc = acc + l_recv[t, h, i].astype(jnp.float32)
            labels = lab_t[h, block_rows(z), :]
            r_t[t, h, block_rows(z), block_lanes(z, xl, c)] = (jax.nn.sigmoid(acc) - labels).astype(jnp.bfloat16)
            mine_r = r_t.at[t, h, block_rows(z), block_lanes(z, xl, c)]
            for dz, dx in feat_offsets:
                pz, px = feat_peer(dz, dx)
                put(mine_r, mine_r, r_s.at[t, h], r_r.at[t, h], (clip, feat_of(pz, px, c)), False)
        for h in chains:
            bytes_of(l_recv.at[t, h], r_r.at[t, h])
            half_r = r_t.at[t, h, :, lanes_c]
            put(half_r, half_r, rc_s.at[t, h], rc_r.at[t, h], partner)
            grad[h] = nt(r_t[t, h, :, lanes_c], phi[:, lanes_c])
            bytes_of(r_t.at[t, h, :, lanes_o], rc_r.at[t, h])
            total = grad[h] + nt(r_t[t, h, :, lanes_o], phi[:, lanes_o])
            grad[h] = total
            g_send[t, h] = total.astype(jnp.bfloat16)

            def send_g(dy, slot):
                yo = lax.rem(y + dy, NY)
                put(g_send.at[t, h, pl.ds(pl.multiple_of(yo * kw, kw), kw), :], g_recv.at[t, slot],
                    g_s.at[t, h], g_r.at[t], (h * NY + yo, feat), False)

            slot = jnp.where(xh == h, -1, 3)
            for dy in (2, 1, 3):
                send_g(dy, slot + dy)

            @pl.when(xh != h)
            def _():
                send_g(0, 3)
        for h in chains:
            @pl.when(xh == h)
            def _():
                g = grad[h, pl.ds(pl.multiple_of(y * kw, kw), kw), :]
                bytes_of(g_recv.at[t], g_r.at[t])
                for i in range(7):
                    g = g + g_recv[t, i].astype(jnp.float32)
                w_new = w_own[...] - 0.25 * g
                w_own[...] = w_new
                w_half = w_new.astype(jnp.bfloat16)
                w_send[t + 1] = w_half
                w_t[t + 1, my_rows, :] = w_half
                for u, dy in clip_offsets:
                    put(w_send.at[t + 1], w_t.at[t + 1, my_rows, :], w_s.at[t + 1], w_r.at[t + 1, h],
                        (clip_of(u, dy), feat), False)
    tr_ref[...] = w_own[...]

    t = STEPS

    def chip_blocks(h, core):
        out = dot(picks[core, 0], logits[h, :, 0:quarter])
        for q in range(1, 4):
            out = out + dot(picks[core, q], logits[h, :, q * quarter:(q + 1) * quarter])
        return out

    def chip_rows(z_, xl_):
        return pl.ds(pl.multiple_of((2 * lax.rem(z_, 4) + xl_) * 16, 16), 16)

    zh = z // 4
    for h in chains:
        wait_w(t, h)
        logits[h] = dot(w_t[t, chain_rows(h), :], phi[...]).astype(jnp.bfloat16)
        s_out[h] = chip_blocks(h, 1 - c).astype(jnp.bfloat16)
        put(s_out.at[h], s_in.at[h], c_s.at[t, h], c_r.at[t, h], partner)
        s_own[h] = chip_blocks(h, c)
        bytes_of(s_in.at[h], c_r.at[t, h])
        total = s_own[h] + s_in[h].astype(jnp.float32)
        s_own[h] = total
        s_sum[h] = total.astype(jnp.bfloat16)

        def send_s(dz, dx, slot):
            pz = h * 4 + lax.rem(z + dz, 4)
            px = 1 - xl if dx else xl
            put(s_sum.at[h, chip_rows(pz, px), :], s_recv.at[slot], l_s.at[t, h], l_r.at[t, 0], (clip, feat_of(pz, px, c)), False)

        slot = jnp.where(zh == h, -1, 7)
        for dz in (2, 1, 3, 0):
            for dx in (1, 0):
                if (dz, dx) != (0, 0):
                    send_s(dz, dx, slot + dx * 4 + dz)

        @pl.when(zh != h)
        def _():
            send_s(0, 0, 7)
    acc = s_own[zh, chip_rows(z, xl), :]
    bytes_of(s_recv, l_r.at[t, 0])
    for i in range(2 * NZ - 1):
        acc = acc + s_recv[i].astype(jnp.float32)
    for q in range(4):
        sc_ref[:, q * quarter:(q + 1) * quarter] = acc[4 * q:4 * q + 4, :]

    for copy in sends:
        copy.wait_send()
    for t in range(STEPS + 1):
        bytes_of(g_recv.at[0], w_s.at[t])
    for h in chains:
        for t in range(STEPS):
            bytes_of(l_recv.at[0, 0], l_s.at[t, h])
            bytes_of(l_recv.at[0, 0], r_s.at[t, h])
        for own, count in ((True, 3), (False, 4)):
            @pl.when((xh == h) == own)
            def _():
                for t in range(STEPS):
                    bytes_of(g_recv.at[0, 0:count], g_s.at[t, h])
        for own, count in ((True, 7), (False, 8)):
            @pl.when((zh == h) == own)
            def _():
                bytes_of(s_recv.at[0:count], l_s.at[STEPS, h])


def per_device(embeds, frequencies, phases, weights, labels):
    nn, ke = embeds.shape
    kc, nf = frequencies.shape
    kw = weights.shape[1]
    kk = labels.shape[1]
    kt = kc * lax.axis_size("clip")
    total_features = nf * lax.axis_size("feat")
    scale = math.sqrt(2.0 / total_features)
    f32, b16 = jnp.float32, jnp.bfloat16
    dma = pltpu.SemaphoreType.DMA
    hbm = pl.BlockSpec(memory_space=pl.ANY)
    vmem = pl.BlockSpec(memory_space=pltpu.VMEM)
    half, quarter = nn // 2, nn // 4
    steps = STEPS + 1
    scratch = [
        pltpu.VMEM((ke, nn), f32),
        pltpu.VMEM((kc, nf), f32),
        pltpu.VMEM((nf // 128, 128), f32),
        pltpu.VMEM((kw, nf), f32),
        pltpu.VMEM((nn, kk), jnp.int32),
        pltpu.VMEM((2, 4, 128, 64), b16),
        pltpu.VMEM((kt, nn), f32),
        pltpu.VMEM((kt, nf), f32),
        pltpu.VMEM((3, ke, half), f32),
        pltpu.VMEM((2 * ke, half), f32),
        pltpu.VMEM((kc, nf), f32),
        pltpu.VMEM((8, 3 * kc, nn), b16),
        pltpu.VMEM((8, nf, 3 * kc), b16),
        pltpu.VMEM((nf, nn), f32),
        pltpu.VMEM((nf, nn), b16),
        pltpu.VMEM((2, kk // 2, nn // 8), f32),
        pltpu.VMEM((kw, nf), f32),
        pltpu.VMEM((steps, kw, nf), b16),
        pltpu.VMEM((steps, kk, nf), b16),
        pltpu.VMEM((2, kk // 2, half), f32),
        pltpu.VMEM((STEPS, 2, kk // 2, half), b16),
        pltpu.VMEM((STEPS, 2, kk // 2, half), b16),
        pltpu.VMEM((STEPS, 2, kk // 2, half), b16),
        pltpu.VMEM((STEPS, 2, 2 * NZ - 1, 16, nn // 8), b16),
        pltpu.VMEM((STEPS, 2, kk // 2, nn), b16),
        pltpu.VMEM((2, kk // 2, nf), f32),
        pltpu.VMEM((STEPS, 2, kk // 2, nf), b16),
        pltpu.VMEM((STEPS, 7, kw, nf), b16),
        pltpu.VMEM((2, kk // 2, nn), b16),
        pltpu.VMEM((2, 128, quarter), b16),
        pltpu.VMEM((2, 128, quarter), b16),
        pltpu.VMEM((2, 128, quarter), f32),
        pltpu.VMEM((2, 128, quarter), b16),
        pltpu.VMEM((2 * NZ - 1, 16, quarter), b16),
        dma((3,)), dma((3,)), dma((2, 2, 4)), dma((2, 2, 4)), dma((2, NZ)), dma((NZ,)),
        dma((4,)), dma((4,)), dma((2, 2, 4)), dma((2, 2, 4)),
        dma((steps,)), dma((steps, 2)), dma((steps, 2)), dma((steps, 2)), dma((steps, 2)), dma((steps, 2)),
        dma((STEPS, 2)), dma((STEPS, 2)), dma((STEPS, 2)), dma((STEPS, 2)), dma((STEPS, 2)), dma((STEPS,)),
        dma((5,)), pltpu.SemaphoreType.REGULAR((3,)),
    ]
    trained_t, scores_t = pl.pallas_call(
        functools.partial(kernel, scale),
        out_shape=(pltpu.VMEM((kw, nf), f32), pltpu.VMEM((4, nn), f32)),
        in_specs=[hbm] * 5,
        out_specs=(vmem, vmem),
        scratch_shapes=scratch,
        compiler_params=pltpu.CompilerParams(
            collective_id=0, has_side_effects=True, vmem_limit_bytes=60 * 1024 * 1024),
    )(embeds.T, frequencies, phases.reshape(nf // 128, 128), weights.T, labels)
    return trained_t.T, scores_t.T


def solution(mesh):
    placed = (P("clip", "feat"), P("clip", "feat"), P("feat"), P("feat", "clip"), P("clip", None))
    return jax.shard_map(
        per_device,
        mesh=mesh,
        in_specs=placed,
        out_specs=(P("feat", "clip"), P("clip", "feat")),
        check_vma=False,
    )
```

```python
import functools
import math

import jax
import jax.numpy as jnp
from jax import lax
from jax.experimental import pallas as pl
from jax.experimental.pallas import tpu as pltpu
from jax.sharding import PartitionSpec as P

STEPS = 2
MESH = pl.DeviceIdType.MESH

NY = 4
NZ = 8

PI_A = 3.1416015625
PI_B = -8.90890987648163e-06
SIN = (9.99999976e-01, -1.66666473e-01, 8.33289467e-03, -1.98005800e-04, 2.58984559e-06)


def scaled_cos_of_twice(h, scale):
    q = jnp.round(h * (1.0 / math.pi))
    w = (h - q * PI_A) - q * PI_B
    w2 = w * w
    root = math.sqrt(2.0 * scale)
    p = root * SIN[4]
    for c in SIN[3::-1]:
        p = p * w2 + root * c
    s = w * p
    return scale - s * s


def bytes_of(ref, sem):
    pltpu.make_async_copy(ref, ref, sem).wait()


def kernel(
    scale,
    e_hbm, f_hbm, ph_hbm, w_hbm, lab_hbm,
    tr_ref, sc_ref,
    e_ref, f_ref, ph_ref, w_ref, lab_ref, picks,
    e_all, f_all, e_raw, e_two, f_rel,
    e3, f3, ang, phi, lab_t,
    w_own, w_send, w_t,
    part, c_send, c_recv, l_send, l_recv, r_t,
    grad, g_send, g_recv, logits, s_out, s_in, s_own, s_sum, s_recv,
    eq_s, eq_r, er_s, er_r, ep_s, ep_r,
    fx_s, fx_r, fy_s, fy_r,
    w_s, w_r, c_s, c_r, l_s, l_r, r_s, r_r, rc_s, rc_r, g_s, g_r,
    in_s, hello,
):
    loads = [
        pltpu.make_async_copy(src, dst, in_s.at[i])
        for i, (src, dst) in enumerate(
            ((e_hbm, e_ref), (f_hbm, f_ref), (w_hbm, w_ref), (ph_hbm, ph_ref), (lab_hbm, lab_ref)))
    ]
    for load in loads:
        load.start()

    clip = lax.axis_index("clip")
    feat = lax.axis_index("feat")
    c = lax.rem(feat, 2)
    xl = lax.rem(feat // 2, 2)
    z = feat // 4
    y = lax.rem(clip, NY)
    xh = clip // NY

    ke = e_ref.shape[0]
    kc = 4 * ke
    nf = f_ref.shape[1]
    nn = e_ref.shape[1]
    half = nn // 2
    quarter = nn // 4
    kw = w_ref.shape[0]

    def feat_of(z_, xl_, c_):
        return (z_ * 2 + xl_) * 2 + c_

    def clip_of(u, dy):
        return ((1 - xh) if u else xh) * NY + lax.rem(y + dy, NY)

    partner = (clip, feat_of(z, xl, 1 - c))
    x_near = (clip, feat_of(z, 1 - xl, c))
    diag = (clip, feat_of(z, 1 - xl, 1 - c))
    x_cross = (clip_of(1, 0), feat_of(z, 1 - xl, c))
    y_right = (clip_of(0, 1), feat)
    y_left = (clip_of(0, NY - 1), feat)
    z_up = (clip, feat_of(lax.rem(z + 1, NZ), xl, c))
    z_down = (clip, feat_of(lax.rem(z + NZ - 1, NZ), xl, c))

    def feat_peer(dz, dx):
        return lax.rem(z + dz, NZ), (1 - xl if dx else xl)

    feat_offsets = [(dz, dx) for dz in (4, 3, 5, 2, 6, 1, 7, 0) for dx in (1, 0) if (dz, dx) != (0, 0)]
    clip_offsets = [(u, dy) for dy in (2, 1, 3, 0) for u in (1, 0) if (u, dy) != (0, 0)]

    barrier = pltpu.get_barrier_semaphore()
    neighbours = [partner, x_near, x_cross, diag, z_up, z_down, y_right, y_left]
    for peer in neighbours:
        pl.semaphore_signal(barrier, inc=1, device_id=peer, device_id_type=MESH)

    my_rows = pl.ds(pl.multiple_of(clip * kw, kw), kw)
    for load in loads[0:3]:
        load.wait()
    w_own[...] = w_ref[...]
    w_send[0] = w_ref[...].astype(jnp.bfloat16)
    w_t[0, my_rows, :] = w_ref[...].astype(jnp.bfloat16)

    pl.semaphore_wait(barrier, len(neighbours))

    def greet(n):
        for peer in (x_near, x_cross, y_right, y_left):
            pl.semaphore_signal(hello.at[n], inc=1, device_id=peer, device_id_type=MESH)

    def greeted(n):
        pl.semaphore_wait(hello.at[n], 4)

    greet(0)
    sends = []

    def put(src, dst, s_sem, r_sem, to, own_sem=True):
        copy = pltpu.make_async_remote_copy(
            src_ref=src, dst_ref=dst, send_sem=s_sem, recv_sem=r_sem, device_id=to, device_id_type=MESH)
        copy.start()
        if own_sem:
            sends.append(copy)

    lanes_c = pl.ds(pl.multiple_of(c * half, half), half)
    lanes_o = pl.ds(pl.multiple_of((1 - c) * half, half), half)

    def e_rows(z_, xl_):
        return pl.ds(pl.multiple_of(z_ * kc + xl_ * (2 * ke), 8), 2 * ke)

    def e_piece(z_, xl_):
        return e_all.at[e_rows(z_, xl_), lanes_c]

    def e_far_piece(z_, xl_, direction):
        lane = pl.multiple_of(c * half + direction * quarter, quarter)
        return e_all.at[e_rows(z_, xl_), pl.ds(lane, quarter)]

    def f_block(clip_, lo, hi):
        return f_all.at[pl.ds(pl.multiple_of(clip_ * kc + lo, 8), hi - lo), :]

    def send_w(u, dy):
        put(w_send.at[0], w_t.at[0, my_rows, :], w_s.at[0], w_r.at[0, 0], (clip_of(u, dy), feat), False)

    put(e_ref.at[:, lanes_o], e_raw.at[0], eq_s.at[0], eq_r.at[0], partner)
    put(e_ref.at[:, lanes_c], e_raw.at[1], eq_s.at[1], eq_r.at[1], x_near)
    put(e_ref.at[:, lanes_o], e_raw.at[2], eq_s.at[2], eq_r.at[2], diag)

    cut = kc // 3
    mid = kc // 2
    put(f_ref.at[cut:kc, :], f_rel.at[cut:kc, :], fx_s.at[1], fx_r.at[1], x_cross)
    put(f_ref.at[0:cut, :], f_rel.at[0:cut, :], fx_s.at[0], fx_r.at[0], x_near)
    lows = (0, mid)

    def f_send(direction, u, k, clip_, lo, hi, src=None):
        dst = f_block(clip_, lo, hi)
        put(dst if src is None else src, dst, fy_s.at[direction, u, k], fy_r.at[direction, u, k],
            y_right if direction == 0 else y_left)

    for k in (0, 1):
        for direction in (0, 1):
            lo = lows[k ^ direction]
            f_send(direction, 0, k, clip, lo, lo + mid, f_ref.at[lo:lo + mid, :])
    def join(own, oth):
        first = c == 0
        e_two[0:ke, :] = jnp.where(first, own, oth)
        e_two[ke:2 * ke, :] = jnp.where(first, oth, own)
        return e_two[...]

    def e_start(o, xl_):
        piece = e_piece(z, xl_)
        put(piece, piece, er_s.at[0, o, 0], er_r.at[0, o, 0], z_up)
        put(piece, piece, er_s.at[1, o, 0], er_r.at[1, o, 0], z_down)
        put(piece, piece, ep_s.at[o, 0], ep_r.at[0], partner)

    bytes_of(e_raw.at[0], eq_r.at[0])
    e_all[e_rows(z, xl), lanes_c] = join(e_ref[:, lanes_c], e_raw[0])
    e_start(0, xl)

    greeted(0)
    greet(1)
    for load in loads[3:]:
        load.wait()
    f_all[pl.ds(pl.multiple_of(clip * kc, 8), kc), :] = f_ref[...]
    row = lax.broadcasted_iota(jnp.int32, (128, 64), 0)
    col = lax.broadcasted_iota(jnp.int32, (128, 64), 1)
    for core in range(2):
        there = col == 8 * (row // 16) + 4 * core + row % 4
        for q in range(4):
            pick = there & (row // 4 % 4 == q)
            picks[core, q] = jnp.where(pick, 1.0, 0.0).astype(jnp.bfloat16)
    first = pl.multiple_of(c * half + (xl * 2 + z // 4) * (nn // 8), nn // 8)
    lab = lab_ref[pl.ds(first, nn // 8), :].astype(jnp.float32).T
    lab_t[0] = lab[0:4 * kw, :]
    lab_t[1] = lab[4 * kw:8 * kw, :]
    for b in range(nf // 128):
        column = jnp.broadcast_to(0.5 * ph_ref[b:b + 1, :], (128, 128)).T
        for n in range(nn // 128):
            ang[128 * b:128 * b + 128, 128 * n:128 * n + 128] = column

    bytes_of(e_raw.at[1], eq_r.at[1])
    bytes_of(e_raw.at[2], eq_r.at[2])
    e_all[e_rows(z, 1 - xl), lanes_c] = join(e_raw[1], e_raw[2])
    e_start(1, 1 - xl)

    def e_step(direction, o, s):
        dz = (NZ - s) if direction == 0 else s
        z_ = lax.rem(z + dz, NZ)
        xl_ = (1 - xl) if o else xl
        piece = e_piece(z_, xl_)
        bytes_of(piece, er_r.at[direction, o, s - 1])
        on = piece if s < 3 else e_far_piece(z_, xl_, direction)
        put(on, on, er_s.at[direction, o, s], er_r.at[direction, o, s], z_up if direction == 0 else z_down)
        put(piece, piece, ep_s.at[o, dz], ep_r.at[dz], partner)

    def e_far(direction, o):
        z_ = lax.rem(z + 4, NZ)
        xl_ = (1 - xl) if o else xl
        piece = e_far_piece(z_, xl_, direction)
        bytes_of(piece, er_r.at[direction, o, 3])
        put(piece, piece, ep_s.at[o, 4 + 4 * direction], ep_r.at[4], partner)

    def e_prep(dz, lanes):
        z_ = lax.rem(z + dz, NZ)
        x = 0.5 * e_all[pl.ds(pl.multiple_of(z_ * kc, 16), kc), lanes]
        hi = x.astype(jnp.bfloat16)
        e3[z_, 0:kc, lanes] = hi
        e3[z_, kc:2 * kc, lanes] = (x - hi.astype(jnp.float32)).astype(jnp.bfloat16)
        e3[z_, 2 * kc:3 * kc, lanes] = hi

    def e_other(dz):
        z_ = lax.rem(z + dz, NZ)
        bytes_of(e_all.at[pl.ds(pl.multiple_of(z_ * kc, 16), kc), lanes_o], ep_r.at[dz])
        e_prep(dz, lanes_o)

    def f_prep(u, dy):
        j = clip_of(u, dy)
        x = f_all[pl.ds(pl.multiple_of(j * kc, 16), kc), :]
        hi = x.astype(jnp.bfloat16)
        lo = (x - hi.astype(jnp.float32)).astype(jnp.bfloat16)
        f3[j] = jnp.concatenate([hi, hi, lo], axis=0).T

    def f_wait(direction, u, k, clip_, lo, hi):
        bytes_of(f_block(clip_, lo, hi), fy_r.at[direction, u, k])

    dot = functools.partial(jnp.dot, preferred_element_type=jnp.float32)

    LAST = 9
    far = lax.rem(z + 4, NZ)
    beside = jnp.where(far == clip_of(1, 2), clip_of(1, 1), clip_of(1, 2))

    def stage_of(j):
        up = lax.rem(j - z + NZ, NZ)
        e_turn = jnp.minimum(up, NZ - up)
        e_turn = e_turn + e_turn // 3
        right = lax.rem(lax.rem(j, NY) - y + NY, NY)
        away = jnp.minimum(right, NY - right)
        f_turn = jnp.where(j // NY == xh, away, 2 + away)
        return jnp.where(j == beside, LAST, jnp.maximum(e_turn, f_turn))

    def products(stage, first, count):
        @pl.loop(0, count)
        def _(i):
            j = lax.rem(xh * NY + first + i, 2 * NY)

            @pl.when(stage_of(j) == stage)
            def _():
                ang[...] = ang[...] + dot(f3[j], e3[j])

    e_step(0, 0, 1)
    e_step(1, 0, 1)
    greeted(1)
    greet(2)
    f_wait(0, 0, 0, clip_of(0, 3), 0, mid)
    f_send(0, 0, 2, clip_of(0, 3), 0, mid)
    f_wait(1, 0, 0, clip_of(0, 1), mid, kc)
    f_send(1, 0, 2, clip_of(0, 1), mid, kc)
    bytes_of(f_rel.at[cut:kc, :], fx_r.at[1])
    put(f_rel.at[cut:kc, :], f_block(clip_of(1, 0), cut, kc), fx_s.at[3], fx_r.at[3], x_near)
    bytes_of(f_rel.at[0:cut, :], fx_r.at[0])
    put(f_rel.at[0:cut, :], f_block(clip, 0, cut), fx_s.at[2], fx_r.at[2], x_cross)
    e_prep(0, lanes_c)
    f_prep(0, 0)
    e_other(0)
    products(0, 0, 8)
    e_step(0, 1, 1)
    e_step(1, 1, 1)
    e_prep(1, lanes_c)
    e_prep(7, lanes_c)
    f_wait(0, 0, 1, clip_of(0, 3), mid, kc)
    f_wait(1, 0, 1, clip_of(0, 1), 0, mid)
    f_prep(0, 1)
    f_prep(0, 3)
    over = clip_of(1, 0)
    bytes_of(f_block(over, 0, cut), fx_r.at[2])
    f_send(0, 1, 0, over, 0, cut)
    f_send(1, 1, 0, over, 0, cut)
    e_step(0, 0, 2)
    e_step(1, 0, 2)
    e_other(1)
    e_other(7)
    bytes_of(f_block(over, cut, kc), fx_r.at[3])
    f_send(0, 1, 1, over, cut, mid)
    f_send(1, 1, 1, over, mid, kc)
    f_send(0, 1, 2, over, mid, kc)
    f_send(1, 1, 2, over, cut, mid)
    products(1, 0, 4)
    e_step(0, 1, 2)
    e_step(1, 1, 2)
    products(1, 4, 4)
    e_prep(2, lanes_c)
    e_prep(6, lanes_c)
    f_wait(0, 0, 2, clip_of(0, 2), 0, mid)
    f_wait(1, 0, 2, clip_of(0, 2), mid, kc)
    f_prep(0, 2)
    f_prep(1, 0)
    e_other(2)
    e_other(6)
    e_step(0, 0, 3)
    e_step(1, 0, 3)
    products(2, 0, 2)
    f_wait(0, 1, 0, clip_of(1, 3), 0, cut)
    f_wait(0, 1, 1, clip_of(1, 3), cut, mid)
    f_send(0, 1, 3, clip_of(1, 3), 0, mid)
    f_wait(1, 1, 0, clip_of(1, 1), 0, cut)
    f_wait(1, 1, 1, clip_of(1, 1), mid, kc)
    f_send(1, 1, 3, clip_of(1, 1), mid, kc)
    greeted(2)
    for u, dy in clip_offsets:
        send_w(u, dy)
    products(2, 2, 6)
    e_step(0, 1, 3)
    e_step(1, 1, 3)
    f_wait(0, 1, 2, clip_of(1, 3), mid, kc)
    f_wait(1, 1, 2, clip_of(1, 1), cut, mid)
    f_prep(1, 1)
    f_prep(1, 3)
    products(3, 4, 4)
    e_prep(3, lanes_c)
    e_prep(5, lanes_c)
    e_far(0, 0)
    e_far(1, 0)
    e_other(3)
    e_other(5)
    products(4, 0, 4)
    e_far(0, 1)
    e_far(1, 1)
    e_prep(4, lanes_c)
    products(4, 4, 4)
    f_wait(0, 1, 3, clip_of(1, 2), 0, mid)
    f_wait(1, 1, 3, clip_of(1, 2), mid, kc)
    f_prep(1, 2)
    e_other(4)

    for n in range(nn // 256):
        cols = slice(256 * n, 256 * n + 256)
        x = ang[:, cols] + dot(f3[beside], e3[beside, :, cols]) + dot(f3[far], e3[far, :, cols])
        phi[:, cols] = scaled_cos_of_twice(x, scale).astype(jnp.bfloat16)

    hk = w_t.shape[1] // 2
    block = nn // 8
    chains = range(2)

    def chain_rows(h):
        return slice(h * hk, (h + 1) * hk)

    def block_rows(z_):
        return pl.ds(pl.multiple_of(lax.rem(z_, 4) * 16, 16), 16)

    def block_lanes(z_, xl_, core=None):
        lane = (xl_ * 2 + z_ // 4) * block
        if core is not None:
            lane = lane + core * half
        return pl.ds(pl.multiple_of(lane, block), block)

    nt = functools.partial(
        lax.dot_general, dimension_numbers=(((1,), (1,)), ((), ())), preferred_element_type=jnp.float32)

    def wait_w(t, h):
        for own, count in ((True, 3), (False, 4)):
            @pl.when((xh == h) == own)
            def _():
                bytes_of(g_recv.at[0, 0:count], w_r.at[t, h])

    def start_logits(t, h):
        w = w_t[t, chain_rows(h), :]
        c_send[t, h] = dot(w, phi[:, lanes_o]).astype(jnp.bfloat16)
        put(c_send.at[t, h], c_recv.at[t, h], c_s.at[t, h], c_r.at[t, h], partner)
        part[h] = dot(w, phi[:, lanes_c])

    def share_logits(t, h):
        bytes_of(c_recv.at[t, h], c_r.at[t, h])
        total = part[h] + c_recv[t, h].astype(jnp.float32)
        part[h] = total
        l_send[t, h] = total.astype(jnp.bfloat16)
        for dz, dx in feat_offsets:
            pz, px = feat_peer(dz, dx)
            put(l_send.at[t, h, block_rows(pz), block_lanes(pz, px)], l_recv.at[t, h, dx * NZ + dz - 1],
                l_s.at[t, h], l_r.at[t, h], (clip, feat_of(pz, px, c)), False)

    bytes_of(g_recv.at[0], w_r.at[0, 0])
    out = dot(w_t[0], phi[:, lanes_o]).astype(jnp.bfloat16)
    for h in chains:
        c_send[0, h] = out[chain_rows(h), :]
        put(c_send.at[0, h], c_recv.at[0, h], c_s.at[0, h], c_r.at[0, h], partner)
    out = dot(w_t[0], phi[:, lanes_c])
    for h in chains:
        part[h] = out[chain_rows(h), :]
    for t in range(STEPS):
        for h in chains:
            if t > 0:
                wait_w(t, h)
                start_logits(t, h)
            share_logits(t, h)
        for h in chains:
            acc = part[h, block_rows(z), block_lanes(z, xl)]
            bytes_of(l_recv.at[t, h], l_r.at[t, h])
            for i in range(2 * NZ - 1):
                acc = acc + l_recv[t, h, i].astype(jnp.float32)
            labels = lab_t[h, block_rows(z), :]
            r_t[t, h, block_rows(z), block_lanes(z, xl, c)] = (jax.nn.sigmoid(acc) - labels).astype(jnp.bfloat16)
            mine_r = r_t.at[t, h, block_rows(z), block_lanes(z, xl, c)]
            for dz, dx in feat_offsets:
                pz, px = feat_peer(dz, dx)
                put(mine_r, mine_r, r_s.at[t, h], r_r.at[t, h], (clip, feat_of(pz, px, c)), False)
        for h in chains:
            bytes_of(l_recv.at[t, h], r_r.at[t, h])
            half_r = r_t.at[t, h, :, lanes_c]
            put(half_r, half_r, rc_s.at[t, h], rc_r.at[t, h], partner)
            grad[h] = nt(r_t[t, h, :, lanes_c], phi[:, lanes_c])
            bytes_of(r_t.at[t, h, :, lanes_o], rc_r.at[t, h])
            total = grad[h] + nt(r_t[t, h, :, lanes_o], phi[:, lanes_o])
            grad[h] = total
            g_send[t, h] = total.astype(jnp.bfloat16)

            def send_g(dy, slot):
                yo = lax.rem(y + dy, NY)
                put(g_send.at[t, h, pl.ds(pl.multiple_of(yo * kw, kw), kw), :], g_recv.at[t, slot],
                    g_s.at[t, h], g_r.at[t], (h * NY + yo, feat), False)

            slot = jnp.where(xh == h, -1, 3)
            for dy in (2, 1, 3):
                send_g(dy, slot + dy)

            @pl.when(xh != h)
            def _():
                send_g(0, 3)
        for h in chains:
            @pl.when(xh == h)
            def _():
                g = grad[h, pl.ds(pl.multiple_of(y * kw, kw), kw), :]
                bytes_of(g_recv.at[t], g_r.at[t])
                for i in range(7):
                    g = g + g_recv[t, i].astype(jnp.float32)
                w_new = w_own[...] - 0.25 * g
                w_own[...] = w_new
                w_half = w_new.astype(jnp.bfloat16)
                w_send[t + 1] = w_half
                w_t[t + 1, my_rows, :] = w_half
                for u, dy in clip_offsets:
                    put(w_send.at[t + 1], w_t.at[t + 1, my_rows, :], w_s.at[t + 1], w_r.at[t + 1, h],
                        (clip_of(u, dy), feat), False)
    tr_ref[...] = w_own[...]

    t = STEPS

    def chip_blocks(h, core):
        out = dot(picks[core, 0], logits[h, :, 0:quarter])
        for q in range(1, 4):
            out = out + dot(picks[core, q], logits[h, :, q * quarter:(q + 1) * quarter])
        return out

    def chip_rows(z_, xl_):
        return pl.ds(pl.multiple_of((2 * lax.rem(z_, 4) + xl_) * 16, 16), 16)

    zh = z // 4
    for h in chains:
        wait_w(t, h)
        logits[h] = dot(w_t[t, chain_rows(h), :], phi[...]).astype(jnp.bfloat16)
        s_out[h] = chip_blocks(h, 1 - c).astype(jnp.bfloat16)
        put(s_out.at[h], s_in.at[h], c_s.at[t, h], c_r.at[t, h], partner)
        s_own[h] = chip_blocks(h, c)
        bytes_of(s_in.at[h], c_r.at[t, h])
        total = s_own[h] + s_in[h].astype(jnp.float32)
        s_own[h] = total
        s_sum[h] = total.astype(jnp.bfloat16)

        def send_s(dz, dx, slot):
            pz = h * 4 + lax.rem(z + dz, 4)
            px = 1 - xl if dx else xl
            put(s_sum.at[h, chip_rows(pz, px), :], s_recv.at[slot], l_s.at[t, h], l_r.at[t, 0], (clip, feat_of(pz, px, c)), False)

        slot = jnp.where(zh == h, -1, 7)
        for dz in (2, 1, 3, 0):
            for dx in (1, 0):
                if (dz, dx) != (0, 0):
                    send_s(dz, dx, slot + dx * 4 + dz)

        @pl.when(zh != h)
        def _():
            send_s(0, 0, 7)
    acc = s_own[zh, chip_rows(z, xl), :]
    bytes_of(s_recv, l_r.at[t, 0])
    for i in range(2 * NZ - 1):
        acc = acc + s_recv[i].astype(jnp.float32)
    for q in range(4):
        sc_ref[:, q * quarter:(q + 1) * quarter] = acc[4 * q:4 * q + 4, :]

    for copy in sends:
        copy.wait_send()
    for t in range(STEPS + 1):
        bytes_of(g_recv.at[0], w_s.at[t])
    for h in chains:
        for t in range(STEPS):
            bytes_of(l_recv.at[0, 0], l_s.at[t, h])
            bytes_of(l_recv.at[0, 0], r_s.at[t, h])
        for own, count in ((True, 3), (False, 4)):
            @pl.when((xh == h) == own)
            def _():
                for t in range(STEPS):
                    bytes_of(g_recv.at[0, 0:count], g_s.at[t, h])
        for own, count in ((True, 7), (False, 8)):
            @pl.when((zh == h) == own)
            def _():
                bytes_of(s_recv.at[0:count], l_s.at[STEPS, h])


def per_device(embeds, frequencies, phases, weights, labels):
    nn, ke = embeds.shape
    kc, nf = frequencies.shape
    kw = weights.shape[1]
    kk = labels.shape[1]
    kt = kc * lax.axis_size("clip")
    total_features = nf * lax.axis_size("feat")
    scale = math.sqrt(2.0 / total_features)
    f32, b16 = jnp.float32, jnp.bfloat16
    dma = pltpu.SemaphoreType.DMA
    hbm = pl.BlockSpec(memory_space=pl.ANY)
    vmem = pl.BlockSpec(memory_space=pltpu.VMEM)
    half, quarter = nn // 2, nn // 4
    steps = STEPS + 1
    scratch = [
        pltpu.VMEM((ke, nn), f32),
        pltpu.VMEM((kc, nf), f32),
        pltpu.VMEM((nf // 128, 128), f32),
        pltpu.VMEM((kw, nf), f32),
        pltpu.VMEM((nn, kk), jnp.int32),
        pltpu.VMEM((2, 4, 128, 64), b16),
        pltpu.VMEM((kt, nn), f32),
        pltpu.VMEM((kt, nf), f32),
        pltpu.VMEM((3, ke, half), f32),
        pltpu.VMEM((2 * ke, half), f32),
        pltpu.VMEM((kc, nf), f32),
        pltpu.VMEM((8, 3 * kc, nn), b16),
        pltpu.VMEM((8, nf, 3 * kc), b16),
        pltpu.VMEM((nf, nn), f32),
        pltpu.VMEM((nf, nn), b16),
        pltpu.VMEM((2, kk // 2, nn // 8), f32),
        pltpu.VMEM((kw, nf), f32),
        pltpu.VMEM((steps, kw, nf), b16),
        pltpu.VMEM((steps, kk, nf), b16),
        pltpu.VMEM((2, kk // 2, half), f32),
        pltpu.VMEM((STEPS, 2, kk // 2, half), b16),
        pltpu.VMEM((STEPS, 2, kk // 2, half), b16),
        pltpu.VMEM((STEPS, 2, kk // 2, half), b16),
        pltpu.VMEM((STEPS, 2, 2 * NZ - 1, 16, nn // 8), b16),
        pltpu.VMEM((STEPS, 2, kk // 2, nn), b16),
        pltpu.VMEM((2, kk // 2, nf), f32),
        pltpu.VMEM((STEPS, 2, kk // 2, nf), b16),
        pltpu.VMEM((STEPS, 7, kw, nf), b16),
        pltpu.VMEM((2, kk // 2, nn), b16),
        pltpu.VMEM((2, 128, quarter), b16),
        pltpu.VMEM((2, 128, quarter), b16),
        pltpu.VMEM((2, 128, quarter), f32),
        pltpu.VMEM((2, 128, quarter), b16),
        pltpu.VMEM((2 * NZ - 1, 16, quarter), b16),
        dma((3,)), dma((3,)), dma((2, 2, 4)), dma((2, 2, 4)), dma((2, NZ + 1)), dma((NZ,)),
        dma((4,)), dma((4,)), dma((2, 2, 4)), dma((2, 2, 4)),
        dma((steps,)), dma((steps, 2)), dma((steps, 2)), dma((steps, 2)), dma((steps, 2)), dma((steps, 2)),
        dma((STEPS, 2)), dma((STEPS, 2)), dma((STEPS, 2)), dma((STEPS, 2)), dma((STEPS, 2)), dma((STEPS,)),
        dma((5,)), pltpu.SemaphoreType.REGULAR((3,)),
    ]
    trained_t, scores_t = pl.pallas_call(
        functools.partial(kernel, scale),
        out_shape=(pltpu.VMEM((kw, nf), f32), pltpu.VMEM((4, nn), f32)),
        in_specs=[hbm] * 5,
        out_specs=(vmem, vmem),
        scratch_shapes=scratch,
        compiler_params=pltpu.CompilerParams(
            collective_id=0, has_side_effects=True, vmem_limit_bytes=60 * 1024 * 1024),
    )(embeds.T, frequencies, phases.reshape(nf // 128, 128), weights.T, labels)
    return trained_t.T, scores_t.T


def solution(mesh):
    placed = (P("clip", "feat"), P("clip", "feat"), P("feat"), P("feat", "clip"), P("clip", None))
    return jax.shard_map(
        per_device,
        mesh=mesh,
        in_specs=placed,
        out_specs=(P("feat", "clip"), P("clip", "feat")),
        check_vma=False,
    )
```

```python
import functools
import math

import jax
import jax.numpy as jnp
from jax import lax
from jax.experimental import pallas as pl
from jax.experimental.pallas import tpu as pltpu
from jax.sharding import PartitionSpec as P

STEPS = 2
MESH = pl.DeviceIdType.MESH

NY = 4
NZ = 8

PI_A = 3.1416015625
PI_B = -8.90890987648163e-06
SIN = (9.99999976e-01, -1.66666473e-01, 8.33289467e-03, -1.98005800e-04, 2.58984559e-06)


def scaled_cos_of_twice(h, scale):
    q = jnp.round(h * (1.0 / math.pi))
    w = (h - q * PI_A) - q * PI_B
    w2 = w * w
    root = math.sqrt(2.0 * scale)
    p = root * SIN[4]
    for c in SIN[3::-1]:
        p = p * w2 + root * c
    s = w * p
    return scale - s * s


def bytes_of(ref, sem):
    pltpu.make_async_copy(ref, ref, sem).wait()


def kernel(
    scale,
    e_hbm, f_hbm, ph_hbm, w_hbm, lab_hbm,
    tr_ref, sc_ref,
    e_ref, f_ref, ph_ref, w_ref, lab_ref, picks,
    e_all, f_all, e_raw, e_two, f_rel,
    e3, f3, ang, phi, lab_t,
    w_own, w_send, w_t,
    part, c_send, c_recv, l_send, l_recv, r_t,
    grad, g_send, g_recv, logits, s_out, s_in, s_own, s_sum, s_recv,
    eq_s, eq_r, er_s, er_r, ep_s, ep_r,
    fx_s, fx_r, fy_s, fy_r,
    w_s, w_r, c_s, c_r, l_s, l_r, r_s, r_r, rc_s, rc_r, g_s, g_r,
    in_s, hello,
):
    loads = [
        pltpu.make_async_copy(src, dst, in_s.at[i])
        for i, (src, dst) in enumerate(
            ((e_hbm, e_ref), (f_hbm, f_ref), (w_hbm, w_ref), (ph_hbm, ph_ref), (lab_hbm, lab_ref)))
    ]
    for load in loads:
        load.start()

    clip = lax.axis_index("clip")
    feat = lax.axis_index("feat")
    c = lax.rem(feat, 2)
    xl = lax.rem(feat // 2, 2)
    z = feat // 4
    y = lax.rem(clip, NY)
    xh = clip // NY

    ke = e_ref.shape[0]
    kc = 4 * ke
    nf = f_ref.shape[1]
    nn = e_ref.shape[1]
    half = nn // 2
    quarter = nn // 4
    kw = w_ref.shape[0]

    def feat_of(z_, xl_, c_):
        return (z_ * 2 + xl_) * 2 + c_

    def clip_of(u, dy):
        return ((1 - xh) if u else xh) * NY + lax.rem(y + dy, NY)

    partner = (clip, feat_of(z, xl, 1 - c))
    x_near = (clip, feat_of(z, 1 - xl, c))
    diag = (clip, feat_of(z, 1 - xl, 1 - c))
    x_cross = (clip_of(1, 0), feat_of(z, 1 - xl, c))
    y_right = (clip_of(0, 1), feat)
    y_left = (clip_of(0, NY - 1), feat)
    z_up = (clip, feat_of(lax.rem(z + 1, NZ), xl, c))
    z_down = (clip, feat_of(lax.rem(z + NZ - 1, NZ), xl, c))

    def feat_peer(dz, dx):
        return lax.rem(z + dz, NZ), (1 - xl if dx else xl)

    feat_offsets = [(dz, dx) for dz in (4, 3, 5, 2, 6, 1, 7, 0) for dx in (1, 0) if (dz, dx) != (0, 0)]
    clip_offsets = [(u, dy) for dy in (2, 1, 3, 0) for u in (1, 0) if (u, dy) != (0, 0)]

    barrier = pltpu.get_barrier_semaphore()
    neighbours = [partner, x_near, x_cross, diag, z_up, z_down, y_right, y_left]
    for peer in neighbours:
        pl.semaphore_signal(barrier, inc=1, device_id=peer, device_id_type=MESH)

    def local_block(clip_):
        return clip_ // NY * 2 + lax.rem(clip_, 2)

    my_chain = y // 2
    my_rows = pl.ds(pl.multiple_of(my_chain * 4 * kw + local_block(clip) * kw, kw), kw)
    for load in loads[0:3]:
        load.wait()
    w_own[...] = w_ref[...]
    w_send[0] = w_ref[...].astype(jnp.bfloat16)
    w_t[0, my_rows, :] = w_ref[...].astype(jnp.bfloat16)

    pl.semaphore_wait(barrier, len(neighbours))

    def greet(n):
        for peer in (x_near, x_cross, y_right, y_left):
            pl.semaphore_signal(hello.at[n], inc=1, device_id=peer, device_id_type=MESH)

    def greeted(n):
        pl.semaphore_wait(hello.at[n], 4)

    greet(0)
    sends = []

    def put(src, dst, s_sem, r_sem, to, own_sem=True):
        copy = pltpu.make_async_remote_copy(
            src_ref=src, dst_ref=dst, send_sem=s_sem, recv_sem=r_sem, device_id=to, device_id_type=MESH)
        copy.start()
        if own_sem:
            sends.append(copy)

    lanes_c = pl.ds(pl.multiple_of(c * half, half), half)
    lanes_o = pl.ds(pl.multiple_of((1 - c) * half, half), half)

    def e_rows(z_, xl_):
        return pl.ds(pl.multiple_of(z_ * kc + xl_ * (2 * ke), 8), 2 * ke)

    def e_piece(z_, xl_):
        return e_all.at[e_rows(z_, xl_), lanes_c]

    def e_far_piece(z_, xl_, direction):
        lane = pl.multiple_of(c * half + direction * quarter, quarter)
        return e_all.at[e_rows(z_, xl_), pl.ds(lane, quarter)]

    def f_block(clip_, lo, hi):
        return f_all.at[pl.ds(pl.multiple_of(clip_ * kc + lo, 8), hi - lo), :]

    def send_w(u, dy):
        put(w_send.at[0], w_t.at[0, my_rows, :], w_s.at[0], w_r.at[0, 0], (clip_of(u, dy), feat), False)

    put(e_ref.at[:, lanes_o], e_raw.at[0], eq_s.at[0], eq_r.at[0], partner)
    put(e_ref.at[:, lanes_c], e_raw.at[1], eq_s.at[1], eq_r.at[1], x_near)
    put(e_ref.at[:, lanes_o], e_raw.at[2], eq_s.at[2], eq_r.at[2], diag)

    cut = kc // 3
    mid = kc // 2
    put(f_ref.at[cut:kc, :], f_rel.at[cut:kc, :], fx_s.at[1], fx_r.at[1], x_cross)
    put(f_ref.at[0:cut, :], f_rel.at[0:cut, :], fx_s.at[0], fx_r.at[0], x_near)
    lows = (0, mid)

    def f_send(direction, u, k, clip_, lo, hi, src=None):
        dst = f_block(clip_, lo, hi)
        put(dst if src is None else src, dst, fy_s.at[direction, u, k], fy_r.at[direction, u, k],
            y_right if direction == 0 else y_left)

    for k in (0, 1):
        for direction in (0, 1):
            lo = lows[k ^ direction]
            f_send(direction, 0, k, clip, lo, lo + mid, f_ref.at[lo:lo + mid, :])
    def join(own, oth):
        first = c == 0
        e_two[0:ke, :] = jnp.where(first, own, oth)
        e_two[ke:2 * ke, :] = jnp.where(first, oth, own)
        return e_two[...]

    def e_start(o, xl_):
        piece = e_piece(z, xl_)
        put(piece, piece, er_s.at[0, o, 0], er_r.at[0, o, 0], z_up)
        put(piece, piece, er_s.at[1, o, 0], er_r.at[1, o, 0], z_down)
        put(piece, piece, ep_s.at[o, 0], ep_r.at[0], partner)

    bytes_of(e_raw.at[0], eq_r.at[0])
    e_all[e_rows(z, xl), lanes_c] = join(e_ref[:, lanes_c], e_raw[0])
    e_start(0, xl)

    greeted(0)
    greet(1)
    for load in loads[3:]:
        load.wait()
    f_all[pl.ds(pl.multiple_of(clip * kc, 8), kc), :] = f_ref[...]
    row = lax.broadcasted_iota(jnp.int32, (128, 64), 0)
    col = lax.broadcasted_iota(jnp.int32, (128, 64), 1)
    for core in range(2):
        there = col == 8 * (row // 16) + 4 * core + row % 4
        for q in range(4):
            pick = there & (row // 4 % 4 == q)
            picks[core, q] = jnp.where(pick, 1.0, 0.0).astype(jnp.bfloat16)
    first = pl.multiple_of(c * half + (xl * 2 + z // 4) * (nn // 8), nn // 8)
    lab = lab_ref[pl.ds(first, nn // 8), :].astype(jnp.float32).T
    for h in range(2):
        for i, of in enumerate((2 * h, 2 * h + 1, NY + 2 * h, NY + 2 * h + 1)):
            lab_t[h, i * kw:(i + 1) * kw, :] = lab[of * kw:(of + 1) * kw, :]
    for b in range(nf // 128):
        column = jnp.broadcast_to(0.5 * ph_ref[b:b + 1, :], (128, 128)).T
        for n in range(nn // 128):
            ang[128 * b:128 * b + 128, 128 * n:128 * n + 128] = column

    bytes_of(e_raw.at[1], eq_r.at[1])
    bytes_of(e_raw.at[2], eq_r.at[2])
    e_all[e_rows(z, 1 - xl), lanes_c] = join(e_raw[1], e_raw[2])
    e_start(1, 1 - xl)

    def e_step(direction, o, s):
        dz = (NZ - s) if direction == 0 else s
        z_ = lax.rem(z + dz, NZ)
        xl_ = (1 - xl) if o else xl
        piece = e_piece(z_, xl_)
        bytes_of(piece, er_r.at[direction, o, s - 1])
        on = piece if s < 3 else e_far_piece(z_, xl_, direction)
        put(on, on, er_s.at[direction, o, s], er_r.at[direction, o, s], z_up if direction == 0 else z_down)
        put(piece, piece, ep_s.at[o, dz], ep_r.at[dz], partner)

    def e_far(direction, o):
        z_ = lax.rem(z + 4, NZ)
        xl_ = (1 - xl) if o else xl
        piece = e_far_piece(z_, xl_, direction)
        bytes_of(piece, er_r.at[direction, o, 3])
        put(piece, piece, ep_s.at[o, 4 + 4 * direction], ep_r.at[4], partner)

    def e_prep(dz, lanes):
        z_ = lax.rem(z + dz, NZ)
        x = 0.5 * e_all[pl.ds(pl.multiple_of(z_ * kc, 16), kc), lanes]
        hi = x.astype(jnp.bfloat16)
        e3[z_, 0:kc, lanes] = hi
        e3[z_, kc:2 * kc, lanes] = (x - hi.astype(jnp.float32)).astype(jnp.bfloat16)
        e3[z_, 2 * kc:3 * kc, lanes] = hi

    def e_other(dz):
        z_ = lax.rem(z + dz, NZ)
        bytes_of(e_all.at[pl.ds(pl.multiple_of(z_ * kc, 16), kc), lanes_o], ep_r.at[dz])
        e_prep(dz, lanes_o)

    def f_prep(u, dy):
        j = clip_of(u, dy)
        x = f_all[pl.ds(pl.multiple_of(j * kc, 16), kc), :]
        hi = x.astype(jnp.bfloat16)
        lo = (x - hi.astype(jnp.float32)).astype(jnp.bfloat16)
        f3[j] = jnp.concatenate([hi, hi, lo], axis=0).T

    def f_wait(direction, u, k, clip_, lo, hi):
        bytes_of(f_block(clip_, lo, hi), fy_r.at[direction, u, k])

    dot = functools.partial(jnp.dot, preferred_element_type=jnp.float32)

    LAST = 9
    far = lax.rem(z + 4, NZ)
    beside = jnp.where(far == clip_of(1, 2), clip_of(1, 1), clip_of(1, 2))

    def stage_of(j):
        up = lax.rem(j - z + NZ, NZ)
        e_turn = jnp.minimum(up, NZ - up)
        e_turn = e_turn + e_turn // 3
        right = lax.rem(lax.rem(j, NY) - y + NY, NY)
        away = jnp.minimum(right, NY - right)
        f_turn = jnp.where(j // NY == xh, away, 2 + away)
        return jnp.where(j == beside, LAST, jnp.maximum(e_turn, f_turn))

    def products(stage, first, count):
        @pl.loop(0, count)
        def _(i):
            j = lax.rem(xh * NY + first + i, 2 * NY)

            @pl.when(stage_of(j) == stage)
            def _():
                ang[...] = ang[...] + dot(f3[j], e3[j])

    e_step(0, 0, 1)
    e_step(1, 0, 1)
    greeted(1)
    greet(2)
    f_wait(0, 0, 0, clip_of(0, 3), 0, mid)
    f_send(0, 0, 2, clip_of(0, 3), 0, mid)
    f_wait(1, 0, 0, clip_of(0, 1), mid, kc)
    f_send(1, 0, 2, clip_of(0, 1), mid, kc)
    bytes_of(f_rel.at[cut:kc, :], fx_r.at[1])
    put(f_rel.at[cut:kc, :], f_block(clip_of(1, 0), cut, kc), fx_s.at[3], fx_r.at[3], x_near)
    bytes_of(f_rel.at[0:cut, :], fx_r.at[0])
    put(f_rel.at[0:cut, :], f_block(clip, 0, cut), fx_s.at[2], fx_r.at[2], x_cross)
    e_prep(0, lanes_c)
    f_prep(0, 0)
    e_other(0)
    products(0, 0, 8)
    e_step(0, 1, 1)
    e_step(1, 1, 1)
    e_prep(1, lanes_c)
    e_prep(7, lanes_c)
    f_wait(0, 0, 1, clip_of(0, 3), mid, kc)
    f_wait(1, 0, 1, clip_of(0, 1), 0, mid)
    f_prep(0, 1)
    f_prep(0, 3)
    over = clip_of(1, 0)
    bytes_of(f_block(over, 0, cut), fx_r.at[2])
    f_send(0, 1, 0, over, 0, cut)
    f_send(1, 1, 0, over, 0, cut)
    e_step(0, 0, 2)
    e_step(1, 0, 2)
    e_other(1)
    e_other(7)
    bytes_of(f_block(over, cut, kc), fx_r.at[3])
    f_send(0, 1, 1, over, cut, mid)
    f_send(1, 1, 1, over, mid, kc)
    f_send(0, 1, 2, over, mid, kc)
    f_send(1, 1, 2, over, cut, mid)
    products(1, 0, 4)
    e_step(0, 1, 2)
    e_step(1, 1, 2)
    products(1, 4, 4)
    e_prep(2, lanes_c)
    e_prep(6, lanes_c)
    f_wait(0, 0, 2, clip_of(0, 2), 0, mid)
    f_wait(1, 0, 2, clip_of(0, 2), mid, kc)
    f_prep(0, 2)
    f_prep(1, 0)
    e_other(2)
    e_other(6)
    e_step(0, 0, 3)
    e_step(1, 0, 3)
    products(2, 0, 2)
    f_wait(0, 1, 0, clip_of(1, 3), 0, cut)
    f_wait(0, 1, 1, clip_of(1, 3), cut, mid)
    f_send(0, 1, 3, clip_of(1, 3), 0, mid)
    f_wait(1, 1, 0, clip_of(1, 1), 0, cut)
    f_wait(1, 1, 1, clip_of(1, 1), mid, kc)
    f_send(1, 1, 3, clip_of(1, 1), mid, kc)
    greeted(2)
    for u, dy in clip_offsets:
        send_w(u, dy)
    products(2, 2, 6)
    e_step(0, 1, 3)
    e_step(1, 1, 3)
    f_wait(0, 1, 2, clip_of(1, 3), mid, kc)
    f_wait(1, 1, 2, clip_of(1, 1), cut, mid)
    f_prep(1, 1)
    f_prep(1, 3)
    products(3, 4, 4)
    e_prep(3, lanes_c)
    e_prep(5, lanes_c)
    e_far(0, 0)
    e_far(1, 0)
    e_other(3)
    e_other(5)
    products(4, 0, 4)
    e_far(0, 1)
    e_far(1, 1)
    e_prep(4, lanes_c)
    products(4, 4, 4)
    f_wait(0, 1, 3, clip_of(1, 2), 0, mid)
    f_wait(1, 1, 3, clip_of(1, 2), mid, kc)
    f_prep(1, 2)
    e_other(4)

    for n in range(nn // 256):
        cols = slice(256 * n, 256 * n + 256)
        x = ang[:, cols] + dot(f3[beside], e3[beside, :, cols]) + dot(f3[far], e3[far, :, cols])
        phi[:, cols] = scaled_cos_of_twice(x, scale).astype(jnp.bfloat16)

    hk = w_t.shape[1] // 2
    block = nn // 8
    chains = range(2)

    def chain_rows(h):
        return slice(h * hk, (h + 1) * hk)

    def block_rows(z_):
        return pl.ds(pl.multiple_of(lax.rem(z_, 4) * 16, 16), 16)

    def block_lanes(z_, xl_, core=None):
        lane = (xl_ * 2 + z_ // 4) * block
        if core is not None:
            lane = lane + core * half
        return pl.ds(pl.multiple_of(lane, block), block)

    nt = functools.partial(
        lax.dot_general, dimension_numbers=(((1,), (1,)), ((), ())), preferred_element_type=jnp.float32)

    def wait_w(t, h):
        for own, count in ((True, 3), (False, 4)):
            @pl.when((my_chain == h) == own)
            def _():
                bytes_of(g_recv.at[0, 0:count], w_r.at[t, h])

    def start_logits(t, h):
        w = w_t[t, chain_rows(h), :]
        c_send[t, h] = dot(w, phi[:, lanes_o]).astype(jnp.bfloat16)
        put(c_send.at[t, h], c_recv.at[t, h], c_s.at[t, h], c_r.at[t, h], partner)
        part[h] = dot(w, phi[:, lanes_c])

    def share_logits(t, h):
        bytes_of(c_recv.at[t, h], c_r.at[t, h])
        total = part[h] + c_recv[t, h].astype(jnp.float32)
        part[h] = total
        l_send[t, h] = total.astype(jnp.bfloat16)
        for dz, dx in feat_offsets:
            pz, px = feat_peer(dz, dx)
            put(l_send.at[t, h, block_rows(pz), block_lanes(pz, px)], l_recv.at[t, h, dx * NZ + dz - 1],
                l_s.at[t, h], l_r.at[t, h], (clip, feat_of(pz, px, c)), False)

    bytes_of(g_recv.at[0], w_r.at[0, 0])
    out = dot(w_t[0], phi[:, lanes_o]).astype(jnp.bfloat16)
    for h in chains:
        c_send[0, h] = out[chain_rows(h), :]
        put(c_send.at[0, h], c_recv.at[0, h], c_s.at[0, h], c_r.at[0, h], partner)
    out = dot(w_t[0], phi[:, lanes_c])
    for h in chains:
        part[h] = out[chain_rows(h), :]
    for t in range(STEPS):
        for h in chains:
            if t > 0:
                wait_w(t, h)
                start_logits(t, h)
            share_logits(t, h)
        for h in chains:
            acc = part[h, block_rows(z), block_lanes(z, xl)]
            bytes_of(l_recv.at[t, h], l_r.at[t, h])
            for i in range(2 * NZ - 1):
                acc = acc + l_recv[t, h, i].astype(jnp.float32)
            labels = lab_t[h, block_rows(z), :]
            r_t[t, h, block_rows(z), block_lanes(z, xl, c)] = (jax.nn.sigmoid(acc) - labels).astype(jnp.bfloat16)
            mine_r = r_t.at[t, h, block_rows(z), block_lanes(z, xl, c)]
            for dz, dx in feat_offsets:
                pz, px = feat_peer(dz, dx)
                put(mine_r, mine_r, r_s.at[t, h], r_r.at[t, h], (clip, feat_of(pz, px, c)), False)
        for h in chains:
            bytes_of(l_recv.at[t, h], r_r.at[t, h])
            half_r = r_t.at[t, h, :, lanes_c]
            put(half_r, half_r, rc_s.at[t, h], rc_r.at[t, h], partner)
            grad[h] = nt(r_t[t, h, :, lanes_c], phi[:, lanes_c])
            bytes_of(r_t.at[t, h, :, lanes_o], rc_r.at[t, h])
            total = grad[h] + nt(r_t[t, h, :, lanes_o], phi[:, lanes_o])
            grad[h] = total
            g_send[t, h] = total.astype(jnp.bfloat16)

            def send_g(u, yo):
                to = clip_of(u, yo - y + NY)
                rows = pl.ds(pl.multiple_of(local_block(to) * kw, kw), kw)
                slot = u * NY + lax.rem(yo - y + NY, NY) - 1
                put(g_send.at[t, h, rows, :], g_recv.at[t, slot], g_s.at[t, h], g_r.at[t], (to, feat), False)

            for yo in (2 * h, 2 * h + 1):
                send_g(1, yo)

                @pl.when(yo != y)
                def _():
                    send_g(0, yo)
        for h in chains:
            @pl.when(my_chain == h)
            def _():
                g = grad[h, pl.ds(pl.multiple_of(local_block(clip) * kw, kw), kw), :]
                bytes_of(g_recv.at[t], g_r.at[t])
                for i in range(7):
                    g = g + g_recv[t, i].astype(jnp.float32)
                w_new = w_own[...] - 0.25 * g
                w_own[...] = w_new
                w_half = w_new.astype(jnp.bfloat16)
                w_send[t + 1] = w_half
                w_t[t + 1, my_rows, :] = w_half
                for u, dy in clip_offsets:
                    put(w_send.at[t + 1], w_t.at[t + 1, my_rows, :], w_s.at[t + 1], w_r.at[t + 1, h],
                        (clip_of(u, dy), feat), False)
    tr_ref[...] = w_own[...]

    t = STEPS

    def chip_blocks(h, core):
        out = dot(picks[core, 0], logits[h, :, 0:quarter])
        for q in range(1, 4):
            out = out + dot(picks[core, q], logits[h, :, q * quarter:(q + 1) * quarter])
        return out

    def chip_rows(z_, xl_):
        return pl.ds(pl.multiple_of((2 * local_block(z_) + xl_) * 16, 16), 16)

    z_chain = lax.rem(z, 4) // 2
    for h in chains:
        wait_w(t, h)
        logits[h] = dot(w_t[t, chain_rows(h), :], phi[...]).astype(jnp.bfloat16)
        s_out[h] = chip_blocks(h, 1 - c).astype(jnp.bfloat16)
        put(s_out.at[h], s_in.at[h], c_s.at[t, h], c_r.at[t, h], partner)
        s_own[h] = chip_blocks(h, c)
        bytes_of(s_in.at[h], c_r.at[t, h])
        total = s_own[h] + s_in[h].astype(jnp.float32)
        s_own[h] = total
        s_sum[h] = total.astype(jnp.bfloat16)

        def send_s(pz, dx):
            px = 1 - xl if dx else xl
            slot = dx * NZ + lax.rem(pz - z + NZ, NZ) - 1
            put(s_sum.at[h, chip_rows(pz, px), :], s_recv.at[slot], l_s.at[t, h], l_r.at[t, 0], (clip, feat_of(pz, px, c)), False)

        for pz in (2 * h, 2 * h + 1, NY + 2 * h, NY + 2 * h + 1):
            send_s(pz, 1)

            @pl.when(pz != z)
            def _():
                send_s(pz, 0)
    acc = s_own[z_chain, chip_rows(z, xl), :]
    bytes_of(s_recv, l_r.at[t, 0])
    for i in range(2 * NZ - 1):
        acc = acc + s_recv[i].astype(jnp.float32)
    for q in range(4):
        sc_ref[:, q * quarter:(q + 1) * quarter] = acc[4 * q:4 * q + 4, :]

    for copy in sends:
        copy.wait_send()
    for t in range(STEPS + 1):
        bytes_of(g_recv.at[0], w_s.at[t])
    for h in chains:
        for t in range(STEPS):
            bytes_of(l_recv.at[0, 0], l_s.at[t, h])
            bytes_of(l_recv.at[0, 0], r_s.at[t, h])
        for own, count in ((True, 3), (False, 4)):
            @pl.when((my_chain == h) == own)
            def _():
                for t in range(STEPS):
                    bytes_of(g_recv.at[0, 0:count], g_s.at[t, h])
        for own, count in ((True, 7), (False, 8)):
            @pl.when((z_chain == h) == own)
            def _():
                bytes_of(s_recv.at[0:count], l_s.at[STEPS, h])


def per_device(embeds, frequencies, phases, weights, labels):
    nn, ke = embeds.shape
    kc, nf = frequencies.shape
    kw = weights.shape[1]
    kk = labels.shape[1]
    kt = kc * lax.axis_size("clip")
    total_features = nf * lax.axis_size("feat")
    scale = math.sqrt(2.0 / total_features)
    f32, b16 = jnp.float32, jnp.bfloat16
    dma = pltpu.SemaphoreType.DMA
    hbm = pl.BlockSpec(memory_space=pl.ANY)
    vmem = pl.BlockSpec(memory_space=pltpu.VMEM)
    half, quarter = nn // 2, nn // 4
    steps = STEPS + 1
    scratch = [
        pltpu.VMEM((ke, nn), f32),
        pltpu.VMEM((kc, nf), f32),
        pltpu.VMEM((nf // 128, 128), f32),
        pltpu.VMEM((kw, nf), f32),
        pltpu.VMEM((nn, kk), jnp.int32),
        pltpu.VMEM((2, 4, 128, 64), b16),
        pltpu.VMEM((kt, nn), f32),
        pltpu.VMEM((kt, nf), f32),
        pltpu.VMEM((3, ke, half), f32),
        pltpu.VMEM((2 * ke, half), f32),
        pltpu.VMEM((kc, nf), f32),
        pltpu.VMEM((8, 3 * kc, nn), b16),
        pltpu.VMEM((8, nf, 3 * kc), b16),
        pltpu.VMEM((nf, nn), f32),
        pltpu.VMEM((nf, nn), b16),
        pltpu.VMEM((2, kk // 2, nn // 8), f32),
        pltpu.VMEM((kw, nf), f32),
        pltpu.VMEM((steps, kw, nf), b16),
        pltpu.VMEM((steps, kk, nf), b16),
        pltpu.VMEM((2, kk // 2, half), f32),
        pltpu.VMEM((STEPS, 2, kk // 2, half), b16),
        pltpu.VMEM((STEPS, 2, kk // 2, half), b16),
        pltpu.VMEM((STEPS, 2, kk // 2, half), b16),
        pltpu.VMEM((STEPS, 2, 2 * NZ - 1, 16, nn // 8), b16),
        pltpu.VMEM((STEPS, 2, kk // 2, nn), b16),
        pltpu.VMEM((2, kk // 2, nf), f32),
        pltpu.VMEM((STEPS, 2, kk // 2, nf), b16),
        pltpu.VMEM((STEPS, 7, kw, nf), b16),
        pltpu.VMEM((2, kk // 2, nn), b16),
        pltpu.VMEM((2, 128, quarter), b16),
        pltpu.VMEM((2, 128, quarter), b16),
        pltpu.VMEM((2, 128, quarter), f32),
        pltpu.VMEM((2, 128, quarter), b16),
        pltpu.VMEM((2 * NZ - 1, 16, quarter), b16),
        dma((3,)), dma((3,)), dma((2, 2, 4)), dma((2, 2, 4)), dma((2, NZ + 1)), dma((NZ,)),
        dma((4,)), dma((4,)), dma((2, 2, 4)), dma((2, 2, 4)),
        dma((steps,)), dma((steps, 2)), dma((steps, 2)), dma((steps, 2)), dma((steps, 2)), dma((steps, 2)),
        dma((STEPS, 2)), dma((STEPS, 2)), dma((STEPS, 2)), dma((STEPS, 2)), dma((STEPS, 2)), dma((STEPS,)),
        dma((5,)), pltpu.SemaphoreType.REGULAR((3,)),
    ]
    trained_t, scores_t = pl.pallas_call(
        functools.partial(kernel, scale),
        out_shape=(pltpu.VMEM((kw, nf), f32), pltpu.VMEM((4, nn), f32)),
        in_specs=[hbm] * 5,
        out_specs=(vmem, vmem),
        scratch_shapes=scratch,
        compiler_params=pltpu.CompilerParams(
            collective_id=0, has_side_effects=True, vmem_limit_bytes=60 * 1024 * 1024),
    )(embeds.T, frequencies, phases.reshape(nf // 128, 128), weights.T, labels)
    return trained_t.T, scores_t.T


def solution(mesh):
    placed = (P("clip", "feat"), P("clip", "feat"), P("feat"), P("feat", "clip"), P("clip", None))
    return jax.shard_map(
        per_device,
        mesh=mesh,
        in_specs=placed,
        out_specs=(P("feat", "clip"), P("clip", "feat")),
        check_vma=False,
    )
```

```python
import functools
import math

import jax
import jax.numpy as jnp
from jax import lax
from jax.experimental import pallas as pl
from jax.experimental.pallas import tpu as pltpu
from jax.sharding import PartitionSpec as P

STEPS = 2
MESH = pl.DeviceIdType.MESH

NY = 4
NZ = 8

PI_A = 3.1416015625
PI_B = -8.90890987648163e-06
SIN = (9.99999976e-01, -1.66666473e-01, 8.33289467e-03, -1.98005800e-04, 2.58984559e-06)


def scaled_cos_of_twice(h, scale):
    q = jnp.round(h * (1.0 / math.pi))
    w = (h - q * PI_A) - q * PI_B
    w2 = w * w
    root = math.sqrt(2.0 * scale)
    p = root * SIN[4]
    for c in SIN[3::-1]:
        p = p * w2 + root * c
    s = w * p
    return scale - s * s


def bytes_of(ref, sem):
    pltpu.make_async_copy(ref, ref, sem).wait()


def kernel(
    scale,
    e_hbm, f_hbm, ph_hbm, w_hbm, lab_hbm,
    tr_ref, sc_ref,
    e_ref, f_ref, ph_ref, w_ref, lab_ref, picks,
    e_all, f_all, e_raw, e_two, f_rel,
    e3, f3, ang, phi, lab_t,
    w_own, w_send, w_t,
    part, c_send, c_recv, l_send, l_recv, r_t,
    grad, g_send, g_recv, logits, s_out, s_in, s_own, s_sum, s_recv,
    eq_s, eq_r, en_s, er_s, er_r, ep_s, ep_r,
    fx_s, fx_r, fy_s, fy_r,
    w_s, w_r, c_s, c_r, l_s, l_r, r_s, r_r, rc_s, rc_r, g_s, g_r,
    in_s, hello,
):
    loads = [
        pltpu.make_async_copy(src, dst, in_s.at[i])
        for i, (src, dst) in enumerate(
            ((e_hbm, e_ref), (f_hbm, f_ref), (w_hbm, w_ref), (ph_hbm, ph_ref), (lab_hbm, lab_ref)))
    ]
    for load in loads:
        load.start()

    clip = lax.axis_index("clip")
    feat = lax.axis_index("feat")
    c = lax.rem(feat, 2)
    xl = lax.rem(feat // 2, 2)
    z = feat // 4
    y = lax.rem(clip, NY)
    xh = clip // NY

    ke = e_ref.shape[0]
    kc = 4 * ke
    nf = f_ref.shape[1]
    nn = e_ref.shape[1]
    half = nn // 2
    quarter = nn // 4
    kw = w_ref.shape[0]

    def feat_of(z_, xl_, c_):
        return (z_ * 2 + xl_) * 2 + c_

    def clip_of(u, dy):
        return ((1 - xh) if u else xh) * NY + lax.rem(y + dy, NY)

    partner = (clip, feat_of(z, xl, 1 - c))
    x_near = (clip, feat_of(z, 1 - xl, c))
    diag = (clip, feat_of(z, 1 - xl, 1 - c))
    x_cross = (clip_of(1, 0), feat_of(z, 1 - xl, c))
    y_right = (clip_of(0, 1), feat)
    y_left = (clip_of(0, NY - 1), feat)
    z_up = (clip, feat_of(lax.rem(z + 1, NZ), xl, c))
    z_down = (clip, feat_of(lax.rem(z + NZ - 1, NZ), xl, c))

    def feat_peer(dz, dx):
        return lax.rem(z + dz, NZ), (1 - xl if dx else xl)

    feat_offsets = [(dz, dx) for dz in (4, 3, 5, 2, 6, 1, 7, 0) for dx in (1, 0) if (dz, dx) != (0, 0)]
    clip_offsets = [(u, dy) for dy in (2, 1, 3, 0) for u in (1, 0) if (u, dy) != (0, 0)]

    barrier = pltpu.get_barrier_semaphore()
    neighbours = [partner, x_near, x_cross, diag, z_up, z_down, y_right, y_left]
    for peer in neighbours:
        pl.semaphore_signal(barrier, inc=1, device_id=peer, device_id_type=MESH)

    def local_block(clip_):
        return clip_ // NY * 2 + lax.rem(clip_, 2)

    my_chain = y // 2
    my_rows = pl.ds(pl.multiple_of(my_chain * 4 * kw + local_block(clip) * kw, kw), kw)
    for load in loads[0:3]:
        load.wait()
    w_own[...] = w_ref[...]
    w_send[0] = w_ref[...].astype(jnp.bfloat16)
    w_t[0, my_rows, :] = w_ref[...].astype(jnp.bfloat16)

    pl.semaphore_wait(barrier, len(neighbours))

    def greet(n):
        for peer in (x_near, x_cross, y_right, y_left):
            pl.semaphore_signal(hello.at[n], inc=1, device_id=peer, device_id_type=MESH)

    def greeted(n):
        pl.semaphore_wait(hello.at[n], 4)

    greet(0)
    sends = []

    def put(src, dst, s_sem, r_sem, to, own_sem=True):
        copy = pltpu.make_async_remote_copy(
            src_ref=src, dst_ref=dst, send_sem=s_sem, recv_sem=r_sem, device_id=to, device_id_type=MESH)
        copy.start()
        if own_sem:
            sends.append(copy)

    lanes_c = pl.ds(pl.multiple_of(c * half, half), half)
    lanes_o = pl.ds(pl.multiple_of((1 - c) * half, half), half)

    def e_rows(z_, xl_):
        return pl.ds(pl.multiple_of(z_ * kc + xl_ * (2 * ke), 8), 2 * ke)

    def e_piece(z_, xl_):
        return e_all.at[e_rows(z_, xl_), lanes_c]

    def e_far_piece(z_, xl_, direction):
        lane = pl.multiple_of(c * half + direction * quarter, quarter)
        return e_all.at[e_rows(z_, xl_), pl.ds(lane, quarter)]

    def f_block(clip_, lo, hi):
        return f_all.at[pl.ds(pl.multiple_of(clip_ * kc + lo, 8), hi - lo), :]

    def send_w(u, dy):
        put(w_send.at[0], w_t.at[0, my_rows, :], w_s.at[0], w_r.at[0, 0], (clip_of(u, dy), feat), False)

    put(e_ref.at[:, lanes_o], e_raw.at[0], eq_s.at[0, 0], eq_r.at[0, 0], partner)
    for q in range(2):
        part_q = slice(q * quarter, (q + 1) * quarter)
        for i, core, to in ((1, c, x_near), (2, 1 - c, diag)):
            lanes_q = pl.ds(pl.multiple_of(core * half + q * quarter, quarter), quarter)
            put(e_ref.at[:, lanes_q], e_raw.at[i, :, part_q], eq_s.at[i, q], eq_r.at[i, q], to)

    cut = kc // 3
    mid = kc // 2
    put(f_ref.at[cut:kc, :], f_rel.at[cut:kc, :], fx_s.at[1], fx_r.at[1], x_cross)
    put(f_ref.at[0:cut, :], f_rel.at[0:cut, :], fx_s.at[0], fx_r.at[0], x_near)
    lows = (0, mid)

    def f_send(direction, u, k, clip_, lo, hi, src=None):
        dst = f_block(clip_, lo, hi)
        put(dst if src is None else src, dst, fy_s.at[direction, u, k], fy_r.at[direction, u, k],
            y_right if direction == 0 else y_left)

    for k in (0, 1):
        for direction in (0, 1):
            lo = lows[k ^ direction]
            f_send(direction, 0, k, clip, lo, lo + mid, f_ref.at[lo:lo + mid, :])
    def join(own, oth):
        first = c == 0
        lanes = own.shape[1]
        e_two[0:ke, 0:lanes] = jnp.where(first, own, oth)
        e_two[ke:2 * ke, 0:lanes] = jnp.where(first, oth, own)
        return e_two[:, 0:lanes]

    bytes_of(e_raw.at[0], eq_r.at[0, 0])
    e_all[e_rows(z, xl), lanes_c] = join(e_ref[:, lanes_c], e_raw[0])
    own_piece = e_piece(z, xl)
    put(own_piece, own_piece, er_s.at[0, 0, 0], er_r.at[0, 0, 0], z_up)
    put(own_piece, own_piece, er_s.at[1, 0, 0], er_r.at[1, 0, 0], z_down)
    put(own_piece, own_piece, ep_s.at[0, 0], ep_r.at[0], partner)

    greeted(0)
    greet(1)
    for load in loads[3:]:
        load.wait()
    f_all[pl.ds(pl.multiple_of(clip * kc, 8), kc), :] = f_ref[...]
    row = lax.broadcasted_iota(jnp.int32, (128, 64), 0)
    col = lax.broadcasted_iota(jnp.int32, (128, 64), 1)
    for core in range(2):
        there = col == 8 * (row // 16) + 4 * core + row % 4
        for q in range(4):
            pick = there & (row // 4 % 4 == q)
            picks[core, q] = jnp.where(pick, 1.0, 0.0).astype(jnp.bfloat16)
    first = pl.multiple_of(c * half + (xl * 2 + z // 4) * (nn // 8), nn // 8)
    lab = lab_ref[pl.ds(first, nn // 8), :].astype(jnp.float32).T
    for h in range(2):
        for i, of in enumerate((2 * h, 2 * h + 1, NY + 2 * h, NY + 2 * h + 1)):
            lab_t[h, i * kw:(i + 1) * kw, :] = lab[of * kw:(of + 1) * kw, :]
    for b in range(nf // 128):
        column = jnp.broadcast_to(0.5 * ph_ref[b:b + 1, :], (128, 128)).T
        for n in range(nn // 128):
            ang[128 * b:128 * b + 128, 128 * n:128 * n + 128] = column

    near_piece = e_piece(z, 1 - xl)
    for q in range(2):
        part_q = slice(q * quarter, (q + 1) * quarter)
        bytes_of(e_raw.at[1, :, part_q], eq_r.at[1, q])
        bytes_of(e_raw.at[2, :, part_q], eq_r.at[2, q])
        lanes_q = pl.ds(pl.multiple_of(c * half + q * quarter, quarter), quarter)
        e_all[e_rows(z, 1 - xl), lanes_q] = join(e_raw[1, :, part_q], e_raw[2, :, part_q])
        near_q = e_far_piece(z, 1 - xl, q)
        put(near_q, near_q, en_s.at[0, q], er_r.at[0, 1, 0], z_up)
        put(near_q, near_q, en_s.at[1, q], er_r.at[1, 1, 0], z_down)
    put(near_piece, near_piece, ep_s.at[1, 0], ep_r.at[0], partner)

    def e_step(direction, o, s):
        dz = (NZ - s) if direction == 0 else s
        z_ = lax.rem(z + dz, NZ)
        xl_ = (1 - xl) if o else xl
        piece = e_piece(z_, xl_)
        bytes_of(piece, er_r.at[direction, o, s - 1])
        on = piece if s < 3 else e_far_piece(z_, xl_, direction)
        put(on, on, er_s.at[direction, o, s], er_r.at[direction, o, s], z_up if direction == 0 else z_down)
        put(piece, piece, ep_s.at[o, dz], ep_r.at[dz], partner)

    def e_far(direction, o):
        z_ = lax.rem(z + 4, NZ)
        xl_ = (1 - xl) if o else xl
        piece = e_far_piece(z_, xl_, direction)
        bytes_of(piece, er_r.at[direction, o, 3])
        put(piece, piece, ep_s.at[o, 4 + 4 * direction], ep_r.at[4], partner)

    def e_prep(dz, lanes):
        z_ = lax.rem(z + dz, NZ)
        x = 0.5 * e_all[pl.ds(pl.multiple_of(z_ * kc, 16), kc), lanes]
        hi = x.astype(jnp.bfloat16)
        e3[z_, 0:kc, lanes] = hi
        e3[z_, kc:2 * kc, lanes] = (x - hi.astype(jnp.float32)).astype(jnp.bfloat16)
        e3[z_, 2 * kc:3 * kc, lanes] = hi

    def e_other(dz):
        z_ = lax.rem(z + dz, NZ)
        bytes_of(e_all.at[pl.ds(pl.multiple_of(z_ * kc, 16), kc), lanes_o], ep_r.at[dz])
        e_prep(dz, lanes_o)

    def f_prep(u, dy):
        j = clip_of(u, dy)
        x = f_all[pl.ds(pl.multiple_of(j * kc, 16), kc), :]
        hi = x.astype(jnp.bfloat16)
        lo = (x - hi.astype(jnp.float32)).astype(jnp.bfloat16)
        f3[j] = jnp.concatenate([hi, hi, lo], axis=0).T

    def f_wait(direction, u, k, clip_, lo, hi):
        bytes_of(f_block(clip_, lo, hi), fy_r.at[direction, u, k])

    dot = functools.partial(jnp.dot, preferred_element_type=jnp.float32)

    LAST = 9
    far = lax.rem(z + 4, NZ)
    beside = jnp.where(far == clip_of(1, 2), clip_of(1, 1), clip_of(1, 2))

    def stage_of(j):
        up = lax.rem(j - z + NZ, NZ)
        e_turn = jnp.minimum(up, NZ - up)
        e_turn = e_turn + e_turn // 3
        right = lax.rem(lax.rem(j, NY) - y + NY, NY)
        away = jnp.minimum(right, NY - right)
        f_turn = jnp.where(j // NY == xh, away, 2 + away)
        return jnp.where(j == beside, LAST, jnp.maximum(e_turn, f_turn))

    def products(stage, first, count):
        @pl.loop(0, count)
        def _(i):
            j = lax.rem(xh * NY + first + i, 2 * NY)

            @pl.when(stage_of(j) == stage)
            def _():
                ang[...] = ang[...] + dot(f3[j], e3[j])

    e_step(0, 0, 1)
    e_step(1, 0, 1)
    greeted(1)
    greet(2)
    f_wait(0, 0, 0, clip_of(0, 3), 0, mid)
    f_send(0, 0, 2, clip_of(0, 3), 0, mid)
    f_wait(1, 0, 0, clip_of(0, 1), mid, kc)
    f_send(1, 0, 2, clip_of(0, 1), mid, kc)
    bytes_of(f_rel.at[cut:kc, :], fx_r.at[1])
    put(f_rel.at[cut:kc, :], f_block(clip_of(1, 0), cut, kc), fx_s.at[3], fx_r.at[3], x_near)
    bytes_of(f_rel.at[0:cut, :], fx_r.at[0])
    put(f_rel.at[0:cut, :], f_block(clip, 0, cut), fx_s.at[2], fx_r.at[2], x_cross)
    e_prep(0, lanes_c)
    f_prep(0, 0)
    e_other(0)
    products(0, 0, 8)
    e_step(0, 1, 1)
    e_step(1, 1, 1)
    e_prep(1, lanes_c)
    e_prep(7, lanes_c)
    f_wait(0, 0, 1, clip_of(0, 3), mid, kc)
    f_wait(1, 0, 1, clip_of(0, 1), 0, mid)
    f_prep(0, 1)
    f_prep(0, 3)
    over = clip_of(1, 0)
    bytes_of(f_block(over, 0, cut), fx_r.at[2])
    f_send(0, 1, 0, over, 0, cut)
    f_send(1, 1, 0, over, 0, cut)
    e_step(0, 0, 2)
    e_step(1, 0, 2)
    e_other(1)
    e_other(7)
    bytes_of(f_block(over, cut, kc), fx_r.at[3])
    f_send(0, 1, 1, over, cut, mid)
    f_send(1, 1, 1, over, mid, kc)
    f_send(0, 1, 2, over, mid, kc)
    f_send(1, 1, 2, over, cut, mid)
    products(1, 0, 4)
    e_step(0, 1, 2)
    e_step(1, 1, 2)
    products(1, 4, 4)
    e_prep(2, lanes_c)
    e_prep(6, lanes_c)
    f_wait(0, 0, 2, clip_of(0, 2), 0, mid)
    f_wait(1, 0, 2, clip_of(0, 2), mid, kc)
    f_prep(0, 2)
    f_prep(1, 0)
    e_other(2)
    e_other(6)
    e_step(0, 0, 3)
    e_step(1, 0, 3)
    f_wait(0, 1, 0, clip_of(1, 3), 0, cut)
    f_wait(0, 1, 1, clip_of(1, 3), cut, mid)
    f_send(0, 1, 3, clip_of(1, 3), 0, mid)
    f_wait(1, 1, 0, clip_of(1, 1), 0, cut)
    f_wait(1, 1, 1, clip_of(1, 1), mid, kc)
    f_send(1, 1, 3, clip_of(1, 1), mid, kc)
    greeted(2)
    for u, dy in clip_offsets:
        send_w(u, dy)
    products(2, 0, 8)
    e_step(0, 1, 3)
    e_step(1, 1, 3)
    f_wait(0, 1, 2, clip_of(1, 3), mid, kc)
    f_wait(1, 1, 2, clip_of(1, 1), cut, mid)
    f_prep(1, 1)
    f_prep(1, 3)
    products(3, 4, 4)
    e_prep(3, lanes_c)
    e_prep(5, lanes_c)
    e_far(0, 0)
    e_far(1, 0)
    e_other(3)
    e_other(5)
    products(4, 0, 4)
    e_far(0, 1)
    e_far(1, 1)
    e_prep(4, lanes_c)
    products(4, 4, 4)
    f_wait(0, 1, 3, clip_of(1, 2), 0, mid)
    f_wait(1, 1, 3, clip_of(1, 2), mid, kc)
    f_prep(1, 2)
    e_other(4)

    for n in range(nn // 256):
        cols = slice(256 * n, 256 * n + 256)
        x = ang[:, cols] + dot(f3[beside], e3[beside, :, cols]) + dot(f3[far], e3[far, :, cols])
        phi[:, cols] = scaled_cos_of_twice(x, scale).astype(jnp.bfloat16)

    hk = w_t.shape[1] // 2
    block = nn // 8
    chains = range(2)

    def chain_rows(h):
        return slice(h * hk, (h + 1) * hk)

    def block_rows(z_):
        return pl.ds(pl.multiple_of(lax.rem(z_, 4) * 16, 16), 16)

    def block_lanes(z_, xl_, core=None):
        lane = (xl_ * 2 + z_ // 4) * block
        if core is not None:
            lane = lane + core * half
        return pl.ds(pl.multiple_of(lane, block), block)

    nt = functools.partial(
        lax.dot_general, dimension_numbers=(((1,), (1,)), ((), ())), preferred_element_type=jnp.float32)

    def wait_w(t, h):
        for own, count in ((True, 3), (False, 4)):
            @pl.when((my_chain == h) == own)
            def _():
                bytes_of(g_recv.at[0, 0:count], w_r.at[t, h])

    def start_logits(t, h):
        w = w_t[t, chain_rows(h), :]
        c_send[t, h] = dot(w, phi[:, lanes_o]).astype(jnp.bfloat16)
        put(c_send.at[t, h], c_recv.at[t, h], c_s.at[t, h], c_r.at[t, h], partner)
        part[h] = dot(w, phi[:, lanes_c])

    def share_logits(t, h):
        bytes_of(c_recv.at[t, h], c_r.at[t, h])
        total = part[h] + c_recv[t, h].astype(jnp.float32)
        part[h] = total
        l_send[t, h] = total.astype(jnp.bfloat16)
        for dz, dx in feat_offsets:
            pz, px = feat_peer(dz, dx)
            put(l_send.at[t, h, block_rows(pz), block_lanes(pz, px)], l_recv.at[t, h, dx * NZ + dz - 1],
                l_s.at[t, h], l_r.at[t, h], (clip, feat_of(pz, px, c)), False)

    bytes_of(g_recv.at[0], w_r.at[0, 0])
    out = dot(w_t[0], phi[:, lanes_o]).astype(jnp.bfloat16)
    for h in chains:
        c_send[0, h] = out[chain_rows(h), :]
        put(c_send.at[0, h], c_recv.at[0, h], c_s.at[0, h], c_r.at[0, h], partner)
    out = dot(w_t[0], phi[:, lanes_c])
    for h in chains:
        part[h] = out[chain_rows(h), :]
    for t in range(STEPS):
        for h in chains:
            if t > 0:
                wait_w(t, h)
                start_logits(t, h)
            share_logits(t, h)
        for h in chains:
            acc = part[h, block_rows(z), block_lanes(z, xl)]
            bytes_of(l_recv.at[t, h], l_r.at[t, h])
            for i in range(2 * NZ - 1):
                acc = acc + l_recv[t, h, i].astype(jnp.float32)
            labels = lab_t[h, block_rows(z), :]
            r_t[t, h, block_rows(z), block_lanes(z, xl, c)] = (jax.nn.sigmoid(acc) - labels).astype(jnp.bfloat16)
            mine_r = r_t.at[t, h, block_rows(z), block_lanes(z, xl, c)]
            for dz, dx in feat_offsets:
                pz, px = feat_peer(dz, dx)
                put(mine_r, mine_r, r_s.at[t, h], r_r.at[t, h], (clip, feat_of(pz, px, c)), False)
        for h in chains:
            bytes_of(l_recv.at[t, h], r_r.at[t, h])
            half_r = r_t.at[t, h, :, lanes_c]
            put(half_r, half_r, rc_s.at[t, h], rc_r.at[t, h], partner)
            grad[h] = nt(r_t[t, h, :, lanes_c], phi[:, lanes_c])
            bytes_of(r_t.at[t, h, :, lanes_o], rc_r.at[t, h])
            total = grad[h] + nt(r_t[t, h, :, lanes_o], phi[:, lanes_o])
            grad[h] = total
            g_send[t, h] = total.astype(jnp.bfloat16)

            def send_g(u, yo):
                to = clip_of(u, yo - y + NY)
                rows = pl.ds(pl.multiple_of(local_block(to) * kw, kw), kw)
                slot = u * NY + lax.rem(yo - y + NY, NY) - 1
                put(g_send.at[t, h, rows, :], g_recv.at[t, slot], g_s.at[t, h], g_r.at[t], (to, feat), False)

            for yo in (2 * h, 2 * h + 1):
                send_g(1, yo)

                @pl.when(yo != y)
                def _():
                    send_g(0, yo)
        for h in chains:
            @pl.when(my_chain == h)
            def _():
                g = grad[h, pl.ds(pl.multiple_of(local_block(clip) * kw, kw), kw), :]
                bytes_of(g_recv.at[t], g_r.at[t])
                for i in range(7):
                    g = g + g_recv[t, i].astype(jnp.float32)
                w_new = w_own[...] - 0.25 * g
                w_own[...] = w_new
                w_half = w_new.astype(jnp.bfloat16)
                w_send[t + 1] = w_half
                w_t[t + 1, my_rows, :] = w_half
                for u, dy in clip_offsets:
                    put(w_send.at[t + 1], w_t.at[t + 1, my_rows, :], w_s.at[t + 1], w_r.at[t + 1, h],
                        (clip_of(u, dy), feat), False)
    tr_ref[...] = w_own[...]

    t = STEPS

    def chip_blocks(h, core):
        out = dot(picks[core, 0], logits[h, :, 0:quarter])
        for q in range(1, 4):
            out = out + dot(picks[core, q], logits[h, :, q * quarter:(q + 1) * quarter])
        return out

    def chip_rows(z_, xl_):
        return pl.ds(pl.multiple_of((2 * local_block(z_) + xl_) * 16, 16), 16)

    z_chain = lax.rem(z, 4) // 2
    for h in chains:
        wait_w(t, h)
        logits[h] = dot(w_t[t, chain_rows(h), :], phi[...]).astype(jnp.bfloat16)
        s_out[h] = chip_blocks(h, 1 - c).astype(jnp.bfloat16)
        put(s_out.at[h], s_in.at[h], c_s.at[t, h], c_r.at[t, h], partner)
        s_own[h] = chip_blocks(h, c)
        bytes_of(s_in.at[h], c_r.at[t, h])
        total = s_own[h] + s_in[h].astype(jnp.float32)
        s_own[h] = total
        s_sum[h] = total.astype(jnp.bfloat16)

        def send_s(pz, dx):
            px = 1 - xl if dx else xl
            slot = dx * NZ + lax.rem(pz - z + NZ, NZ) - 1
            put(s_sum.at[h, chip_rows(pz, px), :], s_recv.at[slot], l_s.at[t, h], l_r.at[t, 0], (clip, feat_of(pz, px, c)), False)

        for pz in (2 * h, 2 * h + 1, NY + 2 * h, NY + 2 * h + 1):
            send_s(pz, 1)

            @pl.when(pz != z)
            def _():
                send_s(pz, 0)
    acc = s_own[z_chain, chip_rows(z, xl), :]
    bytes_of(s_recv, l_r.at[t, 0])
    for i in range(2 * NZ - 1):
        acc = acc + s_recv[i].astype(jnp.float32)
    for q in range(4):
        sc_ref[:, q * quarter:(q + 1) * quarter] = acc[4 * q:4 * q + 4, :]

    for copy in sends:
        copy.wait_send()
    for t in range(STEPS + 1):
        bytes_of(g_recv.at[0], w_s.at[t])
    for h in chains:
        for t in range(STEPS):
            bytes_of(l_recv.at[0, 0], l_s.at[t, h])
            bytes_of(l_recv.at[0, 0], r_s.at[t, h])
        for own, count in ((True, 3), (False, 4)):
            @pl.when((my_chain == h) == own)
            def _():
                for t in range(STEPS):
                    bytes_of(g_recv.at[0, 0:count], g_s.at[t, h])
        for own, count in ((True, 7), (False, 8)):
            @pl.when((z_chain == h) == own)
            def _():
                bytes_of(s_recv.at[0:count], l_s.at[STEPS, h])


def per_device(embeds, frequencies, phases, weights, labels):
    nn, ke = embeds.shape
    kc, nf = frequencies.shape
    kw = weights.shape[1]
    kk = labels.shape[1]
    kt = kc * lax.axis_size("clip")
    total_features = nf * lax.axis_size("feat")
    scale = math.sqrt(2.0 / total_features)
    f32, b16 = jnp.float32, jnp.bfloat16
    dma = pltpu.SemaphoreType.DMA
    hbm = pl.BlockSpec(memory_space=pl.ANY)
    vmem = pl.BlockSpec(memory_space=pltpu.VMEM)
    half, quarter = nn // 2, nn // 4
    steps = STEPS + 1
    scratch = [
        pltpu.VMEM((ke, nn), f32),
        pltpu.VMEM((kc, nf), f32),
        pltpu.VMEM((nf // 128, 128), f32),
        pltpu.VMEM((kw, nf), f32),
        pltpu.VMEM((nn, kk), jnp.int32),
        pltpu.VMEM((2, 4, 128, 64), b16),
        pltpu.VMEM((kt, nn), f32),
        pltpu.VMEM((kt, nf), f32),
        pltpu.VMEM((3, ke, half), f32),
        pltpu.VMEM((2 * ke, half), f32),
        pltpu.VMEM((kc, nf), f32),
        pltpu.VMEM((8, 3 * kc, nn), b16),
        pltpu.VMEM((8, nf, 3 * kc), b16),
        pltpu.VMEM((nf, nn), f32),
        pltpu.VMEM((nf, nn), b16),
        pltpu.VMEM((2, kk // 2, nn // 8), f32),
        pltpu.VMEM((kw, nf), f32),
        pltpu.VMEM((steps, kw, nf), b16),
        pltpu.VMEM((steps, kk, nf), b16),
        pltpu.VMEM((2, kk // 2, half), f32),
        pltpu.VMEM((STEPS, 2, kk // 2, half), b16),
        pltpu.VMEM((STEPS, 2, kk // 2, half), b16),
        pltpu.VMEM((STEPS, 2, kk // 2, half), b16),
        pltpu.VMEM((STEPS, 2, 2 * NZ - 1, 16, nn // 8), b16),
        pltpu.VMEM((STEPS, 2, kk // 2, nn), b16),
        pltpu.VMEM((2, kk // 2, nf), f32),
        pltpu.VMEM((STEPS, 2, kk // 2, nf), b16),
        pltpu.VMEM((STEPS, 7, kw, nf), b16),
        pltpu.VMEM((2, kk // 2, nn), b16),
        pltpu.VMEM((2, 128, quarter), b16),
        pltpu.VMEM((2, 128, quarter), b16),
        pltpu.VMEM((2, 128, quarter), f32),
        pltpu.VMEM((2, 128, quarter), b16),
        pltpu.VMEM((2 * NZ - 1, 16, quarter), b16),
        dma((3, 2)), dma((3, 2)), dma((2, 2)), dma((2, 2, 4)), dma((2, 2, 4)), dma((2, NZ + 1)), dma((NZ,)),
        dma((4,)), dma((4,)), dma((2, 2, 4)), dma((2, 2, 4)),
        dma((steps,)), dma((steps, 2)), dma((steps, 2)), dma((steps, 2)), dma((steps, 2)), dma((steps, 2)),
        dma((STEPS, 2)), dma((STEPS, 2)), dma((STEPS, 2)), dma((STEPS, 2)), dma((STEPS, 2)), dma((STEPS,)),
        dma((5,)), pltpu.SemaphoreType.REGULAR((3,)),
    ]
    trained_t, scores_t = pl.pallas_call(
        functools.partial(kernel, scale),
        out_shape=(pltpu.VMEM((kw, nf), f32), pltpu.VMEM((4, nn), f32)),
        in_specs=[hbm] * 5,
        out_specs=(vmem, vmem),
        scratch_shapes=scratch,
        compiler_params=pltpu.CompilerParams(
            collective_id=0, has_side_effects=True, vmem_limit_bytes=60 * 1024 * 1024),
    )(embeds.T, frequencies, phases.reshape(nf // 128, 128), weights.T, labels)
    return trained_t.T, scores_t.T


def solution(mesh):
    placed = (P("clip", "feat"), P("clip", "feat"), P("feat"), P("feat", "clip"), P("clip", None))
    return jax.shard_map(
        per_device,
        mesh=mesh,
        in_specs=placed,
        out_specs=(P("feat", "clip"), P("clip", "feat")),
        check_vma=False,
    )
```

```python
import functools
import math

import jax
import jax.numpy as jnp
from jax import lax
from jax.experimental import pallas as pl
from jax.experimental.pallas import tpu as pltpu
from jax.sharding import PartitionSpec as P

STEPS = 2
MESH = pl.DeviceIdType.MESH

NY = 4
NZ = 8

PI_A = 3.1416015625
PI_B = -8.90890987648163e-06
SIN = (9.99999976e-01, -1.66666473e-01, 8.33289467e-03, -1.98005800e-04, 2.58984559e-06)


def scaled_cos_of_twice(h, scale):
    q = jnp.round(h * (1.0 / math.pi))
    w = (h - q * PI_A) - q * PI_B
    w2 = w * w
    root = math.sqrt(2.0 * scale)
    p = root * SIN[4]
    for c in SIN[3::-1]:
        p = p * w2 + root * c
    s = w * p
    return scale - s * s


def bytes_of(ref, sem):
    pltpu.make_async_copy(ref, ref, sem).wait()


def kernel(
    scale,
    e_hbm, f_hbm, ph_hbm, w_hbm, lab_hbm,
    tr_ref, sc_ref,
    e_ref, f_ref, ph_ref, w_ref, lab_ref, picks,
    e_all, f_all, e_raw, e_two, f_rel,
    e3, f3, ang, phi, lab_t,
    w_own, w_send, w_t,
    part, c_send, c_recv, l_send, l_recv, r_t,
    grad, g_send, g_recv, logits, s_out, s_in, s_own, s_sum, s_recv,
    eq_s, eq_r, en_s, er_s, er_r, ep_s, ep_r,
    fx_s, fx_r, fy_s, fy_r,
    w_s, w_r, c_s, c_r, l_s, l_r, r_s, r_r, rc_s, rc_r, g_s, g_r,
    in_s, hello,
):
    loads = [
        pltpu.make_async_copy(src, dst, in_s.at[i])
        for i, (src, dst) in enumerate(
            ((e_hbm, e_ref), (f_hbm, f_ref), (w_hbm, w_ref), (ph_hbm, ph_ref), (lab_hbm, lab_ref)))
    ]
    for load in loads:
        load.start()

    clip = lax.axis_index("clip")
    feat = lax.axis_index("feat")
    c = lax.rem(feat, 2)
    xl = lax.rem(feat // 2, 2)
    z = feat // 4
    y = lax.rem(clip, NY)
    xh = clip // NY

    ke = e_ref.shape[0]
    kc = 4 * ke
    nf = f_ref.shape[1]
    nn = e_ref.shape[1]
    half = nn // 2
    quarter = nn // 4
    kw = w_ref.shape[0]

    def feat_of(z_, xl_, c_):
        return (z_ * 2 + xl_) * 2 + c_

    def clip_of(u, dy):
        return ((1 - xh) if u else xh) * NY + lax.rem(y + dy, NY)

    partner = (clip, feat_of(z, xl, 1 - c))
    x_near = (clip, feat_of(z, 1 - xl, c))
    diag = (clip, feat_of(z, 1 - xl, 1 - c))
    x_cross = (clip_of(1, 0), feat_of(z, 1 - xl, c))
    y_right = (clip_of(0, 1), feat)
    y_left = (clip_of(0, NY - 1), feat)
    z_up = (clip, feat_of(lax.rem(z + 1, NZ), xl, c))
    z_down = (clip, feat_of(lax.rem(z + NZ - 1, NZ), xl, c))

    def feat_peer(dz, dx):
        return lax.rem(z + dz, NZ), (1 - xl if dx else xl)

    feat_offsets = [(dz, dx) for dz in (4, 3, 5, 2, 6, 1, 7, 0) for dx in (1, 0) if (dz, dx) != (0, 0)]
    clip_offsets = [(u, dy) for dy in (2, 1, 3, 0) for u in (1, 0) if (u, dy) != (0, 0)]

    barrier = pltpu.get_barrier_semaphore()
    neighbours = [partner, x_near, x_cross, diag, z_up, z_down, y_right, y_left]
    for peer in neighbours:
        pl.semaphore_signal(barrier, inc=1, device_id=peer, device_id_type=MESH)

    def local_block(clip_):
        return clip_ // NY * 2 + lax.rem(clip_, 2)

    my_chain = y // 2
    my_rows = pl.ds(pl.multiple_of(my_chain * 4 * kw + local_block(clip) * kw, kw), kw)
    for load in loads[0:3]:
        load.wait()
    w_own[...] = w_ref[...]
    w_send[0] = w_ref[...].astype(jnp.bfloat16)
    w_t[0, my_rows, :] = w_ref[...].astype(jnp.bfloat16)

    pl.semaphore_wait(barrier, len(neighbours))

    def greet(n):
        for peer in (x_near, x_cross, y_right, y_left):
            pl.semaphore_signal(hello.at[n], inc=1, device_id=peer, device_id_type=MESH)

    def greeted(n):
        pl.semaphore_wait(hello.at[n], 4)

    greet(0)
    sends = []

    def put(src, dst, s_sem, r_sem, to, own_sem=True):
        copy = pltpu.make_async_remote_copy(
            src_ref=src, dst_ref=dst, send_sem=s_sem, recv_sem=r_sem, device_id=to, device_id_type=MESH)
        copy.start()
        if own_sem:
            sends.append(copy)

    lanes_c = pl.ds(pl.multiple_of(c * half, half), half)
    lanes_o = pl.ds(pl.multiple_of((1 - c) * half, half), half)

    def e_rows(z_, xl_):
        return pl.ds(pl.multiple_of(z_ * kc + xl_ * (2 * ke), 8), 2 * ke)

    def e_piece(z_, xl_):
        return e_all.at[e_rows(z_, xl_), lanes_c]

    def e_far_piece(z_, xl_, direction):
        lane = pl.multiple_of(c * half + direction * quarter, quarter)
        return e_all.at[e_rows(z_, xl_), pl.ds(lane, quarter)]

    def f_block(clip_, lo, hi):
        return f_all.at[pl.ds(pl.multiple_of(clip_ * kc + lo, 8), hi - lo), :]

    def send_w(u, dy):
        put(w_send.at[0], w_t.at[0, my_rows, :], w_s.at[0], w_r.at[0, 0], (clip_of(u, dy), feat), False)

    put(e_ref.at[:, lanes_o], e_raw.at[0], eq_s.at[0, 0], eq_r.at[0, 0], partner)
    for q in range(2):
        part_q = slice(q * quarter, (q + 1) * quarter)
        for i, core, to in ((1, c, x_near), (2, 1 - c, diag)):
            lanes_q = pl.ds(pl.multiple_of(core * half + q * quarter, quarter), quarter)
            put(e_ref.at[:, lanes_q], e_raw.at[i, :, part_q], eq_s.at[i, q], eq_r.at[i, q], to)

    cut = kc // 3
    mid = kc // 2
    put(f_ref.at[cut:kc, :], f_rel.at[cut:kc, :], fx_s.at[1], fx_r.at[1], x_cross)
    put(f_ref.at[0:cut, :], f_rel.at[0:cut, :], fx_s.at[0], fx_r.at[0], x_near)
    lows = (0, mid)

    def f_send(direction, u, k, clip_, lo, hi, src=None):
        dst = f_block(clip_, lo, hi)
        put(dst if src is None else src, dst, fy_s.at[direction, u, k], fy_r.at[direction, u, k],
            y_right if direction == 0 else y_left)

    for k in (0, 1):
        for direction in (0, 1):
            lo = lows[k ^ direction]
            f_send(direction, 0, k, clip, lo, lo + mid, f_ref.at[lo:lo + mid, :])
    def join(own, oth):
        first = c == 0
        lanes = own.shape[1]
        e_two[0:ke, 0:lanes] = jnp.where(first, own, oth)
        e_two[ke:2 * ke, 0:lanes] = jnp.where(first, oth, own)
        return e_two[:, 0:lanes]

    bytes_of(e_raw.at[0], eq_r.at[0, 0])
    e_all[e_rows(z, xl), lanes_c] = join(e_ref[:, lanes_c], e_raw[0])
    own_piece = e_piece(z, xl)
    put(own_piece, own_piece, er_s.at[0, 0, 0], er_r.at[0, 0, 0], z_up)
    put(own_piece, own_piece, er_s.at[1, 0, 0], er_r.at[1, 0, 0], z_down)
    put(own_piece, own_piece, ep_s.at[0, 0], ep_r.at[0], partner)

    greeted(0)
    greet(1)
    for load in loads[3:]:
        load.wait()
    f_all[pl.ds(pl.multiple_of(clip * kc, 8), kc), :] = f_ref[...]
    row = lax.broadcasted_iota(jnp.int32, (128, 64), 0)
    col = lax.broadcasted_iota(jnp.int32, (128, 64), 1)
    for core in range(2):
        there = col == 8 * (row // 16) + 4 * core + row % 4
        for q in range(4):
            pick = there & (row // 4 % 4 == q)
            picks[core, q] = jnp.where(pick, 1.0, 0.0).astype(jnp.bfloat16)
    first = pl.multiple_of(c * half + (xl * 2 + z // 4) * (nn // 8), nn // 8)
    lab = lab_ref[pl.ds(first, nn // 8), :].astype(jnp.float32).T
    for h in range(2):
        for i, of in enumerate((2 * h, 2 * h + 1, NY + 2 * h, NY + 2 * h + 1)):
            lab_t[h, i * kw:(i + 1) * kw, :] = lab[of * kw:(of + 1) * kw, :]
    for b in range(nf // 128):
        column = jnp.broadcast_to(0.5 * ph_ref[b:b + 1, :], (128, 128)).T
        for n in range(nn // 128):
            ang[128 * b:128 * b + 128, 128 * n:128 * n + 128] = column

    near_piece = e_piece(z, 1 - xl)
    for q in range(2):
        part_q = slice(q * quarter, (q + 1) * quarter)
        bytes_of(e_raw.at[1, :, part_q], eq_r.at[1, q])
        bytes_of(e_raw.at[2, :, part_q], eq_r.at[2, q])
        lanes_q = pl.ds(pl.multiple_of(c * half + q * quarter, quarter), quarter)
        e_all[e_rows(z, 1 - xl), lanes_q] = join(e_raw[1, :, part_q], e_raw[2, :, part_q])
        near_q = e_far_piece(z, 1 - xl, q)
        put(near_q, near_q, en_s.at[0, q], er_r.at[0, 1, 0], z_up)
        put(near_q, near_q, en_s.at[1, q], er_r.at[1, 1, 0], z_down)
    put(near_piece, near_piece, ep_s.at[1, 0], ep_r.at[0], partner)

    def e_step(direction, o, s):
        dz = (NZ - s) if direction == 0 else s
        z_ = lax.rem(z + dz, NZ)
        xl_ = (1 - xl) if o else xl
        piece = e_piece(z_, xl_)
        bytes_of(piece, er_r.at[direction, o, s - 1])
        on = piece if s < 3 else e_far_piece(z_, xl_, direction)
        put(on, on, er_s.at[direction, o, s], er_r.at[direction, o, s], z_up if direction == 0 else z_down)
        put(piece, piece, ep_s.at[o, dz], ep_r.at[dz], partner)

    def e_far(direction, o):
        z_ = lax.rem(z + 4, NZ)
        xl_ = (1 - xl) if o else xl
        piece = e_far_piece(z_, xl_, direction)
        bytes_of(piece, er_r.at[direction, o, 3])
        put(piece, piece, ep_s.at[o, 4 + 4 * direction], ep_r.at[4], partner)

    def e_prep(dz, lanes):
        z_ = lax.rem(z + dz, NZ)
        x = 0.5 * e_all[pl.ds(pl.multiple_of(z_ * kc, 16), kc), lanes]
        hi = x.astype(jnp.bfloat16)
        e3[z_, 0:kc, lanes] = hi
        e3[z_, kc:2 * kc, lanes] = (x - hi.astype(jnp.float32)).astype(jnp.bfloat16)
        e3[z_, 2 * kc:3 * kc, lanes] = hi

    def e_other(dz):
        z_ = lax.rem(z + dz, NZ)
        bytes_of(e_all.at[pl.ds(pl.multiple_of(z_ * kc, 16), kc), lanes_o], ep_r.at[dz])
        e_prep(dz, lanes_o)

    def f_prep(u, dy):
        j = clip_of(u, dy)
        x = f_all[pl.ds(pl.multiple_of(j * kc, 16), kc), :]
        hi = x.astype(jnp.bfloat16)
        lo = (x - hi.astype(jnp.float32)).astype(jnp.bfloat16)
        f3[j] = jnp.concatenate([hi, hi, lo], axis=0).T

    def f_wait(direction, u, k, clip_, lo, hi):
        bytes_of(f_block(clip_, lo, hi), fy_r.at[direction, u, k])

    dot = functools.partial(jnp.dot, preferred_element_type=jnp.float32)

    LAST = 9
    far = lax.rem(z + 4, NZ)
    beside = jnp.where(far == clip_of(1, 2), clip_of(1, 1), clip_of(1, 2))

    def stage_of(j):
        up = lax.rem(j - z + NZ, NZ)
        e_turn = jnp.minimum(up, NZ - up)
        e_turn = e_turn + e_turn // 3
        right = lax.rem(lax.rem(j, NY) - y + NY, NY)
        away = jnp.minimum(right, NY - right)
        f_turn = jnp.where(j // NY == xh, away, 2 + away)
        return jnp.where(j == beside, LAST, jnp.maximum(e_turn, f_turn))

    def products(stage, first, count):
        @pl.loop(0, count)
        def _(i):
            j = lax.rem(xh * NY + first + i, 2 * NY)

            @pl.when(stage_of(j) == stage)
            def _():
                ang[...] = ang[...] + dot(f3[j], e3[j])

    e_step(0, 0, 1)
    e_step(1, 0, 1)
    greeted(1)
    greet(2)
    f_wait(0, 0, 0, clip_of(0, 3), 0, mid)
    f_send(0, 0, 2, clip_of(0, 3), 0, mid)
    f_wait(1, 0, 0, clip_of(0, 1), mid, kc)
    f_send(1, 0, 2, clip_of(0, 1), mid, kc)
    bytes_of(f_rel.at[cut:kc, :], fx_r.at[1])
    put(f_rel.at[cut:kc, :], f_block(clip_of(1, 0), cut, kc), fx_s.at[3], fx_r.at[3], x_near)
    bytes_of(f_rel.at[0:cut, :], fx_r.at[0])
    put(f_rel.at[0:cut, :], f_block(clip, 0, cut), fx_s.at[2], fx_r.at[2], x_cross)
    e_prep(0, lanes_c)
    f_prep(0, 0)
    e_other(0)
    products(0, 0, 8)
    e_step(0, 1, 1)
    e_step(1, 1, 1)
    e_prep(1, lanes_c)
    e_prep(7, lanes_c)
    f_wait(0, 0, 1, clip_of(0, 3), mid, kc)
    f_wait(1, 0, 1, clip_of(0, 1), 0, mid)
    f_prep(0, 1)
    f_prep(0, 3)
    over = clip_of(1, 0)
    bytes_of(f_block(over, 0, cut), fx_r.at[2])
    f_send(0, 1, 0, over, 0, cut)
    f_send(1, 1, 0, over, 0, cut)
    e_step(0, 0, 2)
    e_step(1, 0, 2)
    e_other(1)
    e_other(7)
    bytes_of(f_block(over, cut, kc), fx_r.at[3])
    f_send(0, 1, 1, over, cut, mid)
    f_send(1, 1, 1, over, mid, kc)
    f_send(0, 1, 2, over, mid, kc)
    f_send(1, 1, 2, over, cut, mid)
    products(1, 0, 4)
    e_step(0, 1, 2)
    e_step(1, 1, 2)
    products(1, 4, 4)
    e_prep(2, lanes_c)
    e_prep(6, lanes_c)
    f_wait(0, 0, 2, clip_of(0, 2), 0, mid)
    f_wait(1, 0, 2, clip_of(0, 2), mid, kc)
    f_prep(0, 2)
    f_prep(1, 0)
    e_other(2)
    e_other(6)
    e_step(0, 0, 3)
    e_step(1, 0, 3)
    f_wait(0, 1, 0, clip_of(1, 3), 0, cut)
    f_wait(0, 1, 1, clip_of(1, 3), cut, mid)
    f_send(0, 1, 3, clip_of(1, 3), 0, mid)
    f_wait(1, 1, 0, clip_of(1, 1), 0, cut)
    f_wait(1, 1, 1, clip_of(1, 1), mid, kc)
    f_send(1, 1, 3, clip_of(1, 1), mid, kc)
    greeted(2)
    for u, dy in clip_offsets:
        send_w(u, dy)
    products(2, 0, 8)
    e_step(0, 1, 3)
    e_step(1, 1, 3)
    f_wait(0, 1, 2, clip_of(1, 3), mid, kc)
    f_wait(1, 1, 2, clip_of(1, 1), cut, mid)
    f_prep(1, 1)
    f_prep(1, 3)
    products(3, 4, 4)
    e_prep(3, lanes_c)
    e_prep(5, lanes_c)
    e_far(0, 0)
    e_far(1, 0)
    e_other(3)
    e_other(5)
    products(4, 0, 4)
    e_far(0, 1)
    e_far(1, 1)
    e_prep(4, lanes_c)
    products(4, 4, 4)
    f_wait(0, 1, 3, clip_of(1, 2), 0, mid)
    f_wait(1, 1, 3, clip_of(1, 2), mid, kc)
    f_prep(1, 2)
    ang[...] = ang[...] + dot(f3[beside], e3[beside])
    e_other(4)

    for n in range(nn // 256):
        cols = slice(256 * n, 256 * n + 256)
        x = ang[:, cols] + dot(f3[far], e3[far, :, cols])
        phi[:, cols] = scaled_cos_of_twice(x, scale).astype(jnp.bfloat16)

    hk = w_t.shape[1] // 2
    block = nn // 8
    chains = range(2)

    def chain_rows(h):
        return slice(h * hk, (h + 1) * hk)

    def block_rows(z_):
        return pl.ds(pl.multiple_of(lax.rem(z_, 4) * 16, 16), 16)

    def block_lanes(z_, xl_, core=None):
        lane = (xl_ * 2 + z_ // 4) * block
        if core is not None:
            lane = lane + core * half
        return pl.ds(pl.multiple_of(lane, block), block)

    nt = functools.partial(
        lax.dot_general, dimension_numbers=(((1,), (1,)), ((), ())), preferred_element_type=jnp.float32)

    def wait_w(t, h):
        for own, count in ((True, 3), (False, 4)):
            @pl.when((my_chain == h) == own)
            def _():
                bytes_of(g_recv.at[0, 0:count], w_r.at[t, h])

    def start_logits(t, h):
        w = w_t[t, chain_rows(h), :]
        c_send[t, h] = dot(w, phi[:, lanes_o]).astype(jnp.bfloat16)
        put(c_send.at[t, h], c_recv.at[t, h], c_s.at[t, h], c_r.at[t, h], partner)
        part[h] = dot(w, phi[:, lanes_c])

    def share_logits(t, h):
        bytes_of(c_recv.at[t, h], c_r.at[t, h])
        total = part[h] + c_recv[t, h].astype(jnp.float32)
        part[h] = total
        l_send[t, h] = total.astype(jnp.bfloat16)
        for dz, dx in feat_offsets:
            pz, px = feat_peer(dz, dx)
            put(l_send.at[t, h, block_rows(pz), block_lanes(pz, px)], l_recv.at[t, h, dx * NZ + dz - 1],
                l_s.at[t, h], l_r.at[t, h], (clip, feat_of(pz, px, c)), False)

    bytes_of(g_recv.at[0], w_r.at[0, 0])
    out = dot(w_t[0], phi[:, lanes_o]).astype(jnp.bfloat16)
    for h in chains:
        c_send[0, h] = out[chain_rows(h), :]
        put(c_send.at[0, h], c_recv.at[0, h], c_s.at[0, h], c_r.at[0, h], partner)
    out = dot(w_t[0], phi[:, lanes_c])
    for h in chains:
        part[h] = out[chain_rows(h), :]
    for t in range(STEPS):
        for h in chains:
            if t > 0:
                wait_w(t, h)
                start_logits(t, h)
            share_logits(t, h)
        for h in chains:
            acc = part[h, block_rows(z), block_lanes(z, xl)]
            bytes_of(l_recv.at[t, h], l_r.at[t, h])
            for i in range(2 * NZ - 1):
                acc = acc + l_recv[t, h, i].astype(jnp.float32)
            labels = lab_t[h, block_rows(z), :]
            r_t[t, h, block_rows(z), block_lanes(z, xl, c)] = (jax.nn.sigmoid(acc) - labels).astype(jnp.bfloat16)
            mine_r = r_t.at[t, h, block_rows(z), block_lanes(z, xl, c)]
            for dz, dx in feat_offsets:
                pz, px = feat_peer(dz, dx)
                put(mine_r, mine_r, r_s.at[t, h], r_r.at[t, h], (clip, feat_of(pz, px, c)), False)
        for h in chains:
            bytes_of(l_recv.at[t, h], r_r.at[t, h])
            half_r = r_t.at[t, h, :, lanes_c]
            put(half_r, half_r, rc_s.at[t, h], rc_r.at[t, h], partner)
            grad[h] = nt(r_t[t, h, :, lanes_c], phi[:, lanes_c])
            bytes_of(r_t.at[t, h, :, lanes_o], rc_r.at[t, h])
            total = grad[h] + nt(r_t[t, h, :, lanes_o], phi[:, lanes_o])
            grad[h] = total
            g_send[t, h] = total.astype(jnp.bfloat16)

            def send_g(u, yo):
                to = clip_of(u, yo - y + NY)
                rows = pl.ds(pl.multiple_of(local_block(to) * kw, kw), kw)
                slot = u * NY + lax.rem(yo - y + NY, NY) - 1
                put(g_send.at[t, h, rows, :], g_recv.at[t, slot], g_s.at[t, h], g_r.at[t], (to, feat), False)

            for yo in (2 * h, 2 * h + 1):
                send_g(1, yo)

                @pl.when(yo != y)
                def _():
                    send_g(0, yo)
        for h in chains:
            @pl.when(my_chain == h)
            def _():
                g = grad[h, pl.ds(pl.multiple_of(local_block(clip) * kw, kw), kw), :]
                bytes_of(g_recv.at[t], g_r.at[t])
                for i in range(7):
                    g = g + g_recv[t, i].astype(jnp.float32)
                w_new = w_own[...] - 0.25 * g
                w_own[...] = w_new
                w_half = w_new.astype(jnp.bfloat16)
                w_send[t + 1] = w_half
                w_t[t + 1, my_rows, :] = w_half
                for u, dy in clip_offsets:
                    put(w_send.at[t + 1], w_t.at[t + 1, my_rows, :], w_s.at[t + 1], w_r.at[t + 1, h],
                        (clip_of(u, dy), feat), False)
    tr_ref[...] = w_own[...]

    t = STEPS

    def chip_blocks(h, core):
        out = dot(picks[core, 0], logits[h, :, 0:quarter])
        for q in range(1, 4):
            out = out + dot(picks[core, q], logits[h, :, q * quarter:(q + 1) * quarter])
        return out

    def chip_rows(z_, xl_):
        return pl.ds(pl.multiple_of((2 * local_block(z_) + xl_) * 16, 16), 16)

    z_chain = lax.rem(z, 4) // 2
    for h in chains:
        wait_w(t, h)
        logits[h] = dot(w_t[t, chain_rows(h), :], phi[...]).astype(jnp.bfloat16)
        s_out[h] = chip_blocks(h, 1 - c).astype(jnp.bfloat16)
        put(s_out.at[h], s_in.at[h], c_s.at[t, h], c_r.at[t, h], partner)
        s_own[h] = chip_blocks(h, c)
        bytes_of(s_in.at[h], c_r.at[t, h])
        total = s_own[h] + s_in[h].astype(jnp.float32)
        s_own[h] = total
        s_sum[h] = total.astype(jnp.bfloat16)

        def send_s(pz, dx):
            px = 1 - xl if dx else xl
            slot = dx * NZ + lax.rem(pz - z + NZ, NZ) - 1
            put(s_sum.at[h, chip_rows(pz, px), :], s_recv.at[slot], l_s.at[t, h], l_r.at[t, 0], (clip, feat_of(pz, px, c)), False)

        for pz in (2 * h, 2 * h + 1, NY + 2 * h, NY + 2 * h + 1):
            send_s(pz, 1)

            @pl.when(pz != z)
            def _():
                send_s(pz, 0)
    acc = s_own[z_chain, chip_rows(z, xl), :]
    bytes_of(s_recv, l_r.at[t, 0])
    for i in range(2 * NZ - 1):
        acc = acc + s_recv[i].astype(jnp.float32)
    for q in range(4):
        sc_ref[:, q * quarter:(q + 1) * quarter] = acc[4 * q:4 * q + 4, :]

    for copy in sends:
        copy.wait_send()
    for t in range(STEPS + 1):
        bytes_of(g_recv.at[0], w_s.at[t])
    for h in chains:
        for t in range(STEPS):
            bytes_of(l_recv.at[0, 0], l_s.at[t, h])
            bytes_of(l_recv.at[0, 0], r_s.at[t, h])
        for own, count in ((True, 3), (False, 4)):
            @pl.when((my_chain == h) == own)
            def _():
                for t in range(STEPS):
                    bytes_of(g_recv.at[0, 0:count], g_s.at[t, h])
        for own, count in ((True, 7), (False, 8)):
            @pl.when((z_chain == h) == own)
            def _():
                bytes_of(s_recv.at[0:count], l_s.at[STEPS, h])


def per_device(embeds, frequencies, phases, weights, labels):
    nn, ke = embeds.shape
    kc, nf = frequencies.shape
    kw = weights.shape[1]
    kk = labels.shape[1]
    kt = kc * lax.axis_size("clip")
    total_features = nf * lax.axis_size("feat")
    scale = math.sqrt(2.0 / total_features)
    f32, b16 = jnp.float32, jnp.bfloat16
    dma = pltpu.SemaphoreType.DMA
    hbm = pl.BlockSpec(memory_space=pl.ANY)
    vmem = pl.BlockSpec(memory_space=pltpu.VMEM)
    half, quarter = nn // 2, nn // 4
    steps = STEPS + 1
    scratch = [
        pltpu.VMEM((ke, nn), f32),
        pltpu.VMEM((kc, nf), f32),
        pltpu.VMEM((nf // 128, 128), f32),
        pltpu.VMEM((kw, nf), f32),
        pltpu.VMEM((nn, kk), jnp.int32),
        pltpu.VMEM((2, 4, 128, 64), b16),
        pltpu.VMEM((kt, nn), f32),
        pltpu.VMEM((kt, nf), f32),
        pltpu.VMEM((3, ke, half), f32),
        pltpu.VMEM((2 * ke, half), f32),
        pltpu.VMEM((kc, nf), f32),
        pltpu.VMEM((8, 3 * kc, nn), b16),
        pltpu.VMEM((8, nf, 3 * kc), b16),
        pltpu.VMEM((nf, nn), f32),
        pltpu.VMEM((nf, nn), b16),
        pltpu.VMEM((2, kk // 2, nn // 8), f32),
        pltpu.VMEM((kw, nf), f32),
        pltpu.VMEM((steps, kw, nf), b16),
        pltpu.VMEM((steps, kk, nf), b16),
        pltpu.VMEM((2, kk // 2, half), f32),
        pltpu.VMEM((STEPS, 2, kk // 2, half), b16),
        pltpu.VMEM((STEPS, 2, kk // 2, half), b16),
        pltpu.VMEM((STEPS, 2, kk // 2, half), b16),
        pltpu.VMEM((STEPS, 2, 2 * NZ - 1, 16, nn // 8), b16),
        pltpu.VMEM((STEPS, 2, kk // 2, nn), b16),
        pltpu.VMEM((2, kk // 2, nf), f32),
        pltpu.VMEM((STEPS, 2, kk // 2, nf), b16),
        pltpu.VMEM((STEPS, 7, kw, nf), b16),
        pltpu.VMEM((2, kk // 2, nn), b16),
        pltpu.VMEM((2, 128, quarter), b16),
        pltpu.VMEM((2, 128, quarter), b16),
        pltpu.VMEM((2, 128, quarter), f32),
        pltpu.VMEM((2, 128, quarter), b16),
        pltpu.VMEM((2 * NZ - 1, 16, quarter), b16),
        dma((3, 2)), dma((3, 2)), dma((2, 2)), dma((2, 2, 4)), dma((2, 2, 4)), dma((2, NZ + 1)), dma((NZ,)),
        dma((4,)), dma((4,)), dma((2, 2, 4)), dma((2, 2, 4)),
        dma((steps,)), dma((steps, 2)), dma((steps, 2)), dma((steps, 2)), dma((steps, 2)), dma((steps, 2)),
        dma((STEPS, 2)), dma((STEPS, 2)), dma((STEPS, 2)), dma((STEPS, 2)), dma((STEPS, 2)), dma((STEPS,)),
        dma((5,)), pltpu.SemaphoreType.REGULAR((3,)),
    ]
    trained_t, scores_t = pl.pallas_call(
        functools.partial(kernel, scale),
        out_shape=(pltpu.VMEM((kw, nf), f32), pltpu.VMEM((4, nn), f32)),
        in_specs=[hbm] * 5,
        out_specs=(vmem, vmem),
        scratch_shapes=scratch,
        compiler_params=pltpu.CompilerParams(
            collective_id=0, has_side_effects=True, vmem_limit_bytes=60 * 1024 * 1024),
    )(embeds.T, frequencies, phases.reshape(nf // 128, 128), weights.T, labels)
    return trained_t.T, scores_t.T


def solution(mesh):
    placed = (P("clip", "feat"), P("clip", "feat"), P("feat"), P("feat", "clip"), P("clip", None))
    return jax.shard_map(
        per_device,
        mesh=mesh,
        in_specs=placed,
        out_specs=(P("feat", "clip"), P("clip", "feat")),
        check_vma=False,
    )
```

```python
import functools
import math

import jax
import jax.numpy as jnp
from jax import lax
from jax.experimental import pallas as pl
from jax.experimental.pallas import tpu as pltpu
from jax.sharding import PartitionSpec as P

STEPS = 2
MESH = pl.DeviceIdType.MESH

NY = 4
NZ = 8

PI_A = 3.1416015625
PI_B = -8.90890987648163e-06
SIN = (9.99999976e-01, -1.66666473e-01, 8.33289467e-03, -1.98005800e-04, 2.58984559e-06)


def scaled_cos_of_twice(h, scale):
    q = jnp.round(h * (1.0 / math.pi))
    w = (h - q * PI_A) - q * PI_B
    w2 = w * w
    root = math.sqrt(2.0 * scale)
    p = root * SIN[4]
    for c in SIN[3::-1]:
        p = p * w2 + root * c
    s = w * p
    return scale - s * s


def bytes_of(ref, sem):
    pltpu.make_async_copy(ref, ref, sem).wait()


def kernel(
    scale,
    e_hbm, f_hbm, ph_hbm, w_hbm, lab_hbm,
    tr_ref, sc_ref,
    e_ref, f_ref, ph_ref, w_ref, lab_ref, picks,
    e_all, f_all, e_raw, e_two, f_rel,
    e3, f3, ang, phi, lab_t,
    w_own, w_send, w_t,
    part, c_send, c_recv, l_send, l_recv, r_t,
    grad, g_send, g_recv, logits, s_out, s_in, s_own, s_sum, s_recv,
    eq_s, eq_r, en_s, er_s, er_r, ep_s, ep_r,
    fx_s, fx_r, fy_s, fy_r,
    w_s, w_r, c_s, c_r, l_s, l_r, r_s, r_r, rc_s, rc_r, g_s, g_r,
    in_s, hello,
):
    loads = [
        pltpu.make_async_copy(src, dst, in_s.at[i])
        for i, (src, dst) in enumerate(
            ((e_hbm, e_ref), (f_hbm, f_ref), (w_hbm, w_ref), (ph_hbm, ph_ref), (lab_hbm, lab_ref)))
    ]
    for load in loads:
        load.start()

    clip = lax.axis_index("clip")
    feat = lax.axis_index("feat")
    c = lax.rem(feat, 2)
    xl = lax.rem(feat // 2, 2)
    z = feat // 4
    y = lax.rem(clip, NY)
    xh = clip // NY

    ke = e_ref.shape[0]
    kc = 4 * ke
    nf = f_ref.shape[1]
    nn = e_ref.shape[1]
    half = nn // 2
    quarter = nn // 4
    kw = w_ref.shape[0]

    def feat_of(z_, xl_, c_):
        return (z_ * 2 + xl_) * 2 + c_

    def clip_of(u, dy):
        return ((1 - xh) if u else xh) * NY + lax.rem(y + dy, NY)

    partner = (clip, feat_of(z, xl, 1 - c))
    x_near = (clip, feat_of(z, 1 - xl, c))
    diag = (clip, feat_of(z, 1 - xl, 1 - c))
    x_cross = (clip_of(1, 0), feat_of(z, 1 - xl, c))
    y_right = (clip_of(0, 1), feat)
    y_left = (clip_of(0, NY - 1), feat)
    z_up = (clip, feat_of(lax.rem(z + 1, NZ), xl, c))
    z_down = (clip, feat_of(lax.rem(z + NZ - 1, NZ), xl, c))

    def feat_peer(dz, dx):
        return lax.rem(z + dz, NZ), (1 - xl if dx else xl)

    feat_offsets = [(dz, dx) for dz in (4, 3, 5, 2, 6, 1, 7, 0) for dx in (1, 0) if (dz, dx) != (0, 0)]
    clip_offsets = [(u, dy) for dy in (2, 1, 3, 0) for u in (1, 0) if (u, dy) != (0, 0)]

    barrier = pltpu.get_barrier_semaphore()
    neighbours = [partner, x_near, x_cross, diag, z_up, z_down, y_right, y_left]
    for peer in neighbours:
        pl.semaphore_signal(barrier, inc=1, device_id=peer, device_id_type=MESH)

    def local_block(clip_):
        return clip_ // NY * 2 + lax.rem(clip_, 2)

    my_chain = y // 2
    my_rows = pl.ds(pl.multiple_of(my_chain * 4 * kw + local_block(clip) * kw, kw), kw)
    for load in loads[0:3]:
        load.wait()
    w_own[...] = w_ref[...]
    w_send[0] = w_ref[...].astype(jnp.bfloat16)
    w_t[0, my_rows, :] = w_ref[...].astype(jnp.bfloat16)

    pl.semaphore_wait(barrier, len(neighbours))

    def greet(n):
        for peer in (x_near, x_cross, y_right, y_left):
            pl.semaphore_signal(hello.at[n], inc=1, device_id=peer, device_id_type=MESH)

    def greeted(n):
        pl.semaphore_wait(hello.at[n], 4)

    greet(0)
    sends = []

    def put(src, dst, s_sem, r_sem, to, own_sem=True):
        copy = pltpu.make_async_remote_copy(
            src_ref=src, dst_ref=dst, send_sem=s_sem, recv_sem=r_sem, device_id=to, device_id_type=MESH)
        copy.start()
        if own_sem:
            sends.append(copy)

    lanes_c = pl.ds(pl.multiple_of(c * half, half), half)
    lanes_o = pl.ds(pl.multiple_of((1 - c) * half, half), half)

    def e_rows(z_, xl_):
        return pl.ds(pl.multiple_of(z_ * kc + xl_ * (2 * ke), 8), 2 * ke)

    def e_piece(z_, xl_):
        return e_all.at[e_rows(z_, xl_), lanes_c]

    def e_far_piece(z_, xl_, direction):
        lane = pl.multiple_of(c * half + direction * quarter, quarter)
        return e_all.at[e_rows(z_, xl_), pl.ds(lane, quarter)]

    def f_block(clip_, lo, hi):
        return f_all.at[pl.ds(pl.multiple_of(clip_ * kc + lo, 8), hi - lo), :]

    def send_w(u, dy):
        put(w_send.at[0], w_t.at[0, my_rows, :], w_s.at[0], w_r.at[0, 0], (clip_of(u, dy), feat), False)

    put(e_ref.at[:, lanes_o], e_raw.at[0], eq_s.at[0, 0], eq_r.at[0, 0], partner)
    for q in range(2):
        part_q = slice(q * quarter, (q + 1) * quarter)
        for i, core, to in ((1, c, x_near), (2, 1 - c, diag)):
            lanes_q = pl.ds(pl.multiple_of(core * half + q * quarter, quarter), quarter)
            put(e_ref.at[:, lanes_q], e_raw.at[i, :, part_q], eq_s.at[i, q], eq_r.at[i, q], to)

    cut = kc // 3
    mid = kc // 2
    put(f_ref.at[cut:kc, :], f_rel.at[cut:kc, :], fx_s.at[1], fx_r.at[1], x_cross)
    put(f_ref.at[0:cut, :], f_rel.at[0:cut, :], fx_s.at[0], fx_r.at[0], x_near)
    lows = (0, mid)

    def f_send(direction, u, k, clip_, lo, hi, src=None):
        dst = f_block(clip_, lo, hi)
        put(dst if src is None else src, dst, fy_s.at[direction, u, k], fy_r.at[direction, u, k],
            y_right if direction == 0 else y_left)

    for k in (0, 1):
        for direction in (0, 1):
            lo = lows[k ^ direction]
            f_send(direction, 0, k, clip, lo, lo + mid, f_ref.at[lo:lo + mid, :])
    def join(own, oth):
        first = c == 0
        lanes = own.shape[1]
        e_two[0:ke, 0:lanes] = jnp.where(first, own, oth)
        e_two[ke:2 * ke, 0:lanes] = jnp.where(first, oth, own)
        return e_two[:, 0:lanes]

    bytes_of(e_raw.at[0], eq_r.at[0, 0])
    e_all[e_rows(z, xl), lanes_c] = join(e_ref[:, lanes_c], e_raw[0])
    own_piece = e_piece(z, xl)
    put(own_piece, own_piece, er_s.at[0, 0, 0], er_r.at[0, 0, 0], z_up)
    put(own_piece, own_piece, er_s.at[1, 0, 0], er_r.at[1, 0, 0], z_down)
    put(own_piece, own_piece, ep_s.at[0, 0], ep_r.at[0], partner)

    greeted(0)
    greet(1)
    for load in loads[3:]:
        load.wait()
    f_all[pl.ds(pl.multiple_of(clip * kc, 8), kc), :] = f_ref[...]
    row = lax.broadcasted_iota(jnp.int32, (128, 64), 0)
    col = lax.broadcasted_iota(jnp.int32, (128, 64), 1)
    for core in range(2):
        there = col == 8 * (row // 16) + 4 * core + row % 4
        for q in range(4):
            pick = there & (row // 4 % 4 == q)
            picks[core, q] = jnp.where(pick, 1.0, 0.0).astype(jnp.bfloat16)
    first = pl.multiple_of(c * half + (xl * 2 + z // 4) * (nn // 8), nn // 8)
    lab = lab_ref[pl.ds(first, nn // 8), :].astype(jnp.float32).T
    for h in range(2):
        for i, of in enumerate((2 * h, 2 * h + 1, NY + 2 * h, NY + 2 * h + 1)):
            lab_t[h, i * kw:(i + 1) * kw, :] = lab[of * kw:(of + 1) * kw, :]
    for b in range(nf // 128):
        column = jnp.broadcast_to(0.5 * ph_ref[b:b + 1, :], (128, 128)).T
        for n in range(nn // 128):
            ang[128 * b:128 * b + 128, 128 * n:128 * n + 128] = column

    near_piece = e_piece(z, 1 - xl)
    for q in range(2):
        part_q = slice(q * quarter, (q + 1) * quarter)
        bytes_of(e_raw.at[1, :, part_q], eq_r.at[1, q])
        bytes_of(e_raw.at[2, :, part_q], eq_r.at[2, q])
        lanes_q = pl.ds(pl.multiple_of(c * half + q * quarter, quarter), quarter)
        e_all[e_rows(z, 1 - xl), lanes_q] = join(e_raw[1, :, part_q], e_raw[2, :, part_q])
        near_q = e_far_piece(z, 1 - xl, q)
        put(near_q, near_q, en_s.at[0, q], er_r.at[0, 1, 0], z_up)
        put(near_q, near_q, en_s.at[1, q], er_r.at[1, 1, 0], z_down)
    put(near_piece, near_piece, ep_s.at[1, 0], ep_r.at[0], partner)

    def e_step(direction, o, s):
        dz = (NZ - s) if direction == 0 else s
        z_ = lax.rem(z + dz, NZ)
        xl_ = (1 - xl) if o else xl
        piece = e_piece(z_, xl_)
        bytes_of(piece, er_r.at[direction, o, s - 1])
        on = piece if s < 3 else e_far_piece(z_, xl_, direction)
        put(on, on, er_s.at[direction, o, s], er_r.at[direction, o, s], z_up if direction == 0 else z_down)
        put(piece, piece, ep_s.at[o, dz], ep_r.at[dz], partner)

    def e_far(direction, o):
        z_ = lax.rem(z + 4, NZ)
        xl_ = (1 - xl) if o else xl
        piece = e_far_piece(z_, xl_, direction)
        bytes_of(piece, er_r.at[direction, o, 3])
        put(piece, piece, ep_s.at[o, 4 + 4 * direction], ep_r.at[4], partner)

    def e_prep(dz, lanes):
        z_ = lax.rem(z + dz, NZ)
        x = 0.5 * e_all[pl.ds(pl.multiple_of(z_ * kc, 16), kc), lanes]
        hi = x.astype(jnp.bfloat16)
        e3[z_, 0:kc, lanes] = hi
        e3[z_, kc:2 * kc, lanes] = (x - hi.astype(jnp.float32)).astype(jnp.bfloat16)
        e3[z_, 2 * kc:3 * kc, lanes] = hi

    def e_other(dz):
        z_ = lax.rem(z + dz, NZ)
        bytes_of(e_all.at[pl.ds(pl.multiple_of(z_ * kc, 16), kc), lanes_o], ep_r.at[dz])
        e_prep(dz, lanes_o)

    def f_prep(u, dy):
        j = clip_of(u, dy)
        x = f_all[pl.ds(pl.multiple_of(j * kc, 16), kc), :]
        hi = x.astype(jnp.bfloat16)
        lo = (x - hi.astype(jnp.float32)).astype(jnp.bfloat16)
        f3[j] = jnp.concatenate([hi, hi, lo], axis=0).T

    def f_wait(direction, u, k, clip_, lo, hi):
        bytes_of(f_block(clip_, lo, hi), fy_r.at[direction, u, k])

    dot = functools.partial(jnp.dot, preferred_element_type=jnp.float32)

    LAST = 9
    far = lax.rem(z + 4, NZ)
    beside = jnp.where(far == clip_of(1, 2), clip_of(1, 1), clip_of(1, 2))

    def stage_of(j):
        up = lax.rem(j - z + NZ, NZ)
        e_turn = jnp.minimum(up, NZ - up)
        e_turn = e_turn + e_turn // 3
        right = lax.rem(lax.rem(j, NY) - y + NY, NY)
        away = jnp.minimum(right, NY - right)
        f_turn = jnp.where(j // NY == xh, away, 2 + away)
        return jnp.where(j == beside, LAST, jnp.maximum(e_turn, f_turn))

    def products(stage, first, count):
        @pl.loop(0, count)
        def _(i):
            j = lax.rem(xh * NY + first + i, 2 * NY)

            @pl.when(stage_of(j) == stage)
            def _():
                ang[...] = ang[...] + dot(f3[j], e3[j])

    e_step(0, 0, 1)
    e_step(1, 0, 1)
    greeted(1)
    greet(2)
    f_wait(0, 0, 0, clip_of(0, 3), 0, mid)
    f_send(0, 0, 2, clip_of(0, 3), 0, mid)
    f_wait(1, 0, 0, clip_of(0, 1), mid, kc)
    f_send(1, 0, 2, clip_of(0, 1), mid, kc)
    bytes_of(f_rel.at[cut:kc, :], fx_r.at[1])
    put(f_rel.at[cut:kc, :], f_block(clip_of(1, 0), cut, kc), fx_s.at[3], fx_r.at[3], x_near)
    bytes_of(f_rel.at[0:cut, :], fx_r.at[0])
    put(f_rel.at[0:cut, :], f_block(clip, 0, cut), fx_s.at[2], fx_r.at[2], x_cross)
    e_prep(0, lanes_c)
    f_prep(0, 0)
    e_other(0)
    products(0, 0, 8)
    e_step(0, 1, 1)
    e_step(1, 1, 1)
    e_prep(1, lanes_c)
    e_prep(7, lanes_c)
    f_wait(0, 0, 1, clip_of(0, 3), mid, kc)
    f_wait(1, 0, 1, clip_of(0, 1), 0, mid)
    f_prep(0, 1)
    f_prep(0, 3)
    over = clip_of(1, 0)
    bytes_of(f_block(over, 0, cut), fx_r.at[2])
    f_send(0, 1, 0, over, 0, cut)
    f_send(1, 1, 0, over, 0, cut)
    e_step(0, 0, 2)
    e_step(1, 0, 2)
    e_other(1)
    e_other(7)
    bytes_of(f_block(over, cut, kc), fx_r.at[3])
    f_send(0, 1, 1, over, cut, mid)
    f_send(1, 1, 1, over, mid, kc)
    f_send(0, 1, 2, over, mid, kc)
    f_send(1, 1, 2, over, cut, mid)
    products(1, 0, 4)
    e_step(0, 1, 2)
    e_step(1, 1, 2)
    products(1, 4, 4)
    e_prep(2, lanes_c)
    e_prep(6, lanes_c)
    f_wait(0, 0, 2, clip_of(0, 2), 0, mid)
    f_wait(1, 0, 2, clip_of(0, 2), mid, kc)
    f_prep(0, 2)
    f_prep(1, 0)
    e_other(2)
    e_other(6)
    e_step(0, 0, 3)
    e_step(1, 0, 3)
    f_wait(0, 1, 0, clip_of(1, 3), 0, cut)
    f_wait(0, 1, 1, clip_of(1, 3), cut, mid)
    f_send(0, 1, 3, clip_of(1, 3), 0, mid)
    f_wait(1, 1, 0, clip_of(1, 1), 0, cut)
    f_wait(1, 1, 1, clip_of(1, 1), mid, kc)
    f_send(1, 1, 3, clip_of(1, 1), mid, kc)
    greeted(2)
    for u, dy in clip_offsets:
        send_w(u, dy)
    products(2, 0, 8)
    e_step(0, 1, 3)
    e_step(1, 1, 3)
    f_wait(0, 1, 2, clip_of(1, 3), mid, kc)
    f_wait(1, 1, 2, clip_of(1, 1), cut, mid)
    f_prep(1, 1)
    f_prep(1, 3)
    products(3, 4, 4)
    e_prep(3, lanes_c)
    e_prep(5, lanes_c)
    e_far(0, 0)
    e_far(1, 0)
    e_other(3)
    e_other(5)
    products(4, 0, 4)
    e_far(0, 1)
    e_far(1, 1)
    e_prep(4, lanes_c)
    products(4, 4, 4)
    f_wait(0, 1, 3, clip_of(1, 2), 0, mid)
    f_wait(1, 1, 3, clip_of(1, 2), mid, kc)
    f_prep(1, 2)
    ang[...] = ang[...] + dot(f3[beside], e3[beside])
    e_other(4)

    for n in range(nn // 256):
        cols = slice(256 * n, 256 * n + 256)
        x = ang[:, cols] + dot(f3[far], e3[far, :, cols])
        phi[:, cols] = scaled_cos_of_twice(x, scale).astype(jnp.bfloat16)

    hk = w_t.shape[1] // 2
    block = nn // 8
    chains = range(2)

    def chain_rows(h):
        return slice(h * hk, (h + 1) * hk)

    def block_rows(z_):
        return pl.ds(pl.multiple_of(lax.rem(z_, 4) * 16, 16), 16)

    def block_lanes(z_, xl_, core=None):
        lane = (xl_ * 2 + z_ // 4) * block
        if core is not None:
            lane = lane + core * half
        return pl.ds(pl.multiple_of(lane, block), block)

    nt = functools.partial(
        lax.dot_general, dimension_numbers=(((1,), (1,)), ((), ())), preferred_element_type=jnp.float32)

    def wait_w(t, h):
        for own, count in ((True, 3), (False, 4)):
            @pl.when((my_chain == h) == own)
            def _():
                bytes_of(g_recv.at[0, 0:count], w_r.at[t, h])

    def start_logits(t, h):
        w = w_t[t, chain_rows(h), :]
        c_send[t, h] = dot(w, phi[:, lanes_o]).astype(jnp.bfloat16)
        put(c_send.at[t, h], c_recv.at[t, h], c_s.at[t, h], c_r.at[t, h], partner)
        part[h] = dot(w, phi[:, lanes_c])

    def share_logits(t, h):
        bytes_of(c_recv.at[t, h], c_r.at[t, h])
        total = part[h] + c_recv[t, h].astype(jnp.float32)
        part[h] = total
        l_send[t, h] = total.astype(jnp.bfloat16)
        for dz, dx in feat_offsets:
            pz, px = feat_peer(dz, dx)
            put(l_send.at[t, h, block_rows(pz), block_lanes(pz, px)], l_recv.at[t, h, dx * NZ + dz - 1],
                l_s.at[t, h], l_r.at[t, h], (clip, feat_of(pz, px, c)), False)

    bytes_of(g_recv.at[0], w_r.at[0, 0])
    out = dot(w_t[0], phi[:, lanes_o]).astype(jnp.bfloat16)
    for h in chains:
        c_send[0, h] = out[chain_rows(h), :]
        put(c_send.at[0, h], c_recv.at[0, h], c_s.at[0, h], c_r.at[0, h], partner)
    out = dot(w_t[0], phi[:, lanes_c])
    for h in chains:
        part[h] = out[chain_rows(h), :]
    for t in range(STEPS):
        for h in chains:
            if t > 0:
                wait_w(t, h)
                start_logits(t, h)
            share_logits(t, h)
        for h in chains:
            acc = part[h, block_rows(z), block_lanes(z, xl)]
            bytes_of(l_recv.at[t, h], l_r.at[t, h])
            for i in range(2 * NZ - 1):
                acc = acc + l_recv[t, h, i].astype(jnp.float32)
            labels = lab_t[h, block_rows(z), :]
            r_t[t, h, block_rows(z), block_lanes(z, xl, c)] = (jax.nn.sigmoid(acc) - labels).astype(jnp.bfloat16)
            mine_r = r_t.at[t, h, block_rows(z), block_lanes(z, xl, c)]
            for dz, dx in feat_offsets:
                pz, px = feat_peer(dz, dx)
                put(mine_r, mine_r, r_s.at[t, h], r_r.at[t, h], (clip, feat_of(pz, px, c)), False)
        for h in chains:
            bytes_of(l_recv.at[t, h], r_r.at[t, h])
            half_r = r_t.at[t, h, :, lanes_c]
            put(half_r, half_r, rc_s.at[t, h], rc_r.at[t, h], partner)
            grad[h] = nt(r_t[t, h, :, lanes_c], phi[:, lanes_c])
            bytes_of(r_t.at[t, h, :, lanes_o], rc_r.at[t, h])
            total = grad[h] + nt(r_t[t, h, :, lanes_o], phi[:, lanes_o])
            grad[h] = total
            g_send[t, h] = total.astype(jnp.bfloat16)

            def send_g(u, yo):
                to = clip_of(u, yo - y + NY)
                rows = pl.ds(pl.multiple_of(local_block(to) * kw, kw), kw)
                slot = u * NY + lax.rem(yo - y + NY, NY) - 1
                put(g_send.at[t, h, rows, :], g_recv.at[t, slot], g_s.at[t, h], g_r.at[t], (to, feat), False)

            for yo in (2 * h, 2 * h + 1):
                send_g(1, yo)
            for yo in (2 * h, 2 * h + 1):
                @pl.when(yo != y)
                def _():
                    send_g(0, yo)
        for h in chains:
            @pl.when(my_chain == h)
            def _():
                g = grad[h, pl.ds(pl.multiple_of(local_block(clip) * kw, kw), kw), :]
                bytes_of(g_recv.at[t], g_r.at[t])
                for i in range(7):
                    g = g + g_recv[t, i].astype(jnp.float32)
                w_new = w_own[...] - 0.25 * g
                w_own[...] = w_new
                w_half = w_new.astype(jnp.bfloat16)
                w_send[t + 1] = w_half
                w_t[t + 1, my_rows, :] = w_half
                for u, dy in clip_offsets:
                    put(w_send.at[t + 1], w_t.at[t + 1, my_rows, :], w_s.at[t + 1], w_r.at[t + 1, h],
                        (clip_of(u, dy), feat), False)
    tr_ref[...] = w_own[...]

    t = STEPS

    def chip_blocks(h, core):
        out = dot(picks[core, 0], logits[h, :, 0:quarter])
        for q in range(1, 4):
            out = out + dot(picks[core, q], logits[h, :, q * quarter:(q + 1) * quarter])
        return out

    def chip_rows(z_, xl_):
        return pl.ds(pl.multiple_of((2 * local_block(z_) + xl_) * 16, 16), 16)

    z_chain = lax.rem(z, 4) // 2
    for h in chains:
        wait_w(t, h)
        logits[h] = dot(w_t[t, chain_rows(h), :], phi[...]).astype(jnp.bfloat16)
        s_out[h] = chip_blocks(h, 1 - c).astype(jnp.bfloat16)
        put(s_out.at[h], s_in.at[h], c_s.at[t, h], c_r.at[t, h], partner)
        s_own[h] = chip_blocks(h, c)
        bytes_of(s_in.at[h], c_r.at[t, h])
        total = s_own[h] + s_in[h].astype(jnp.float32)
        s_own[h] = total
        s_sum[h] = total.astype(jnp.bfloat16)

        def send_s(pz, dx):
            px = 1 - xl if dx else xl
            slot = dx * NZ + lax.rem(pz - z + NZ, NZ) - 1
            put(s_sum.at[h, chip_rows(pz, px), :], s_recv.at[slot], l_s.at[t, h], l_r.at[t, 0], (clip, feat_of(pz, px, c)), False)

        for pz in (2 * h, 2 * h + 1, NY + 2 * h, NY + 2 * h + 1):
            send_s(pz, 1)
        for pz in (2 * h, 2 * h + 1, NY + 2 * h, NY + 2 * h + 1):
            @pl.when(pz != z)
            def _():
                send_s(pz, 0)
    acc = s_own[z_chain, chip_rows(z, xl), :]
    bytes_of(s_recv, l_r.at[t, 0])
    for i in range(2 * NZ - 1):
        acc = acc + s_recv[i].astype(jnp.float32)
    for q in range(4):
        sc_ref[:, q * quarter:(q + 1) * quarter] = acc[4 * q:4 * q + 4, :]

    for copy in sends:
        copy.wait_send()
    for t in range(STEPS + 1):
        bytes_of(g_recv.at[0], w_s.at[t])
    for h in chains:
        for t in range(STEPS):
            bytes_of(l_recv.at[0, 0], l_s.at[t, h])
            bytes_of(l_recv.at[0, 0], r_s.at[t, h])
        for own, count in ((True, 3), (False, 4)):
            @pl.when((my_chain == h) == own)
            def _():
                for t in range(STEPS):
                    bytes_of(g_recv.at[0, 0:count], g_s.at[t, h])
        for own, count in ((True, 7), (False, 8)):
            @pl.when((z_chain == h) == own)
            def _():
                bytes_of(s_recv.at[0:count], l_s.at[STEPS, h])


def per_device(embeds, frequencies, phases, weights, labels):
    nn, ke = embeds.shape
    kc, nf = frequencies.shape
    kw = weights.shape[1]
    kk = labels.shape[1]
    kt = kc * lax.axis_size("clip")
    total_features = nf * lax.axis_size("feat")
    scale = math.sqrt(2.0 / total_features)
    f32, b16 = jnp.float32, jnp.bfloat16
    dma = pltpu.SemaphoreType.DMA
    hbm = pl.BlockSpec(memory_space=pl.ANY)
    vmem = pl.BlockSpec(memory_space=pltpu.VMEM)
    half, quarter = nn // 2, nn // 4
    steps = STEPS + 1
    scratch = [
        pltpu.VMEM((ke, nn), f32),
        pltpu.VMEM((kc, nf), f32),
        pltpu.VMEM((nf // 128, 128), f32),
        pltpu.VMEM((kw, nf), f32),
        pltpu.VMEM((nn, kk), jnp.int32),
        pltpu.VMEM((2, 4, 128, 64), b16),
        pltpu.VMEM((kt, nn), f32),
        pltpu.VMEM((kt, nf), f32),
        pltpu.VMEM((3, ke, half), f32),
        pltpu.VMEM((2 * ke, half), f32),
        pltpu.VMEM((kc, nf), f32),
        pltpu.VMEM((8, 3 * kc, nn), b16),
        pltpu.VMEM((8, nf, 3 * kc), b16),
        pltpu.VMEM((nf, nn), f32),
        pltpu.VMEM((nf, nn), b16),
        pltpu.VMEM((2, kk // 2, nn // 8), f32),
        pltpu.VMEM((kw, nf), f32),
        pltpu.VMEM((steps, kw, nf), b16),
        pltpu.VMEM((steps, kk, nf), b16),
        pltpu.VMEM((2, kk // 2, half), f32),
        pltpu.VMEM((STEPS, 2, kk // 2, half), b16),
        pltpu.VMEM((STEPS, 2, kk // 2, half), b16),
        pltpu.VMEM((STEPS, 2, kk // 2, half), b16),
        pltpu.VMEM((STEPS, 2, 2 * NZ - 1, 16, nn // 8), b16),
        pltpu.VMEM((STEPS, 2, kk // 2, nn), b16),
        pltpu.VMEM((2, kk // 2, nf), f32),
        pltpu.VMEM((STEPS, 2, kk // 2, nf), b16),
        pltpu.VMEM((STEPS, 7, kw, nf), b16),
        pltpu.VMEM((2, kk // 2, nn), b16),
        pltpu.VMEM((2, 128, quarter), b16),
        pltpu.VMEM((2, 128, quarter), b16),
        pltpu.VMEM((2, 128, quarter), f32),
        pltpu.VMEM((2, 128, quarter), b16),
        pltpu.VMEM((2 * NZ - 1, 16, quarter), b16),
        dma((3, 2)), dma((3, 2)), dma((2, 2)), dma((2, 2, 4)), dma((2, 2, 4)), dma((2, NZ + 1)), dma((NZ,)),
        dma((4,)), dma((4,)), dma((2, 2, 4)), dma((2, 2, 4)),
        dma((steps,)), dma((steps, 2)), dma((steps, 2)), dma((steps, 2)), dma((steps, 2)), dma((steps, 2)),
        dma((STEPS, 2)), dma((STEPS, 2)), dma((STEPS, 2)), dma((STEPS, 2)), dma((STEPS, 2)), dma((STEPS,)),
        dma((5,)), pltpu.SemaphoreType.REGULAR((3,)),
    ]
    trained_t, scores_t = pl.pallas_call(
        functools.partial(kernel, scale),
        out_shape=(pltpu.VMEM((kw, nf), f32), pltpu.VMEM((4, nn), f32)),
        in_specs=[hbm] * 5,
        out_specs=(vmem, vmem),
        scratch_shapes=scratch,
        compiler_params=pltpu.CompilerParams(
            collective_id=0, has_side_effects=True, vmem_limit_bytes=60 * 1024 * 1024),
    )(embeds.T, frequencies, phases.reshape(nf // 128, 128), weights.T, labels)
    return trained_t.T, scores_t.T


def solution(mesh):
    placed = (P("clip", "feat"), P("clip", "feat"), P("feat"), P("feat", "clip"), P("clip", None))
    return jax.shard_map(
        per_device,
        mesh=mesh,
        in_specs=placed,
        out_specs=(P("feat", "clip"), P("clip", "feat")),
        check_vma=False,
    )
```
